32 devices in a mesh: section: 2 (over core), dp: 16 (over z, y, x).
Axes of the slice: x: 2, y: 2, z: 4, core: 2. Of those that a mesh axis runs over, the one named last changes fastest.
Arguments:
- audio_in: bfloat16 [2, 16, 96, 1024], P(None, 'dp'), may hold values from -6 to 6
- out_grad: bfloat16 [2, 16, 96, 1024], P(None, 'dp'), may hold values from -6 to 6
- item_len: int32 [2, 16], P(None, 'dp'), may hold values from 24 to 96, as said below
- rel_bucket: int32 [96], replicated, may hold values from 0 to 31, as said below
- w_qkv: float32 [2, 1024, 3072], P('section', 'dp'), may hold values from -0.1875 to 0.1875
- w_out: float32 [2, 1024, 1024], P('section', 'dp'), may hold values from -0.625 to 0.625
- w_up: float32 [2, 1024, 4096], P('section', 'dp'), may hold values from -0.1875 to 0.1875
- w_down: float32 [2, 4096, 1024], P('section', 'dp'), may hold values from -0.09375 to 0.09375
- ln1_gain: float32 [2, 1024], P('section', 'dp'), may hold values from 0.1 to 1.9
- ln1_bias: float32 [2, 1024], P('section', 'dp'), may hold values from -3 to 3
- ln2_gain: float32 [2, 1024], P('section', 'dp'), may hold values from 0.1 to 1.9
- ln2_bias: float32 [2, 1024], P('section', 'dp'), may hold values from -3 to 3
- b_out: float32 [2, 1024], P('section', 'dp'), may hold values from -3 to 3
- b_up: float32 [2, 4096], P('section', 'dp'), may hold values from -3 to 3
- b_down: float32 [2, 1024], P('section', 'dp'), may hold values from -3 to 3
- rel_table: float32 [2, 512], P('section', 'dp'), may hold values from -4 to 4
Outputs:
- layer_outputs: bfloat16 [2, 2, 16, 96, 1024], P('section', None, 'dp')
- input_grads: float32 [2, 2, 16, 96, 1024], P('section', None, 'dp')
- grad_w_qkv: float32 [2, 1024, 3072], P('section', 'dp')
- grad_w_out: float32 [2, 1024, 1024], P('section', 'dp')
- grad_w_up: float32 [2, 1024, 4096], P('section', 'dp')
- grad_w_down: float32 [2, 4096, 1024], P('section', 'dp')
- grad_ln1_gain: float32 [2, 1024], P('section', 'dp')
- grad_ln1_bias: float32 [2, 1024], P('section', 'dp')
- grad_ln2_gain: float32 [2, 1024], P('section', 'dp')
- grad_ln2_bias: float32 [2, 1024], P('section', 'dp')
- grad_b_out: float32 [2, 1024], P('section', 'dp')
- grad_b_up: float32 [2, 4096], P('section', 'dp')
- grad_b_down: float32 [2, 1024], P('section', 'dp')
- grad_rel_table: float32 [2, 512], P('section', 'dp')
The draws below stay inside these ranges and needn't reach their ends.
Inputs may be any that keep to these rules, and one draw needn't show every extreme that they name: `item_len`: an item with more than 48 tokens is in the long bucket, else in the short one. Some item has 96 tokens and some 96/4. `rel_bucket`: entry d is the bucket of a key d positions before its query: equal to d for d < 16, never falling, each bucket used.
All inputs are finite; a program needn't handle non-finite values.
Results may differ from the reference program's by a relative error of at most 0.015.
The reference program's roundings to bfloat16 on the way count: a program that leaves them out, or rounds other values in their place, can miss the bound.
Values may be sent and summed in bfloat16 or wider, within the bound.
A program may use at most 256 MiB of HBM per device.

```python
import math
import jax
import jax.numpy as jnp
from jax import lax

D = 1024
H = 16
HD = 64
FF = 4096
NB = 32
MICRO = 2
LMAX = 96
ITEMS = 16


def draw_item_len(key, part):
    keys = jax.random.split(key, 5)
    count = MICRO * ITEMS
    longer = jax.random.randint(keys[0], (count,), 0, 7) < 3
    short_len = jax.random.randint(keys[1], (count,), LMAX // 4, LMAX // 2 + 1)
    long_len = jax.random.randint(keys[2], (count,), LMAX // 2 + 1, LMAX + 1)
    lengths = jnp.where(longer, long_len, short_len)
    first = jax.random.randint(keys[3], (), 0, count)
    second = (first + jax.random.randint(keys[4], (), 1, count)) % count
    lengths = lengths.at[first].set(LMAX).at[second].set(LMAX // 4)
    return lengths.reshape(MICRO, ITEMS).astype(jnp.int32)


def draw_rel_bucket(key, part):
    half = NB // 2
    spots = jax.random.permutation(key, LMAX - half - 1) + half + 1
    marks = jnp.zeros((LMAX,), jnp.int32).at[spots[:half - 1]].set(1)
    distance = jnp.arange(LMAX, dtype=jnp.int32)
    return jnp.where(distance < half, distance, half + jnp.cumsum(marks)).astype(jnp.int32)


def block_levels(key, dims, cuts, low, largest):
    level, own = 1.0, jax.random.fold_in(key, 6)
    for dim, blocks in cuts:
        heights = jnp.exp(jax.random.uniform(jax.random.fold_in(own, dim), (blocks,), jnp.float32, low / len(cuts), largest / len(cuts)))
        level = level * jnp.repeat(heights, dims[dim] // blocks).reshape([-1 if axis == dim else 1 for axis in range(len(dims))])
    return level


def normal_values(rng, dims, scale, limit, shards=(), kind=jnp.bfloat16):
    result = jax.random.normal(rng, dims, jnp.float32) * scale
    if len(shards) > 0:
        result = block_levels(rng, dims, shards, -0.22, 0.18) * result
    return jnp.clip(result, min=-limit, max=limit).astype(kind)


def setup_inputs(seed: int = 0) -> dict:
    key_of = jax.random.split(jax.random.key(seed), 17)
    return {
        "audio_in": normal_values(key_of[0], (MICRO, ITEMS, LMAX, D), 1.0, 6.0, ((1, 16),)),
        "out_grad": normal_values(key_of[1], (MICRO, ITEMS, LMAX, D), 1.0, 6.0, ((1, 16),)),
        "item_len": draw_item_len(jax.random.fold_in(key_of[16], 71), 0),
        "rel_bucket": draw_rel_bucket(jax.random.fold_in(key_of[16], 71), 0),
        "w_qkv": normal_values(key_of[4], (2, D, 3 * D), D ** -0.5, 0.1875, ((0, 2), (1, 16)), jnp.float32),
        "w_out": normal_values(key_of[5], (2, D, D), (8 * D // LMAX) ** -0.5, 0.625, ((0, 2), (1, 16)), jnp.float32),
        "w_up": normal_values(key_of[6], (2, D, FF), D ** -0.5, 0.1875, ((0, 2), (1, 16)), jnp.float32),
        "w_down": normal_values(key_of[7], (2, FF, D), FF ** -0.5, 0.09375, ((0, 2), (1, 16)), jnp.float32),
        "ln1_gain": jnp.clip(1.0 + 0.18 * jax.random.normal(key_of[8], (2, D), jnp.float32), 0.1, 1.9),
        "ln1_bias": normal_values(key_of[9], (2, D), 0.3, 3.0, ((0, 2), (1, 16)), jnp.float32),
        "ln2_gain": jnp.clip(1.0 + 0.18 * jax.random.normal(key_of[10], (2, D), jnp.float32), 0.1, 1.9),
        "ln2_bias": normal_values(key_of[11], (2, D), 0.3, 3.0, ((0, 2), (1, 16)), jnp.float32),
        "b_out": normal_values(key_of[12], (2, D), 0.5, 3.0, ((0, 2), (1, 16)), jnp.float32),
        "b_up": normal_values(key_of[13], (2, FF), 0.5, 3.0, ((0, 2), (1, 16)), jnp.float32),
        "b_down": normal_values(key_of[14], (2, D), 0.5, 3.0, ((0, 2), (1, 16)), jnp.float32),
        "rel_table": normal_values(key_of[15], (2, NB * H), 1.0, 4.0, ((0, 2), (1, 16)), jnp.float32),
    }


@jax.custom_vjp
def low(v):
    return lax.optimization_barrier(v.astype(jnp.bfloat16)).astype(jnp.float32)

@jax.custom_vjp
def low_back(v):
    return v

def low_keep(v):
    return (low(v), None)

def low_pass(kept, grad):
    return (grad,)

def back_keep(v):
    return (v, None)

def back_low(kept, grad):
    return (low(grad),)
low.defvjp(low_keep, low_pass)
low_back.defvjp(back_keep, back_low)
epsilon = 1e-05
highest = lax.Precision.HIGHEST

def norm_rows(values):
    centre = values - lax.optimization_barrier(jnp.mean(values, axis=-1, keepdims=True))
    return centre * lax.rsqrt(lax.optimization_barrier(jnp.mean(centre * centre, axis=-1, keepdims=True)) + epsilon)

def make_bias(table_flat, buckets):
    position = jnp.arange(LMAX)
    distance = jnp.clip(position[:, None] - position[None, :], 0, LMAX - 1)
    grid = buckets[distance]
    table = table_flat.reshape(NB, H)
    values = table[grid]
    keep = (position[None, :] <= position[:, None])[:, :, None]
    return jnp.transpose(jnp.where(keep, values, 0.0), (2, 0, 1))

def layer(params, bias, inputs, length):
    w_qkv, w_out, w_up, w_down, gain_one, shift_one, gain_two, shift_two, bias_out, bias_up, bias_down = params
    group = inputs.shape[0]
    position = jnp.arange(LMAX)
    normed = low(norm_rows(inputs) * gain_one + shift_one)
    qkv = low(low_back(jnp.einsum('gld,de->gle', normed, w_qkv, precision=highest)))
    query = qkv[..., :D].reshape(group, LMAX, H, HD)
    keys = qkv[..., D:2 * D].reshape(group, LMAX, H, HD)
    values = qkv[..., 2 * D:].reshape(group, LMAX, H, HD)
    scores = jnp.einsum('gihd,gjhd->ghij', query, keys, precision=highest) * HD ** (-0.5) + bias[None]
    visible = (position[None, :] <= position[:, None])[None, None] & (position[None, None, None, :] < length[:, None, None, None])
    scores = low_back(jnp.where(visible, scores, -1000000000.0))
    raised = jnp.exp(scores - lax.optimization_barrier(jnp.max(scores, axis=-1, keepdims=True)))
    probs = raised / lax.optimization_barrier(jnp.sum(raised, axis=-1, keepdims=True))
    mixed = jnp.einsum('ghij,gjhd->gihd', low(probs), values, precision=highest).reshape(group, LMAX, D)
    mixed = low(low_back(mixed))
    middle = inputs + low_back(jnp.einsum('gld,de->gle', mixed, w_out, precision=highest) + bias_out)
    second = low(norm_rows(middle) * gain_two + shift_two)
    hidden = low_back(jnp.einsum('gld,df->glf', second, w_up, precision=highest) + bias_up)
    activated = low(jax.nn.gelu(hidden))
    branch = low_back(jnp.einsum('glf,fd->gld', activated, w_down, precision=highest) + bias_down)
    valid = (position[None, :] < length[:, None]).astype(jnp.float32)[:, :, None]
    return (middle + branch) * valid

def reference(audio_in, out_grad, item_len, rel_bucket, w_qkv, w_out, w_up, w_down, ln1_gain, ln1_bias, ln2_gain, ln2_bias, b_out, b_up, b_down, rel_table):
    masters = (w_qkv, w_out, w_up, w_down, ln1_gain, ln1_bias, ln2_gain, ln2_bias, b_out, b_up, b_down, rel_table)
    count = MICRO * ITEMS
    group = math.gcd(count, 2 ** ((4096 // LMAX).bit_length() - 1))
    slabs = count // group
    audio = audio_in.astype(jnp.float32).reshape(slabs, group, LMAX, D)
    lengths = item_len.reshape(slabs, group)
    probe = jnp.zeros_like(audio)

    def pair(first, second, bias_first, bias_second, slab, shift, length):
        coarse = layer(first, bias_first, slab, length)
        fine = layer(second, bias_second, low_back(low(coarse) + shift), length)
        return (coarse, fine)
    pair_saved = jax.checkpoint(pair)

    def whole(params, audio_all, probe_all):
        rounded = tuple((low(part) for part in params))
        first = tuple((part[0] for part in rounded[:11]))
        second = tuple((part[1] for part in rounded[:11]))
        bias_first = make_bias(rounded[11][0], rel_bucket)
        bias_second = make_bias(rounded[11][1], rel_bucket)

        def step(carry, pieces):
            return (carry, pair_saved(first, second, bias_first, bias_second, pieces[0], pieces[1], pieces[2]))
        _, outputs = lax.scan(step, 0, (audio_all, probe_all, lengths))
        return outputs
    (coarse, fine), pullback = jax.vjp(whole, masters, audio, probe)
    cotangent = (jnp.zeros_like(coarse), out_grad.astype(jnp.float32).reshape(slabs, group, LMAX, D))
    grad_masters, grad_audio, grad_probe = pullback(cotangent)
    shape_full = (MICRO, ITEMS, LMAX, D)
    layer_outputs = jnp.stack([coarse.reshape(shape_full), fine.reshape(shape_full)]).astype(jnp.bfloat16)
    input_grads = jnp.stack([grad_audio.reshape(shape_full), grad_probe.reshape(shape_full)])
    return (layer_outputs, input_grads, grad_masters[0], grad_masters[1], grad_masters[2], grad_masters[3], grad_masters[4], grad_masters[5], grad_masters[6], grad_masters[7], grad_masters[8], grad_masters[9], grad_masters[10], grad_masters[11])
```

```python
import jax
import jax.numpy as jnp
from jax import lax
from jax.experimental import pallas as pl
from jax.experimental.pallas import tpu as pltpu
from jax.sharding import PartitionSpec as P

H = 16
NB = 32


epsilon = 1e-05
highest = lax.Precision.HIGHEST


def passed_along(block, axis, distance):
    devices = range(lax.axis_size(axis))
    route = [(i - distance, i) for i in devices if i - distance in devices]
    return lax.ppermute(block, axis, route)


def norm_rows(values):
    centre = values - jnp.mean(values, axis=-1, keepdims=True)
    return centre * lax.rsqrt(jnp.mean(centre * centre, axis=-1, keepdims=True) + epsilon)


def norm_affine(values, gain, shift):
    return norm_rows(values) * gain + shift


def contract_rows(left, right):
    return lax.dot_general(
        left, right, (((0,), (0,)), ((), ())), preferred_element_type=jnp.float32
    )


def contract_cols(left, right):
    return lax.dot_general(
        left, right, (((1,), (1,)), ((), ())), preferred_element_type=jnp.float32
    )


def toeplitz_rows(values):
    heads, length = values.shape
    reverse = jnp.flip(values, axis=1)
    padded = jnp.concatenate([reverse, jnp.zeros_like(reverse)], axis=1)
    tiled = jnp.tile(padded, (1, length))[:, : length * (2 * length - 1)]
    return tiled.reshape(heads, length, 2 * length - 1)[:, :, length - 1 :]


def diagonal_sums(grid):
    heads, length, _ = grid.shape
    widened = jnp.concatenate([jnp.zeros((heads, length, length - 1), grid.dtype), grid], axis=2)
    flat = widened.reshape(heads, length * (2 * length - 1))
    flat = jnp.concatenate([flat, jnp.zeros((heads, length), grid.dtype)], axis=1)
    folded = jnp.sum(flat.reshape(heads, length, 2 * length), axis=1)
    return jnp.flip(folded[:, :length], axis=1)


def bucket_table(buckets):
    return (buckets[None, :] == jnp.arange(NB, dtype=jnp.int32)[:, None]).astype(jnp.float32)


def make_bias(table_flat, onehot):
    table = table_flat.astype(jnp.float32).reshape(NB, H)
    per_distance = jnp.dot(table.T, onehot, precision=highest)
    return toeplitz_rows(per_distance)


def weight_terms(factors):
    normed, d_qkv, mixed, d_attn, second, d_hidden, activated, d_branch = factors
    return (
        contract_rows(normed, d_qkv),
        contract_rows(mixed, d_attn),
        contract_rows(second, d_hidden),
        contract_rows(activated, d_branch),
    )


def forward_item(inputs, length, bias, weights):
    (
        w_qkv,
        w_out,
        w_up,
        w_down,
        gain_one,
        shift_one,
        gain_two,
        shift_two,
        bias_out,
        bias_up,
        bias_down,
    ) = weights
    rows, width = inputs.shape
    heads = bias.shape[0]
    head_dim = width // heads
    scale = head_dim ** (-0.5)
    position = jnp.arange(rows)
    visible = (position[None, :] <= position[:, None])[None] & (position[None, None, :] < length)
    valid = (position < length).astype(jnp.float32)[:, None]
    normed = norm_affine(
        inputs, gain_one.astype(jnp.float32), shift_one.astype(jnp.float32)
    ).astype(jnp.bfloat16)
    qkv = jnp.dot(normed, w_qkv, preferred_element_type=jnp.float32).astype(jnp.bfloat16)
    query = qkv[:, :width].reshape(rows, heads, head_dim)
    keys = qkv[:, width : 2 * width].reshape(rows, heads, head_dim)
    values = qkv[:, 2 * width :].reshape(rows, heads, head_dim)
    scores = (
        jnp.einsum("ihd,jhd->hij", query, keys, preferred_element_type=jnp.float32) * scale + bias
    )
    scores = jnp.where(visible, scores, -1000000000.0)
    raised = jnp.exp(scores - jnp.max(scores, axis=-1, keepdims=True))
    probs = raised / jnp.sum(raised, axis=-1, keepdims=True)
    probs_low = probs.astype(jnp.bfloat16)
    mixed = (
        jnp.einsum("hij,jhd->ihd", probs_low, values, preferred_element_type=jnp.float32)
        .reshape(rows, width)
        .astype(jnp.bfloat16)
    )
    middle = (
        inputs
        + jnp.dot(mixed, w_out, preferred_element_type=jnp.float32)
        + bias_out.astype(jnp.float32)
    )
    second = norm_affine(
        middle, gain_two.astype(jnp.float32), shift_two.astype(jnp.float32)
    ).astype(jnp.bfloat16)
    hidden = jnp.dot(second, w_up, preferred_element_type=jnp.float32) + bias_up.astype(jnp.float32)
    activated = jax.nn.gelu(hidden).astype(jnp.bfloat16)
    result = (
        middle
        + jnp.dot(activated, w_down, preferred_element_type=jnp.float32)
        + bias_down.astype(jnp.float32)
    ) * valid
    saved = (
        normed,
        query,
        keys,
        values,
        probs,
        probs_low,
        mixed,
        middle,
        second,
        hidden,
        activated,
        valid,
    )
    return (result, saved)


def backward_item(inputs, length, bias, weights, upstream, onehot):
    (
        w_qkv,
        w_out,
        w_up,
        w_down,
        gain_one,
        shift_one,
        gain_two,
        shift_two,
        bias_out,
        bias_up,
        bias_down,
    ) = weights
    _, saved = forward_item(inputs, length, bias, weights)
    (
        normed,
        query,
        keys,
        values,
        probs,
        probs_low,
        mixed,
        middle,
        second,
        hidden,
        activated,
        valid,
    ) = saved
    rows, width = inputs.shape
    heads = bias.shape[0]
    head_dim = width // heads
    scale = head_dim ** (-0.5)
    direct = upstream * valid
    d_branch = direct.astype(jnp.bfloat16)
    grad_bdown = jnp.sum(d_branch.astype(jnp.float32), axis=0)
    d_activated = contract_cols(d_branch, w_down)
    _, gelu_back = jax.vjp(jax.nn.gelu, hidden)
    d_hidden = gelu_back(d_activated)[0].astype(jnp.bfloat16)
    grad_bup = jnp.sum(d_hidden.astype(jnp.float32), axis=0)
    d_second = contract_cols(d_hidden, w_up)
    _, second_back = jax.vjp(
        norm_affine, middle, gain_two.astype(jnp.float32), shift_two.astype(jnp.float32)
    )
    d_middle, grad_gain_two, grad_shift_two = second_back(d_second)
    d_middle = d_middle + direct
    d_attn = d_middle.astype(jnp.bfloat16)
    grad_bout = jnp.sum(d_attn.astype(jnp.float32), axis=0)
    d_mixed = contract_cols(d_attn, w_out).astype(jnp.bfloat16).reshape(rows, heads, head_dim)
    grad_values = jnp.einsum("hij,ihd->jhd", probs_low, d_mixed, preferred_element_type=jnp.float32)
    d_probs = jnp.einsum("ihd,jhd->hij", d_mixed, values, preferred_element_type=jnp.float32)
    d_scores = (probs * (d_probs - jnp.sum(probs * d_probs, axis=-1, keepdims=True))).astype(
        jnp.bfloat16
    )
    grad_query = (
        jnp.einsum("hij,jhd->ihd", d_scores, keys, preferred_element_type=jnp.float32) * scale
    )
    grad_keys = (
        jnp.einsum("hij,ihd->jhd", d_scores, query, preferred_element_type=jnp.float32) * scale
    )
    d_qkv = jnp.concatenate(
        [
            grad_query.reshape(rows, width),
            grad_keys.reshape(rows, width),
            grad_values.reshape(rows, width),
        ],
        axis=1,
    ).astype(jnp.bfloat16)
    d_normed = contract_cols(d_qkv, w_qkv)
    _, first_back = jax.vjp(
        norm_affine, inputs, gain_one.astype(jnp.float32), shift_one.astype(jnp.float32)
    )
    d_inputs, grad_gain_one, grad_shift_one = first_back(d_normed)
    d_inputs = d_inputs + d_middle
    per_distance = diagonal_sums(d_scores.astype(jnp.float32))
    grad_table = jnp.dot(onehot, per_distance.T, precision=highest).reshape(-1)
    factors = (normed, d_qkv, mixed, d_attn, second, d_hidden, activated, d_branch)
    small = (
        grad_gain_one,
        grad_shift_one,
        grad_gain_two,
        grad_shift_two,
        grad_bout,
        grad_bup,
        grad_bdown,
        grad_table,
    )
    return (d_inputs, factors, small)


def local(
    audio_in,
    out_grad,
    item_len,
    rel_bucket,
    w_qkv,
    w_out,
    w_up,
    w_down,
    ln1_gain,
    ln1_bias,
    ln2_gain,
    ln2_bias,
    b_out,
    b_up,
    b_down,
    rel_table,
):
    section = lax.axis_index("section")
    micro = audio_in.shape[0]
    rows = audio_in.shape[2]
    width = audio_in.shape[3]
    qkv_part = w_qkv[0].astype(jnp.bfloat16)
    out_part = w_out[0].astype(jnp.bfloat16)
    up_part = w_up[0].astype(jnp.bfloat16)
    down_part = w_down[0].astype(jnp.bfloat16)
    gain_one_part = ln1_gain[0].astype(jnp.bfloat16)
    shift_one_part = ln1_bias[0].astype(jnp.bfloat16)
    gain_two_part = ln2_gain[0].astype(jnp.bfloat16)
    shift_two_part = ln2_bias[0].astype(jnp.bfloat16)
    bias_out_part = b_out[0].astype(jnp.bfloat16)
    bias_up_part = b_up[0].astype(jnp.bfloat16)
    bias_down_part = b_down[0].astype(jnp.bfloat16)
    table_part = rel_table[0].astype(jnp.bfloat16)
    parts = (
        qkv_part,
        out_part,
        up_part,
        down_part,
        gain_one_part,
        shift_one_part,
        gain_two_part,
        shift_two_part,
        bias_out_part,
        bias_up_part,
        bias_down_part,
        table_part,
    )
    gathered = (
        lax.all_gather(qkv_part, "dp", axis=0, tiled=True),
        lax.all_gather(out_part, "dp", axis=0, tiled=True),
        lax.all_gather(up_part, "dp", axis=0, tiled=True),
        lax.all_gather(down_part, "dp", axis=0, tiled=True),
        lax.all_gather(gain_one_part, "dp", axis=0, tiled=True),
        lax.all_gather(shift_one_part, "dp", axis=0, tiled=True),
        lax.all_gather(gain_two_part, "dp", axis=0, tiled=True),
        lax.all_gather(shift_two_part, "dp", axis=0, tiled=True),
        lax.all_gather(bias_out_part, "dp", axis=0, tiled=True),
        lax.all_gather(bias_up_part, "dp", axis=0, tiled=True),
        lax.all_gather(bias_down_part, "dp", axis=0, tiled=True),
        lax.all_gather(table_part, "dp", axis=0, tiled=True),
    )
    onehot = bucket_table(rel_bucket)
    weights = gathered[:11]
    bias = make_bias(gathered[11], onehot)
    lengths = item_len[:, 0]
    hidden_width = gathered[2].shape[1]

    def run_forward(layer_in, length):
        return forward_item(layer_in.astype(jnp.float32), length, bias, weights)[0]

    def skip_forward(layer_in, length):
        return jnp.zeros(layer_in.shape, jnp.float32)

    incoming = jnp.zeros((rows, width), jnp.bfloat16)
    produced = []
    taken = []
    for tick in range(micro + 1):
        slot = tick - section
        active = jnp.logical_and(slot >= 0, slot < micro)
        length = lengths[jnp.clip(slot, 0, micro - 1)]
        own = audio_in[min(tick, micro - 1), 0]
        layer_in = jnp.where(section == 0, own, incoming)
        layer_out = lax.cond(active, run_forward, skip_forward, layer_in, length).astype(
            jnp.bfloat16
        )
        produced.append(layer_out)
        taken.append(layer_in)
        if tick < micro:
            incoming = passed_along(layer_out, "section", 1)
    outputs = jnp.stack(
        [jnp.where(section == 0, produced[batch], produced[batch + 1]) for batch in range(micro)]
    )
    kept = jnp.stack(
        [jnp.where(section == 0, taken[batch], taken[batch + 1]) for batch in range(micro)]
    )
    regathered = (
        lax.all_gather(qkv_part, "dp", axis=0, tiled=True),
        lax.all_gather(out_part, "dp", axis=0, tiled=True),
        lax.all_gather(up_part, "dp", axis=0, tiled=True),
        lax.all_gather(down_part, "dp", axis=0, tiled=True),
        lax.all_gather(gain_one_part, "dp", axis=0, tiled=True),
        lax.all_gather(shift_one_part, "dp", axis=0, tiled=True),
        lax.all_gather(gain_two_part, "dp", axis=0, tiled=True),
        lax.all_gather(shift_two_part, "dp", axis=0, tiled=True),
        lax.all_gather(bias_out_part, "dp", axis=0, tiled=True),
        lax.all_gather(bias_up_part, "dp", axis=0, tiled=True),
        lax.all_gather(bias_down_part, "dp", axis=0, tiled=True),
        lax.all_gather(table_part, "dp", axis=0, tiled=True),
    )
    back_weights = regathered[:11]
    back_bias = make_bias(regathered[11], onehot)

    def run_backward(layer_in, length, upstream):
        return backward_item(
            layer_in.astype(jnp.float32), length, back_bias, back_weights, upstream, onehot
        )

    def skip_backward(layer_in, length, upstream):
        zero_rows = jnp.zeros((rows, width), jnp.bfloat16)
        zero_triple = jnp.zeros((rows, 3 * width), jnp.bfloat16)
        zero_hidden = jnp.zeros((rows, hidden_width), jnp.bfloat16)
        factors = (
            zero_rows,
            zero_triple,
            zero_rows,
            zero_rows,
            zero_rows,
            zero_hidden,
            zero_hidden,
            zero_rows,
        )
        small = tuple((jnp.zeros(piece.shape, jnp.float32) for piece in gathered[4:]))
        return (jnp.zeros(upstream.shape, jnp.float32), factors, small)

    small_totals = tuple((jnp.zeros(piece.shape, jnp.float32) for piece in gathered[4:]))
    shares = tuple((jnp.zeros(piece.shape, jnp.float32) for piece in parts))
    returned = jnp.zeros((rows, width), jnp.bfloat16)
    results = []
    sent_list = []
    factor_list = []
    for tick in range(micro + 1):
        slot = tick - 1 + section
        active = jnp.logical_and(slot >= 0, slot < micro)
        pick = jnp.clip(slot, 0, micro - 1)
        length = lengths[pick]
        layer_in = kept[pick]
        target = out_grad[min(tick, micro - 1), 0].astype(jnp.float32)
        upstream = jnp.where(section == 1, target, returned.astype(jnp.float32))
        d_inputs, factors, small = lax.cond(
            active, run_backward, skip_backward, layer_in, length, upstream
        )
        factor_list.append(factors)
        small_totals = tuple((total + term for total, term in zip(small_totals, small)))
        results.append(d_inputs)
        if tick < micro:
            sent = d_inputs.astype(jnp.bfloat16)
            sent_list.append(lax.optimization_barrier(sent))
            returned = passed_along(sent, "section", -1)
    stacked = tuple(
        (jnp.concatenate([entry[index] for entry in factor_list], axis=0) for index in range(8))
    )
    totals = weight_terms(stacked) + small_totals
    shares = (
        lax.psum_scatter(totals[0], "dp", scatter_dimension=0, tiled=True),
        lax.psum_scatter(totals[1], "dp", scatter_dimension=0, tiled=True),
        lax.psum_scatter(totals[2], "dp", scatter_dimension=0, tiled=True),
        lax.psum_scatter(totals[3], "dp", scatter_dimension=0, tiled=True),
        lax.psum_scatter(totals[4], "dp", scatter_dimension=0, tiled=True),
        lax.psum_scatter(totals[5], "dp", scatter_dimension=0, tiled=True),
        lax.psum_scatter(totals[6], "dp", scatter_dimension=0, tiled=True),
        lax.psum_scatter(totals[7], "dp", scatter_dimension=0, tiled=True),
        lax.psum_scatter(totals[8], "dp", scatter_dimension=0, tiled=True),
        lax.psum_scatter(totals[9], "dp", scatter_dimension=0, tiled=True),
        lax.psum_scatter(totals[10], "dp", scatter_dimension=0, tiled=True),
        lax.psum_scatter(totals[11], "dp", scatter_dimension=0, tiled=True),
    )
    input_grads = jnp.stack(
        [
            jnp.where(section == 0, results[batch + 1], sent_list[batch].astype(jnp.float32))
            for batch in range(micro)
        ]
    )
    grads_out = tuple((share[None] for share in shares))
    return (outputs[None, :, None], input_grads[None, :, None]) + grads_out


E5 = 1e-05
F32 = jnp.float32
BF = jnp.bfloat16
MESH = pl.DeviceIdType.MESH
GELU_K = 0.7978845608028654


class Place:
    def __init__(self):
        self.s = lax.axis_index("section")
        d = lax.axis_index("dp")
        self.x = d % 2
        self.y = (d // 2) % 2
        self.z = (d // 4) % 2
        self.h = d // 8

    def device(self, s=None, x=None, y=None, z=None, h=None):
        s = self.s if s is None else s
        x = self.x if x is None else x
        y = self.y if y is None else y
        z = self.z if z is None else z
        h = self.h if h is None else h
        return (s, x + 2 * y + 4 * z + 8 * h)

    def sibling(self):
        return self.device(s=1 - self.s)

    def team(self, k):
        kx, kz = k % 2, k // 2
        px = self.x + kx * (1 - 2 * self.x)
        pz = self.z + kz * (1 - 2 * self.z)
        return self.device(x=px, z=pz), px + 2 * pz

    def peers(self):
        return (
            self.sibling(),
            self.team(1)[0],
            self.team(2)[0],
            self.team(3)[0],
            self.device(y=1 - self.y),
            self.device(h=1 - self.h),
        )


def meet(peers):
    bell = pltpu.get_barrier_semaphore()
    for peer in peers:
        pl.semaphore_signal(bell, inc=1, device_id=peer, device_id_type=MESH)
    pl.semaphore_wait(bell, len(peers))


def remote(src, dst, send, recv, device):
    return pltpu.make_async_remote_copy(
        src_ref=src, dst_ref=dst, send_sem=send, recv_sem=recv, device_id=device, device_id_type=MESH
    )


def gather_kernel(s1, w2, sp, W1, W2, SP, ls, ss_a, rs_a, ss_y, rs_y, ss_h, rs_h, ss_s, rs_s, ss_p, rs_p):
    p = Place()
    s, x, y, z, h = p.s, p.x, p.y, p.z, p.h
    sib, ypeer, hpeer = p.sibling(), p.device(y=1 - y), p.device(h=1 - h)
    meet(p.peers())
    t = x + 2 * z
    local_sp = pltpu.make_async_copy(sp, SP.at[h, z, y, x, s], ls.at[0])
    local_sp.start()
    mine = pltpu.make_async_copy(s1.at[t], W1.at[s, h, z, y, x], ls.at[1])
    mine.start()
    pending = []
    spread = []
    for k in (1, 2, 3):
        device, slot = p.team(k)
        cp = remote(s1.at[slot], W1.at[s, h, z, y, x], ss_a.at[k - 1], rs_a.at[k - 1], device)
        cp.start()
        spread.append(cp)
    q = 2 * h + y
    own2 = pltpu.make_async_copy(w2, W2.at[s, q], ls.at[2])
    own2.start()

    def rows(hh, yy):
        return W1.at[s, hh, :, yy]

    def down(hh, yy):
        return W2.at[s, 2 * hh + yy]

    def push(src, dst, ss, rs, index, device):
        cp = remote(src, dst, ss.at[index], rs.at[index], device)
        cp.start()
        pending.append(cp)
        return cp

    y0 = push(w2, down(h, y), ss_y, rs_y, 0, ypeer)
    h0 = push(w2, down(h, y), ss_h, rs_h, 0, hpeer)
    s0 = [push(w2, down(h, y), ss_s, rs_s, 0, sib)]
    local_sp.wait()
    views = (
        (SP.at[h, z, y, x, s], sib),
        (SP.at[h, z, y, x], p.team(1)[0]),
        (SP.at[h, z, y], ypeer),
        (SP.at[h, z], p.team(2)[0]),
        (SP.at[h], hpeer),
    )
    for index, (view, device) in enumerate(views):
        cp = remote(view, view, ss_p.at[index], rs_p.at[index], device)
        cp.start()
        cp.wait()
    mine.wait()
    for cp in spread:
        cp.wait_recv()
    y1 = push(rows(h, y), rows(h, y), ss_y, rs_y, 1, ypeer)
    h1 = push(rows(h, y), rows(h, y), ss_h, rs_h, 1, hpeer)
    s0.append(push(rows(h, y), rows(h, y), ss_s, rs_s, 1, sib))
    g = 1 - h
    h0.wait_recv()
    y2 = push(down(g, y), down(g, y), ss_y, rs_y, 2, ypeer)
    s0.append(push(down(g, y), down(g, y), ss_s, rs_s, 2, sib))
    h1.wait_recv()
    y3 = push(rows(g, y), rows(g, y), ss_y, rs_y, 3, ypeer)
    s0.append(push(rows(g, y), rows(g, y), ss_s, rs_s, 3, sib))
    v = 1 - y
    y0.wait_recv()
    s0.append(push(down(h, v), down(h, v), ss_s, rs_s, 4, sib))
    y1.wait_recv()
    s0.append(push(rows(h, v), rows(h, v), ss_s, rs_s, 5, sib))
    y2.wait_recv()
    s0.append(push(down(g, v), down(g, v), ss_s, rs_s, 6, sib))
    y3.wait_recv()
    s0.append(push(rows(g, v), rows(g, v), ss_s, rs_s, 7, sib))
    for cp in s0:
        cp.wait_recv()
    own2.wait()
    for cp in pending + spread:
        cp.wait_send()


def dot(a, b):
    return jnp.dot(a, b, preferred_element_type=F32)


def dot_nt(a, b):
    return lax.dot_general(a, b, (((1,), (1,)), ((), ())), preferred_element_type=F32)


def dot_tn(a, b):
    return lax.dot_general(a, b, (((0,), (0,)), ((), ())), preferred_element_type=F32)


def rows_norm(v):
    centre = v - jnp.mean(v, axis=-1, keepdims=True)
    scale = lax.rsqrt(jnp.mean(centre * centre, axis=-1, keepdims=True) + E5)
    return centre * scale, scale


def norm_back(cot, normed, scale, gain):
    inner = cot * gain
    return scale * (
        inner
        - jnp.mean(inner, axis=-1, keepdims=True)
        - normed * jnp.mean(inner * normed, axis=-1, keepdims=True)
    )


def column_sum(v):
    return jnp.sum(v, axis=0, keepdims=True)


def split_heads(block, count, size):
    lane = lax.broadcasted_iota(jnp.int32, block.shape, 1) // size
    return jnp.concatenate([jnp.where(lane == i, block, jnp.zeros_like(block)) for i in range(count)], axis=0)


def join_heads(block, count, size):
    rows = block.shape[0] // count
    lane = lax.broadcasted_iota(jnp.int32, (rows, block.shape[1]), 1) // size
    total = jnp.where(lane == 0, block[:rows], 0.0)
    for i in range(1, count):
        total = jnp.where(lane == i, block[i * rows : (i + 1) * rows], total)
    return total


def layers_kernel(
    x_ref, og_ref, lens, vec, bias, W1, W2,
    lo, ig, g1, g2, sg, sb, dsum,
    XIN, DY, A, C, FA, MIX, QKV, PR, U, HM, DZ, DAT, DU, DQ,
    XA, XC, XF, XM, XDZ, XDAT, XDU, XDQ, RB, SB, OWN, DH,
    ss_g, rs_g, ss_r, rs_r, ss_x, rs_x, ss_o, rs_o, ls,
):
    p = Place()
    s = p.s
    t = p.x + 2 * p.z
    sib = p.sibling()
    heads, hd = 4, 64
    rows = x_ref.shape[1]
    wide = heads * hd
    meet((sib, p.team(1)[0], p.team(2)[0], p.team(3)[0]))

    XIN[0] = x_ref[s]
    DY[2] = og_ref[s]

    def gather_start(ref, c):
        for k in (1, 2, 3):
            device, _ = p.team(k)
            remote(ref.at[t], ref.at[t], ss_g.at[c, k], rs_g.at[c, k], device).start()

    def gather_take(ref, c, k):
        device, slot = p.team(k)
        remote(ref.at[slot], ref.at[slot], ss_g.at[c, k], rs_g.at[c, k], device).wait_recv()

    def gather_end(ref, c):
        for k in (1, 2, 3):
            device, _ = p.team(k)
            remote(ref.at[t], ref.at[t], ss_g.at[c, k], rs_g.at[c, k], device).wait_send()

    def reduce_put(c, k, part):
        @pl.when(k == 0)
        def _():
            OWN[...] = part

        @pl.when(k > 0)
        def _():
            SB[k] = part.astype(BF)
            device, _ = p.team(k)
            remote(SB.at[k], RB.at[c, k], ss_r.at[c, k], rs_r.at[c, k], device).start()

    def reduce_end(c):
        total = OWN[...]
        for k in (1, 2, 3):
            device, _ = p.team(k)
            remote(SB.at[k], RB.at[c, k], ss_r.at[c, k], rs_r.at[c, k], device).wait()
            total = total + RB[c, k].astype(F32)
        return total

    def each_item(ref, c, body):
        def step(k, carry):
            @pl.when(k > 0)
            def _():
                gather_take(ref, c, k)

            body(k, p.team(k)[1])
            return carry

        lax.fori_loop(0, 4, step, 0)
        gather_end(ref, c)

    def share(layer, pairs):
        @pl.when(s != layer)
        def _():
            for index, src, dst in pairs:
                remote(src.at[layer], dst, ss_x.at[index], rs_x.at[index], sib).start()

    def row(layer, index):
        return vec[layer, index : index + 1, :]

    def wo(layer):
        return W2[layer, :, 0:64, :].reshape(wide, W2.shape[3])

    def wdn(layer):
        return W2[layer, :, 64:, :].reshape(W2.shape[1] * (W2.shape[2] - 64), W2.shape[3])

    position = lax.broadcasted_iota(jnp.int32, (rows, 1), 0)
    valid = (position < lens[t]).astype(F32)

    def forward(layer, carry):
        xin = XIN[layer].astype(F32)
        normed, _ = rows_norm(xin)
        A[layer, t] = (normed * row(layer, 0) + row(layer, 1)).astype(BF)
        c = 2 * layer
        gather_start(A.at[layer], c)

        def attend(k, i):
            qkv = dot(A[layer, i], W1[layer, :, : 3 * wide]).astype(BF)
            QKV[layer, i] = qkv
            stack = split_heads(qkv[:, :wide], heads, hd)
            scores = dot_nt(stack, qkv[:, wide : 2 * wide]) * (hd ** (-0.5)) + bias[layer]
            column = lax.broadcasted_iota(jnp.int32, scores.shape, 1)
            scores = jnp.where(column < lens[i], scores, -1000000000.0)
            raised = jnp.exp(scores - jnp.max(scores, axis=-1, keepdims=True))
            probs = raised / jnp.sum(raised, axis=-1, keepdims=True)
            PR[layer, i] = probs
            mixed = join_heads(dot(probs.astype(BF), qkv[:, 2 * wide :]), heads, hd).astype(BF)
            MIX[layer, i] = mixed
            reduce_put(c, k, dot(mixed, wo(layer)))

        each_item(A.at[layer], c, attend)
        hmid = xin + reduce_end(c) + row(layer, 4)
        HM[layer] = hmid
        normed, _ = rows_norm(hmid)
        C[layer, t] = (normed * row(layer, 2) + row(layer, 3)).astype(BF)
        gather_start(C.at[layer], c + 1)

        def feed(k, i):
            u = dot(C[layer, i], W1[layer, :, 3 * wide :]) + row(layer, 6)
            U[layer, i] = u
            f = (0.5 * u * (1.0 + jnp.tanh(GELU_K * (u + 0.044715 * (u * u * u))))).astype(BF)
            FA[layer, i] = f
            reduce_put(c + 1, k, dot(f, wdn(layer)))

        each_item(C.at[layer], c + 1, feed)
        out = (valid * (HM[layer] + reduce_end(c + 1) + row(layer, 5))).astype(BF)
        XIN[layer + 1] = out
        share(layer, ((0, A, XA), (1, MIX, XM), (2, C, XC), (3, FA, XF)))
        return carry

    lax.fori_loop(0, 2, forward, 0)
    for layer in (0, 1):
        there = remote(XIN.at[layer + 1], lo.at[s], ss_o.at[0], rs_o.at[0], sib)
        here = pltpu.make_async_copy(XIN.at[layer + 1], lo.at[s], ls.at[0])

        @pl.when(s == layer)
        def _():
            here.start()
            here.wait()

        @pl.when(s != layer)
        def _():
            there.start()

    dsum[...] = jnp.zeros_like(dsum)
    sb[...] = jnp.zeros_like(sb)

    def backward(back, carry):
        layer = 1 - back
        c = 4 + 2 * back
        dyv = valid * DY[layer + 1].astype(F32)
        DZ[layer, t] = dyv.astype(BF)
        gather_start(DZ.at[layer], c)
        sg[layer, 5:6, :] = column_sum(dyv)

        def feed(k, i):
            u = U[layer, i]
            square = u * u
            th = jnp.tanh(GELU_K * (u + 0.044715 * (square * u)))
            slope = 0.5 * (1.0 + th) + (0.5 * GELU_K) * u * (1.0 - th * th) * (1.0 + 0.134145 * square)
            du = (dot_nt(DZ[layer, i], wdn(layer)) * slope).astype(BF)
            DU[layer, i] = du
            sb[layer] += column_sum(du.astype(F32))
            reduce_put(c, k, dot_nt(du, W1[layer, :, 3 * wide :]))

        each_item(DZ.at[layer], c, feed)
        dc = reduce_end(c)
        normed, scale = rows_norm(HM[layer])
        sg[layer, 2:3, :] = column_sum(dc * normed)
        sg[layer, 3:4, :] = column_sum(dc)
        dh = valid * DY[layer + 1].astype(F32) + norm_back(dc, normed, scale, row(layer, 2))
        DH[...] = dh
        dattn = dh.astype(BF)
        DAT[layer, t] = dattn
        gather_start(DAT.at[layer], c + 1)
        sg[layer, 4:5, :] = column_sum(dattn.astype(F32))

        def attend(k, i):
            dmixed = dot_nt(DAT[layer, i], wo(layer)).astype(BF)
            qkv = QKV[layer, i]
            probs = PR[layer, i]
            stack = split_heads(dmixed, heads, hd)
            dprobs = dot_nt(stack, qkv[:, 2 * wide :])
            dscores = (probs * (dprobs - jnp.sum(probs * dprobs, axis=-1, keepdims=True))).astype(BF)
            dsum[layer] += dscores.astype(F32)
            dq = join_heads(dot(dscores, qkv[:, wide : 2 * wide]), heads, hd) * (hd ** (-0.5))
            dk = dot_tn(dscores, split_heads(qkv[:, :wide], heads, hd)) * (hd ** (-0.5))
            dv = dot_tn(probs.astype(BF), stack)
            DQ[layer, i, :, :wide] = dq.astype(BF)
            DQ[layer, i, :, wide : 2 * wide] = dk.astype(BF)
            DQ[layer, i, :, 2 * wide :] = dv.astype(BF)
            reduce_put(c + 1, k, dot_nt(DQ[layer, i], W1[layer, :, : 3 * wide]))

        each_item(DAT.at[layer], c + 1, attend)
        da = reduce_end(c + 1)
        normed, scale = rows_norm(XIN[layer].astype(F32))
        sg[layer, 0:1, :] = column_sum(da * normed)
        sg[layer, 1:2, :] = column_sum(da)
        dx = DH[...] + norm_back(da, normed, scale, row(layer, 0))
        low = dx.astype(BF)
        DY[layer] = low
        IGS = DH
        IGS[...] = jnp.where(layer == 1, low.astype(F32), dx)
        there = remote(IGS, ig.at[s], ss_o.at[1], rs_o.at[1], sib)
        here = pltpu.make_async_copy(IGS, ig.at[s], ls.at[0])

        @pl.when(s == layer)
        def _():
            here.start()
            here.wait()

        @pl.when(s != layer)
        def _():
            there.start()
            there.wait_send()

        share(layer, ((4, DZ, XDZ), (5, DAT, XDAT), (6, DU, XDU), (7, DQ, XDQ)))

        @pl.when(s == layer)
        def _():
            for index, src, dst in (
                (0, A, XA), (1, MIX, XM), (2, C, XC), (3, FA, XF),
                (4, DZ, XDZ), (5, DAT, XDAT), (6, DU, XDU), (7, DQ, XDQ),
            ):
                remote(src.at[layer], dst, ss_x.at[index], rs_x.at[index], sib).wait_recv()

            def flat(ref, lanes):
                block = ref[:, :, lanes]
                return block.reshape(block.shape[0] * block.shape[1], block.shape[2])

            def product(own_l, other_l, own_r, other_r, lanes, span):
                every = pl.ds(0, span)
                return dot_tn(flat(own_l, lanes), flat(own_r, every)) + dot_tn(
                    flat(other_l, lanes), flat(other_r, every)
                )

            def tile(j, carry):
                lanes = pl.ds(pl.multiple_of(j * 256, 256), 256)
                g1[lanes, : 3 * wide] = product(
                    A.at[layer], XA, DQ.at[layer], XDQ, lanes, 3 * wide
                ).astype(BF)
                g1[lanes, 3 * wide :] = product(
                    C.at[layer], XC, DU.at[layer], XDU, lanes, U.shape[3]
                ).astype(BF)
                g2[j, 64:, :] = product(
                    FA.at[layer], XF, DZ.at[layer], XDZ, lanes, x_ref.shape[2]
                ).astype(BF)
                return carry

            lax.fori_loop(0, 4, tile, 0)
            out = product(MIX.at[layer], XM, DAT.at[layer], XDAT, pl.ds(0, wide), x_ref.shape[2]).astype(BF)
            for j in range(4):
                g2[j, 0:64, :] = out[j * 64 : (j + 1) * 64]

        return carry

    lax.fori_loop(0, 2, backward, 0)
    for index, src, dst in (
        (0, A, XA), (1, MIX, XM), (2, C, XC), (3, FA, XF),
        (4, DZ, XDZ), (5, DAT, XDAT), (6, DU, XDU), (7, DQ, XDQ),
    ):
        remote(src.at[1 - s], dst, ss_x.at[index], rs_x.at[index], sib).wait_send()
    remote(XIN.at[1], lo.at[1 - s], ss_o.at[0], rs_o.at[0], sib).wait()
    remote(DH, ig.at[1 - s], ss_o.at[1], rs_o.at[1], sib).wait_recv()


def scatter_kernel(
    g1, g2, msg, o1, o2, so,
    YR1, YR2, ZS1, ZS2, ZR1, ZR2, TS, TR, M, MR,
    ss_y, rs_y, ss_h, rs_h, ss_t, rs_t, ss_m, rs_m,
):
    p = Place()
    x, y, z, h, s = p.x, p.y, p.z, p.h, p.s
    ypeer, hpeer = p.device(y=1 - y), p.device(h=1 - h)
    meet(p.peers())
    g, v = 1 - h, 1 - y
    ys = []
    for n, hh in enumerate((g, h)):
        a = remote(g1.at[hh, :, v], YR1.at[hh], ss_y.at[2 * n], rs_y.at[2 * n], ypeer)
        b = remote(g2.at[2 * hh + v], YR2.at[hh], ss_y.at[2 * n + 1], rs_y.at[2 * n + 1], ypeer)
        a.start()
        b.start()
        ys += [a, b]
    M[...] = msg[...]
    steps = (
        (M.at[g], MR.at[0:1, 0:2, 0:2, 0:2, 0:2], M.at[h], hpeer),
    )
    del steps

    def fold(n, send, keep, land, device):
        cp = remote(send, land, ss_m.at[n], rs_m.at[n], device)
        cp.start()
        cp.wait()
        keep[...] += land[...]

    fold(0, M.at[g], M.at[h], MR.at[0], hpeer)
    fold(1, M.at[h, 1 - z], M.at[h, z], MR.at[1, 0], p.team(2)[0])
    fold(2, M.at[h, z, v], M.at[h, z, y], MR.at[1, 1, 0], ypeer)
    fold(3, M.at[h, z, y, 1 - x], M.at[h, z, y, x], MR.at[1, 1, 1, 0], p.team(1)[0])
    fold(4, M.at[h, z, y, x, 1 - s], M.at[h, z, y, x, s], MR.at[1, 1, 1, 1, 0], p.sibling())
    so[...] = M[h, z, y, x, s]
    for cp in ys[:2]:
        cp.wait_recv()
    ZS1[...] = (g1[g, :, y].astype(F32) + YR1[g].astype(F32)).astype(BF)
    ZS2[...] = (g2[2 * g + y].astype(F32) + YR2[g].astype(F32)).astype(BF)
    za = remote(ZS1, ZR1, ss_h.at[0], rs_h.at[0], hpeer)
    zb = remote(ZS2, ZR2, ss_h.at[1], rs_h.at[1], hpeer)
    za.start()
    zb.start()
    for cp in ys[2:]:
        cp.wait_recv()
    za.wait_recv()
    t = x + 2 * z

    def total(zz, xx):
        return g1[h, zz, y, xx].astype(F32) + YR1[h, zz, xx].astype(F32) + ZR1[zz, xx].astype(F32)

    ts = []
    for k in (1, 2, 3):
        device, _ = p.team(k)
        kx, kz = k % 2, k // 2
        xx = x + kx * (1 - 2 * x)
        zz = z + kz * (1 - 2 * z)
        TS[k] = total(zz, xx).astype(BF)
        cp = remote(TS.at[k], TR.at[k], ss_t.at[k], rs_t.at[k], device)
        cp.start()
        ts.append(cp)
    o1[t] = total(z, x)
    zb.wait_recv()
    o2[...] = g2[2 * h + y].astype(F32) + YR2[h].astype(F32) + ZR2[...].astype(F32)
    for k in (1, 2, 3):
        ts[k - 1].wait_recv()
        _, slot = p.team(k)
        o1[slot] = TR[k].astype(F32)
    for cp in ys + [za, zb] + ts:
        cp.wait_send()


def vm(n=1):
    return [pl.BlockSpec(memory_space=pltpu.VMEM)] * n


def hb(n=1):
    return [pl.BlockSpec(memory_space=pltpu.HBM)] * n


def sems(*shape):
    return pltpu.SemaphoreType.DMA(shape)


def shape_of(dims, kind):
    return jax.ShapeDtypeStruct(dims, kind)


def team_local(
    audio_in, out_grad, item_len, rel_bucket, w_qkv, w_out, w_up, w_down,
    ln1_gain, ln1_bias, ln2_gain, ln2_bias, b_out, b_up, b_down, rel_table,
):
    s = lax.axis_index("section")
    d = lax.axis_index("dp")
    x, y, z, h = d % 2, (d // 2) % 2, (d // 4) % 2, d // 8
    rows, width = audio_in.shape[2], audio_in.shape[3]
    part = w_qkv.shape[1]
    hidden = w_up.shape[2]
    block = hidden // 16
    wide, team_ff = width // 4, hidden // 4
    cols = 3 * wide + team_ff
    tall = part + block

    part_qkv = w_qkv[0].astype(BF).reshape(part, 3, 2, 2, 2, 2, 64).transpose(3, 5, 0, 1, 2, 4, 6)
    part_up = w_up[0].astype(BF).reshape(part, 2, 2, 2, 2, block).transpose(2, 4, 0, 1, 3, 5)
    s1 = jnp.concatenate(
        [part_qkv.reshape(4, part, 3 * wide), part_up.reshape(4, part, team_ff)], axis=2
    )
    w2 = jnp.concatenate([w_out[0], w_down[0]], axis=0).astype(BF)
    vectors = jnp.concatenate(
        [ln1_gain, ln1_bias, ln2_gain, ln2_bias, b_out, b_down, b_up], axis=1
    ).reshape(-1, 128)
    vectors = lax.reduce_precision(vectors, 8, 7)
    table = jnp.pad(lax.reduce_precision(rel_table, 8, 7), ((0, 0), (0, 96)))
    counts = jnp.pad(item_len.astype(F32).reshape(1, 2), ((0, 0), (0, 126)))
    small = jnp.concatenate(
        [vectors, table, counts, jnp.zeros((8 - 2 - vectors.shape[0], 128), F32)], axis=0
    )

    W1, W2, SP = pl.pallas_call(
        gather_kernel,
        out_shape=(
            shape_of((2, 2, 2, 2, 2, part, cols), BF),
            shape_of((2, 4, tall, width), BF),
            shape_of((2, 2, 2, 2, 2, 8, 128), F32),
        ),
        in_specs=hb(3),
        out_specs=tuple(hb(3)),
        scratch_shapes=[
            sems(3), sems(3), sems(3), sems(4), sems(4), sems(2), sems(2), sems(8), sems(8), sems(5), sems(5),
        ],
        compiler_params=pltpu.CompilerParams(collective_id=0, has_side_effects=True),
        name="gather_weights",
    )(s1, w2, small)

    SPd = SP.reshape(16, 2, 8, 128).transpose(1, 0, 2, 3)
    six = SPd[:, :, :3].reshape(2, 16, 6, 64).transpose(0, 2, 1, 3).reshape(2, 6, width)
    ups = SPd[:, :, 3:5].reshape(2, 2, 2, 2, 2, block)
    ups = lax.dynamic_index_in_dim(lax.dynamic_index_in_dim(ups, z, 2, False), x, 3, False)
    vec = jnp.concatenate([six, ups.reshape(2, 1, team_ff), jnp.zeros((2, 1, width), F32)], axis=1)
    lens_all = SPd[0, :, 6, :2]
    lens = lax.dynamic_index_in_dim(lens_all, s, 1, False).reshape(2, 2, 2, 2)
    lens = lax.dynamic_index_in_dim(lax.dynamic_index_in_dim(lens, h, 0, False), y, 1, False)
    lens = lens.reshape(4).astype(jnp.int32)
    onehot = bucket_table(rel_bucket)
    tables = SPd[:, :, 5, :32].reshape(2, NB, 2, 2, 2, 2)
    tables = lax.dynamic_index_in_dim(lax.dynamic_index_in_dim(tables, z, 3, False), x, 4, False)
    tables = tables.reshape(2, NB, 4)
    distance = jnp.einsum("lbh,bm->lhm", tables, onehot, precision=highest).reshape(8, rows)
    bias = toeplitz_rows(distance).reshape(2, 4, rows, rows)
    causal = jnp.arange(rows)[None, :] <= jnp.arange(rows)[:, None]
    bias = jnp.where(causal, bias, -1000000000.0).reshape(2, 4 * rows, rows)

    W1f = W1.reshape(2, width, cols)
    act = lambda n: pltpu.VMEM((2, 4, rows, n), BF)
    mate = lambda n: pltpu.VMEM((4, rows, n), BF)
    lo, ig, g1, g2, sg, sb, dsum = pl.pallas_call(
        layers_kernel,
        out_shape=(
            shape_of((2, rows, width), BF),
            shape_of((2, rows, width), F32),
            shape_of((width, cols), BF),
            shape_of((4, tall, width), BF),
            shape_of((2, 8, width), F32),
            shape_of((2, 1, team_ff), F32),
            shape_of((2, 4 * rows, rows), F32),
        ),
        in_specs=vm(2) + [pl.BlockSpec(memory_space=pltpu.SMEM)] + vm(4),
        out_specs=tuple(vm(7)),
        scratch_shapes=[
            pltpu.VMEM((3, rows, width), BF), pltpu.VMEM((3, rows, width), BF),
            act(width), act(width), act(team_ff), act(wide), act(3 * wide),
            pltpu.VMEM((2, 4, 4 * rows, rows), F32), pltpu.VMEM((2, 4, rows, team_ff), F32),
            pltpu.VMEM((2, rows, width), F32),
            act(width), act(width), act(team_ff), act(3 * wide),
            mate(width), mate(width), mate(team_ff), mate(wide),
            mate(width), mate(width), mate(team_ff), mate(3 * wide),
            pltpu.VMEM((8, 4, rows, width), BF), pltpu.VMEM((4, rows, width), BF),
            pltpu.VMEM((rows, width), F32), pltpu.VMEM((rows, width), F32),
            sems(8, 4), sems(8, 4), sems(8, 4), sems(8, 4), sems(8), sems(8), sems(2), sems(2), sems(1),
        ],
        compiler_params=pltpu.CompilerParams(
            collective_id=1, has_side_effects=True, vmem_limit_bytes=62 << 20
        ),
        name="layers",
    )(audio_in.reshape(2, rows, width), out_grad.reshape(2, rows, width), lens, vec, bias, W1f, W2)

    per_distance = diagonal_sums(dsum.reshape(8, rows, rows))
    buckets = jnp.einsum("bm,cm->cb", onehot, per_distance, precision=highest).reshape(2, 2, 2, NB)
    spot = ((jnp.arange(2)[:, None] == z) & (jnp.arange(2)[None, :] == x)).astype(F32)
    table_msg = jnp.einsum("lhyb,zx->lbhzyx", buckets, spot, precision=highest).reshape(2, 16, 32)
    table_msg = jnp.pad(table_msg, ((0, 0), (0, 0), (0, 96))).reshape(2, 16, 1, 128)
    six_msg = sg[:, :6].reshape(2, 6, 16, 64).transpose(0, 2, 1, 3).reshape(2, 16, 3, 128)
    up_msg = sb.reshape(2, 2, 1, 2, 1, 2, 128) * spot.reshape(1, 1, 2, 1, 2, 1, 1)
    up_msg = up_msg.reshape(2, 16, 2, 128)
    msg = jnp.concatenate([six_msg, up_msg, table_msg, jnp.zeros((2, 16, 2, 128), F32)], axis=2)
    msg = msg.transpose(1, 0, 2, 3).reshape(2, 2, 2, 2, 2, 8, 128)

    o1, o2, so = pl.pallas_call(
        scatter_kernel,
        out_shape=(
            shape_of((4, part, cols), F32),
            shape_of((tall, width), F32),
            shape_of((8, 128), F32),
        ),
        in_specs=vm(3),
        out_specs=tuple(vm(3)),
        scratch_shapes=[
            pltpu.VMEM((2, 2, 2, part, cols), BF), pltpu.VMEM((2, tall, width), BF),
            pltpu.VMEM((2, 2, part, cols), BF), pltpu.VMEM((tall, width), BF),
            pltpu.VMEM((2, 2, part, cols), BF), pltpu.VMEM((tall, width), BF),
            pltpu.VMEM((4, part, cols), BF), pltpu.VMEM((4, part, cols), BF),
            pltpu.VMEM((2, 2, 2, 2, 2, 8, 128), F32), pltpu.VMEM((2, 2, 2, 2, 2, 8, 128), F32),
            sems(4), sems(4), sems(2), sems(2), sems(4), sems(4), sems(5), sems(5),
        ],
        compiler_params=pltpu.CompilerParams(
            collective_id=2, has_side_effects=True, vmem_limit_bytes=62 << 20
        ),
        name="scatter_grads",
    )(g1.reshape(2, 2, 2, 2, part, cols), g2, msg)

    grad_qkv = o1[:, :, : 3 * wide].reshape(2, 2, part, 3, 2, 2, 64).transpose(2, 3, 4, 0, 5, 1, 6)
    grad_up = o1[:, :, 3 * wide :].reshape(2, 2, part, 2, 2, block).transpose(2, 3, 0, 4, 1, 5)
    six_out = so[:3].reshape(6, 64)
    return (
        lo[None, :, None],
        ig[None, :, None],
        grad_qkv.reshape(1, part, 3 * width),
        o2[None, :part],
        grad_up.reshape(1, part, hidden),
        o2[None, part:],
        six_out[0:1],
        six_out[1:2],
        six_out[2:3],
        six_out[3:4],
        six_out[4:5],
        so[3:5].reshape(1, block),
        six_out[5:6],
        so[5:6, :32],
    )


def solution(mesh):
    fits = mesh.shape["dp"] == 16 and mesh.shape["section"] == 2
    return jax.shard_map(
        team_local if fits else local,
        mesh=mesh,
        in_specs=(
            P(None, "dp", None, None),
            P(None, "dp", None, None),
            P(None, "dp"),
            P(),
            P("section", "dp", None),
            P("section", "dp", None),
            P("section", "dp", None),
            P("section", "dp", None),
            P("section", "dp"),
            P("section", "dp"),
            P("section", "dp"),
            P("section", "dp"),
            P("section", "dp"),
            P("section", "dp"),
            P("section", "dp"),
            P("section", "dp"),
        ),
        out_specs=(
            P("section", None, "dp", None, None),
            P("section", None, "dp", None, None),
            P("section", "dp", None),
            P("section", "dp", None),
            P("section", "dp", None),
            P("section", "dp", None),
            P("section", "dp"),
            P("section", "dp"),
            P("section", "dp"),
            P("section", "dp"),
            P("section", "dp"),
            P("section", "dp"),
            P("section", "dp"),
            P("section", "dp"),
        ),
        check_vma=False,
    )
```

```python
import jax
import jax.numpy as jnp
from jax import lax
from jax.experimental import pallas as pl
from jax.experimental.pallas import tpu as pltpu
from jax.sharding import PartitionSpec as P

H = 16
NB = 32


epsilon = 1e-05
highest = lax.Precision.HIGHEST


def passed_along(block, axis, distance):
    devices = range(lax.axis_size(axis))
    route = [(i - distance, i) for i in devices if i - distance in devices]
    return lax.ppermute(block, axis, route)


def norm_rows(values):
    centre = values - jnp.mean(values, axis=-1, keepdims=True)
    return centre * lax.rsqrt(jnp.mean(centre * centre, axis=-1, keepdims=True) + epsilon)


def norm_affine(values, gain, shift):
    return norm_rows(values) * gain + shift


def contract_rows(left, right):
    return lax.dot_general(
        left, right, (((0,), (0,)), ((), ())), preferred_element_type=jnp.float32
    )


def contract_cols(left, right):
    return lax.dot_general(
        left, right, (((1,), (1,)), ((), ())), preferred_element_type=jnp.float32
    )


def toeplitz_rows(values):
    heads, length = values.shape
    reverse = jnp.flip(values, axis=1)
    padded = jnp.concatenate([reverse, jnp.zeros_like(reverse)], axis=1)
    tiled = jnp.tile(padded, (1, length))[:, : length * (2 * length - 1)]
    return tiled.reshape(heads, length, 2 * length - 1)[:, :, length - 1 :]


def diagonal_sums(grid):
    heads, length, _ = grid.shape
    widened = jnp.concatenate([jnp.zeros((heads, length, length - 1), grid.dtype), grid], axis=2)
    flat = widened.reshape(heads, length * (2 * length - 1))
    flat = jnp.concatenate([flat, jnp.zeros((heads, length), grid.dtype)], axis=1)
    folded = jnp.sum(flat.reshape(heads, length, 2 * length), axis=1)
    return jnp.flip(folded[:, :length], axis=1)


def bucket_table(buckets):
    return (buckets[None, :] == jnp.arange(NB, dtype=jnp.int32)[:, None]).astype(jnp.float32)


def make_bias(table_flat, onehot):
    table = table_flat.astype(jnp.float32).reshape(NB, H)
    per_distance = jnp.dot(table.T, onehot, precision=highest)
    return toeplitz_rows(per_distance)


def weight_terms(factors):
    normed, d_qkv, mixed, d_attn, second, d_hidden, activated, d_branch = factors
    return (
        contract_rows(normed, d_qkv),
        contract_rows(mixed, d_attn),
        contract_rows(second, d_hidden),
        contract_rows(activated, d_branch),
    )


def forward_item(inputs, length, bias, weights):
    (
        w_qkv,
        w_out,
        w_up,
        w_down,
        gain_one,
        shift_one,
        gain_two,
        shift_two,
        bias_out,
        bias_up,
        bias_down,
    ) = weights
    rows, width = inputs.shape
    heads = bias.shape[0]
    head_dim = width // heads
    scale = head_dim ** (-0.5)
    position = jnp.arange(rows)
    visible = (position[None, :] <= position[:, None])[None] & (position[None, None, :] < length)
    valid = (position < length).astype(jnp.float32)[:, None]
    normed = norm_affine(
        inputs, gain_one.astype(jnp.float32), shift_one.astype(jnp.float32)
    ).astype(jnp.bfloat16)
    qkv = jnp.dot(normed, w_qkv, preferred_element_type=jnp.float32).astype(jnp.bfloat16)
    query = qkv[:, :width].reshape(rows, heads, head_dim)
    keys = qkv[:, width : 2 * width].reshape(rows, heads, head_dim)
    values = qkv[:, 2 * width :].reshape(rows, heads, head_dim)
    scores = (
        jnp.einsum("ihd,jhd->hij", query, keys, preferred_element_type=jnp.float32) * scale + bias
    )
    scores = jnp.where(visible, scores, -1000000000.0)
    raised = jnp.exp(scores - jnp.max(scores, axis=-1, keepdims=True))
    probs = raised / jnp.sum(raised, axis=-1, keepdims=True)
    probs_low = probs.astype(jnp.bfloat16)
    mixed = (
        jnp.einsum("hij,jhd->ihd", probs_low, values, preferred_element_type=jnp.float32)
        .reshape(rows, width)
        .astype(jnp.bfloat16)
    )
    middle = (
        inputs
        + jnp.dot(mixed, w_out, preferred_element_type=jnp.float32)
        + bias_out.astype(jnp.float32)
    )
    second = norm_affine(
        middle, gain_two.astype(jnp.float32), shift_two.astype(jnp.float32)
    ).astype(jnp.bfloat16)
    hidden = jnp.dot(second, w_up, preferred_element_type=jnp.float32) + bias_up.astype(jnp.float32)
    activated = jax.nn.gelu(hidden).astype(jnp.bfloat16)
    result = (
        middle
        + jnp.dot(activated, w_down, preferred_element_type=jnp.float32)
        + bias_down.astype(jnp.float32)
    ) * valid
    saved = (
        normed,
        query,
        keys,
        values,
        probs,
        probs_low,
        mixed,
        middle,
        second,
        hidden,
        activated,
        valid,
    )
    return (result, saved)


def backward_item(inputs, length, bias, weights, upstream, onehot):
    (
        w_qkv,
        w_out,
        w_up,
        w_down,
        gain_one,
        shift_one,
        gain_two,
        shift_two,
        bias_out,
        bias_up,
        bias_down,
    ) = weights
    _, saved = forward_item(inputs, length, bias, weights)
    (
        normed,
        query,
        keys,
        values,
        probs,
        probs_low,
        mixed,
        middle,
        second,
        hidden,
        activated,
        valid,
    ) = saved
    rows, width = inputs.shape
    heads = bias.shape[0]
    head_dim = width // heads
    scale = head_dim ** (-0.5)
    direct = upstream * valid
    d_branch = direct.astype(jnp.bfloat16)
    grad_bdown = jnp.sum(d_branch.astype(jnp.float32), axis=0)
    d_activated = contract_cols(d_branch, w_down)
    _, gelu_back = jax.vjp(jax.nn.gelu, hidden)
    d_hidden = gelu_back(d_activated)[0].astype(jnp.bfloat16)
    grad_bup = jnp.sum(d_hidden.astype(jnp.float32), axis=0)
    d_second = contract_cols(d_hidden, w_up)
    _, second_back = jax.vjp(
        norm_affine, middle, gain_two.astype(jnp.float32), shift_two.astype(jnp.float32)
    )
    d_middle, grad_gain_two, grad_shift_two = second_back(d_second)
    d_middle = d_middle + direct
    d_attn = d_middle.astype(jnp.bfloat16)
    grad_bout = jnp.sum(d_attn.astype(jnp.float32), axis=0)
    d_mixed = contract_cols(d_attn, w_out).astype(jnp.bfloat16).reshape(rows, heads, head_dim)
    grad_values = jnp.einsum("hij,ihd->jhd", probs_low, d_mixed, preferred_element_type=jnp.float32)
    d_probs = jnp.einsum("ihd,jhd->hij", d_mixed, values, preferred_element_type=jnp.float32)
    d_scores = (probs * (d_probs - jnp.sum(probs * d_probs, axis=-1, keepdims=True))).astype(
        jnp.bfloat16
    )
    grad_query = (
        jnp.einsum("hij,jhd->ihd", d_scores, keys, preferred_element_type=jnp.float32) * scale
    )
    grad_keys = (
        jnp.einsum("hij,ihd->jhd", d_scores, query, preferred_element_type=jnp.float32) * scale
    )
    d_qkv = jnp.concatenate(
        [
            grad_query.reshape(rows, width),
            grad_keys.reshape(rows, width),
            grad_values.reshape(rows, width),
        ],
        axis=1,
    ).astype(jnp.bfloat16)
    d_normed = contract_cols(d_qkv, w_qkv)
    _, first_back = jax.vjp(
        norm_affine, inputs, gain_one.astype(jnp.float32), shift_one.astype(jnp.float32)
    )
    d_inputs, grad_gain_one, grad_shift_one = first_back(d_normed)
    d_inputs = d_inputs + d_middle
    per_distance = diagonal_sums(d_scores.astype(jnp.float32))
    grad_table = jnp.dot(onehot, per_distance.T, precision=highest).reshape(-1)
    factors = (normed, d_qkv, mixed, d_attn, second, d_hidden, activated, d_branch)
    small = (
        grad_gain_one,
        grad_shift_one,
        grad_gain_two,
        grad_shift_two,
        grad_bout,
        grad_bup,
        grad_bdown,
        grad_table,
    )
    return (d_inputs, factors, small)


def local(
    audio_in,
    out_grad,
    item_len,
    rel_bucket,
    w_qkv,
    w_out,
    w_up,
    w_down,
    ln1_gain,
    ln1_bias,
    ln2_gain,
    ln2_bias,
    b_out,
    b_up,
    b_down,
    rel_table,
):
    section = lax.axis_index("section")
    micro = audio_in.shape[0]
    rows = audio_in.shape[2]
    width = audio_in.shape[3]
    qkv_part = w_qkv[0].astype(jnp.bfloat16)
    out_part = w_out[0].astype(jnp.bfloat16)
    up_part = w_up[0].astype(jnp.bfloat16)
    down_part = w_down[0].astype(jnp.bfloat16)
    gain_one_part = ln1_gain[0].astype(jnp.bfloat16)
    shift_one_part = ln1_bias[0].astype(jnp.bfloat16)
    gain_two_part = ln2_gain[0].astype(jnp.bfloat16)
    shift_two_part = ln2_bias[0].astype(jnp.bfloat16)
    bias_out_part = b_out[0].astype(jnp.bfloat16)
    bias_up_part = b_up[0].astype(jnp.bfloat16)
    bias_down_part = b_down[0].astype(jnp.bfloat16)
    table_part = rel_table[0].astype(jnp.bfloat16)
    parts = (
        qkv_part,
        out_part,
        up_part,
        down_part,
        gain_one_part,
        shift_one_part,
        gain_two_part,
        shift_two_part,
        bias_out_part,
        bias_up_part,
        bias_down_part,
        table_part,
    )
    gathered = (
        lax.all_gather(qkv_part, "dp", axis=0, tiled=True),
        lax.all_gather(out_part, "dp", axis=0, tiled=True),
        lax.all_gather(up_part, "dp", axis=0, tiled=True),
        lax.all_gather(down_part, "dp", axis=0, tiled=True),
        lax.all_gather(gain_one_part, "dp", axis=0, tiled=True),
        lax.all_gather(shift_one_part, "dp", axis=0, tiled=True),
        lax.all_gather(gain_two_part, "dp", axis=0, tiled=True),
        lax.all_gather(shift_two_part, "dp", axis=0, tiled=True),
        lax.all_gather(bias_out_part, "dp", axis=0, tiled=True),
        lax.all_gather(bias_up_part, "dp", axis=0, tiled=True),
        lax.all_gather(bias_down_part, "dp", axis=0, tiled=True),
        lax.all_gather(table_part, "dp", axis=0, tiled=True),
    )
    onehot = bucket_table(rel_bucket)
    weights = gathered[:11]
    bias = make_bias(gathered[11], onehot)
    lengths = item_len[:, 0]
    hidden_width = gathered[2].shape[1]

    def run_forward(layer_in, length):
        return forward_item(layer_in.astype(jnp.float32), length, bias, weights)[0]

    def skip_forward(layer_in, length):
        return jnp.zeros(layer_in.shape, jnp.float32)

    incoming = jnp.zeros((rows, width), jnp.bfloat16)
    produced = []
    taken = []
    for tick in range(micro + 1):
        slot = tick - section
        active = jnp.logical_and(slot >= 0, slot < micro)
        length = lengths[jnp.clip(slot, 0, micro - 1)]
        own = audio_in[min(tick, micro - 1), 0]
        layer_in = jnp.where(section == 0, own, incoming)
        layer_out = lax.cond(active, run_forward, skip_forward, layer_in, length).astype(
            jnp.bfloat16
        )
        produced.append(layer_out)
        taken.append(layer_in)
        if tick < micro:
            incoming = passed_along(layer_out, "section", 1)
    outputs = jnp.stack(
        [jnp.where(section == 0, produced[batch], produced[batch + 1]) for batch in range(micro)]
    )
    kept = jnp.stack(
        [jnp.where(section == 0, taken[batch], taken[batch + 1]) for batch in range(micro)]
    )
    regathered = (
        lax.all_gather(qkv_part, "dp", axis=0, tiled=True),
        lax.all_gather(out_part, "dp", axis=0, tiled=True),
        lax.all_gather(up_part, "dp", axis=0, tiled=True),
        lax.all_gather(down_part, "dp", axis=0, tiled=True),
        lax.all_gather(gain_one_part, "dp", axis=0, tiled=True),
        lax.all_gather(shift_one_part, "dp", axis=0, tiled=True),
        lax.all_gather(gain_two_part, "dp", axis=0, tiled=True),
        lax.all_gather(shift_two_part, "dp", axis=0, tiled=True),
        lax.all_gather(bias_out_part, "dp", axis=0, tiled=True),
        lax.all_gather(bias_up_part, "dp", axis=0, tiled=True),
        lax.all_gather(bias_down_part, "dp", axis=0, tiled=True),
        lax.all_gather(table_part, "dp", axis=0, tiled=True),
    )
    back_weights = regathered[:11]
    back_bias = make_bias(regathered[11], onehot)

    def run_backward(layer_in, length, upstream):
        return backward_item(
            layer_in.astype(jnp.float32), length, back_bias, back_weights, upstream, onehot
        )

    def skip_backward(layer_in, length, upstream):
        zero_rows = jnp.zeros((rows, width), jnp.bfloat16)
        zero_triple = jnp.zeros((rows, 3 * width), jnp.bfloat16)
        zero_hidden = jnp.zeros((rows, hidden_width), jnp.bfloat16)
        factors = (
            zero_rows,
            zero_triple,
            zero_rows,
            zero_rows,
            zero_rows,
            zero_hidden,
            zero_hidden,
            zero_rows,
        )
        small = tuple((jnp.zeros(piece.shape, jnp.float32) for piece in gathered[4:]))
        return (jnp.zeros(upstream.shape, jnp.float32), factors, small)

    small_totals = tuple((jnp.zeros(piece.shape, jnp.float32) for piece in gathered[4:]))
    shares = tuple((jnp.zeros(piece.shape, jnp.float32) for piece in parts))
    returned = jnp.zeros((rows, width), jnp.bfloat16)
    results = []
    sent_list = []
    factor_list = []
    for tick in range(micro + 1):
        slot = tick - 1 + section
        active = jnp.logical_and(slot >= 0, slot < micro)
        pick = jnp.clip(slot, 0, micro - 1)
        length = lengths[pick]
        layer_in = kept[pick]
        target = out_grad[min(tick, micro - 1), 0].astype(jnp.float32)
        upstream = jnp.where(section == 1, target, returned.astype(jnp.float32))
        d_inputs, factors, small = lax.cond(
            active, run_backward, skip_backward, layer_in, length, upstream
        )
        factor_list.append(factors)
        small_totals = tuple((total + term for total, term in zip(small_totals, small)))
        results.append(d_inputs)
        if tick < micro:
            sent = d_inputs.astype(jnp.bfloat16)
            sent_list.append(lax.optimization_barrier(sent))
            returned = passed_along(sent, "section", -1)
    stacked = tuple(
        (jnp.concatenate([entry[index] for entry in factor_list], axis=0) for index in range(8))
    )
    totals = weight_terms(stacked) + small_totals
    shares = (
        lax.psum_scatter(totals[0], "dp", scatter_dimension=0, tiled=True),
        lax.psum_scatter(totals[1], "dp", scatter_dimension=0, tiled=True),
        lax.psum_scatter(totals[2], "dp", scatter_dimension=0, tiled=True),
        lax.psum_scatter(totals[3], "dp", scatter_dimension=0, tiled=True),
        lax.psum_scatter(totals[4], "dp", scatter_dimension=0, tiled=True),
        lax.psum_scatter(totals[5], "dp", scatter_dimension=0, tiled=True),
        lax.psum_scatter(totals[6], "dp", scatter_dimension=0, tiled=True),
        lax.psum_scatter(totals[7], "dp", scatter_dimension=0, tiled=True),
        lax.psum_scatter(totals[8], "dp", scatter_dimension=0, tiled=True),
        lax.psum_scatter(totals[9], "dp", scatter_dimension=0, tiled=True),
        lax.psum_scatter(totals[10], "dp", scatter_dimension=0, tiled=True),
        lax.psum_scatter(totals[11], "dp", scatter_dimension=0, tiled=True),
    )
    input_grads = jnp.stack(
        [
            jnp.where(section == 0, results[batch + 1], sent_list[batch].astype(jnp.float32))
            for batch in range(micro)
        ]
    )
    grads_out = tuple((share[None] for share in shares))
    return (outputs[None, :, None], input_grads[None, :, None]) + grads_out


E5 = 1e-05
F32 = jnp.float32
BF = jnp.bfloat16
MESH = pl.DeviceIdType.MESH
GELU_K = 0.7978845608028654
HD = 64


class Place:
    def __init__(self):
        self.s = lax.axis_index("section")
        d = lax.axis_index("dp")
        self.x = d % 2
        self.y = (d // 2) % 2
        self.z = (d // 4) % 2
        self.h = d // 8
        self.t = self.x + 2 * self.z

    def device(self, s=None, x=None, y=None, z=None, h=None):
        s = self.s if s is None else s
        x = self.x if x is None else x
        y = self.y if y is None else y
        z = self.z if z is None else z
        h = self.h if h is None else h
        return (s, x + 2 * y + 4 * z + 8 * h)

    def sibling(self):
        return self.device(s=1 - self.s)

    def across_y(self):
        return self.device(y=1 - self.y)

    def across_h(self):
        return self.device(h=1 - self.h)

    def mate(self, k):
        return self.x + (k % 2) * (1 - 2 * self.x), self.z + (k // 2) * (1 - 2 * self.z)

    def team(self, k):
        px, pz = self.mate(k)
        return self.device(x=px, z=pz), px + 2 * pz


def remote(src, dst, send, recv, device):
    return pltpu.make_async_remote_copy(
        src_ref=src, dst_ref=dst, send_sem=send, recv_sem=recv, device_id=device, device_id_type=MESH
    )


def dot(a, b):
    return jnp.dot(a, b, preferred_element_type=F32)


def dot_nt(a, b):
    return lax.dot_general(a, b, (((1,), (1,)), ((), ())), preferred_element_type=F32)


def dot_tn(a, b):
    return lax.dot_general(a, b, (((0,), (0,)), ((), ())), preferred_element_type=F32)


def rows_norm(v):
    centre = v - jnp.mean(v, axis=-1, keepdims=True)
    scale = lax.rsqrt(jnp.mean(centre * centre, axis=-1, keepdims=True) + E5)
    return centre * scale, scale


def norm_back(cot, normed, scale, gain):
    inner = cot * gain
    return scale * (
        inner
        - jnp.mean(inner, axis=-1, keepdims=True)
        - normed * jnp.mean(inner * normed, axis=-1, keepdims=True)
    )


def column_sum(v):
    return jnp.sum(v, axis=0, keepdims=True)


def lanes_of(shape, axis=1):
    return lax.broadcasted_iota(jnp.int32, shape, axis)


def split_heads(block, count, size):
    lane = lanes_of(block.shape) // size
    return jnp.concatenate([jnp.where(lane == i, block, jnp.zeros_like(block)) for i in range(count)], axis=0)


def join_heads(block, count, size):
    rows = block.shape[0] // count
    lane = lanes_of((rows, block.shape[1])) // size
    total = jnp.where(lane == 0, block[:rows], 0.0)
    for i in range(1, count):
        total = jnp.where(lane == i, block[i * rows : (i + 1) * rows], total)
    return total


def turn(block, shift):
    width = block.shape[1]
    shift = shift % width
    return jnp.concatenate([block[:, width - shift :], block[:, : width - shift]], axis=1)


def skew(block, length, sign):
    row = lanes_of(block.shape, 0) % length
    for bit in range(7):
        block = jnp.where((row // 2**bit) % 2 == 1, turn(block, sign * 2**bit), block)
    return block


class Part:
    def __init__(self, index, pieces, **refs):
        self.index = index
        self.pieces = pieces
        self.chunks = 2 + pieces
        for name, ref in refs.items():
            setattr(self, name, ref)

    def strip(self, c, rows):
        step = rows // self.pieces
        return pl.ds((c - 2) * step, step)


def step_kernel(
    x_ref, og_ref, il_ref, rb_ref, wq_in, wo_in, wu_in, wd_in,
    v0_ref, v1_ref, v2_ref, v3_ref, v4_ref, v5_ref, bu_ref, rt_ref,
    lo, ig, OQ, OO, OU, OD, OT,
    SQ, SU, WQ, WO, WU, WD, XIN, DY, A, C, FA, MIX, QKV, PR, UF, HM, DZ, DAT, DU, DQ,
    XA, XC, XF, XM, XDZ, XDAT, XDU, XDQ, RB, SB, OWN, DH,
    GQ, GO, GU, GD, YQ, YO, YU, YD, ZSQ, ZSO, ZSU, ZSD, ZRQ, ZRO, ZRU, ZRD, TSQ, TRQ, TSU, TRU,
    SPT, SPX, VEC, LEN, BIAS, PD, SGV, SBU, DS, MT, MR,
    ls, ss_a, rs_a, ss_wy, rs_wy, ss_wh, rs_wh, ss_ws, rs_ws, ss_p, rs_p,
    ss_g, rs_g, ss_r, rs_r, ss_x, rs_x, ss_o, rs_o,
    ss_gy, rs_gy, ss_gh, rs_gh, ss_gt, rs_gt, ss_m, rs_m,
):
    p = Place()
    s, x, y, z, h, t = p.s, p.x, p.y, p.z, p.h, p.t
    sib, ypeer, hpeer = p.sibling(), p.across_y(), p.across_h()
    rows, width = x_ref.shape[1], x_ref.shape[2]
    heads = 4
    wide = heads * HD
    ff = FA.shape[3]
    part_rows = WO.shape[2]
    block = WD.shape[2]

    first = Part(0, 1, W=WQ, V=WO, S=SQ, G=GQ, R=GO, Y=YQ, YR=YO, ZS=ZSQ, ZSR=ZSO, ZR=ZRQ, ZRR=ZRO,
                 TS=TSQ, TR=TRQ, O=OQ, OR=OO)
    second = Part(1, 2, W=WU, V=WD, S=SU, G=GU, R=GD, Y=YU, YR=YD, ZS=ZSU, ZSR=ZSD, ZR=ZRU, ZRR=ZRD,
                  TS=TSU, TR=TRU, O=OU, OR=OD)

    loads = [
        pltpu.make_async_copy(wq_in.at[:, pl.ds(width * i, width)], UF.at[pl.ds(576 + 64 * i, 64)], ls.at[i])
        for i in range(3)
    ]
    loads.append(pltpu.make_async_copy(wo_in, UF.at[pl.ds(0, 64)], ls.at[3]))
    loads += [
        pltpu.make_async_copy(wu_in.at[:, pl.ds(width * i, width)], UF.at[pl.ds(320 + 64 * i, 64)], ls.at[4 + i])
        for i in range(4)
    ]
    loads.append(pltpu.make_async_copy(wd_in, UF.at[pl.ds(64, 256)], ls.at[8]))
    for cp in loads:
        cp.start()

    bell = pltpu.get_barrier_semaphore()
    everyone = (sib, p.team(1)[0], p.team(2)[0], p.team(3)[0], ypeer, hpeer)
    for peer in everyone:
        pl.semaphore_signal(bell, inc=1, device_id=peer, device_id_type=MESH)

    for cp in loads[:4]:
        cp.wait()
    for i in range(3):
        for hh in range(2):
            for zz in range(2):
                base = (2 * zz + 4 * hh) * 128
                even = UF[576 + 64 * i : 640 + 64 * i, base : base + 128].astype(BF)
                odd = UF[576 + 64 * i : 640 + 64 * i, base + 128 : base + 256].astype(BF)
                at = (2 * i + hh) * 128
                SQ[2 * zz, :, at : at + 128] = jnp.concatenate([even[:, :HD], odd[:, :HD]], axis=1)
                SQ[2 * zz + 1, :, at : at + 128] = jnp.concatenate([even[:, HD:], odd[:, HD:]], axis=1)
    WQ[s, h, z, y, x] = SQ[t]
    q = 2 * h + y
    WO[s, q] = UF[0:64, :].astype(BF)
    pl.semaphore_wait(bell, len(everyone))

    def w_team(part, k):
        device, slot = p.team(k)
        return remote(
            part.S.at[slot], part.W.at[s, h, z, y, x], ss_a.at[part.index, k], rs_a.at[part.index, k], device
        )

    def w_view(part, c, hh, yy):
        if c < 2:
            return part.W.at[s, hh, c, yy]
        return part.V.at[s, 2 * hh + yy, part.strip(c, part.V.shape[2])]

    def w_y(part, c, n):
        view = w_view(part, c, h + n * (1 - 2 * h), y)
        return remote(view, view, ss_wy.at[part.index, n, c], rs_wy.at[part.index, n, c], ypeer)

    def w_h(part, c):
        view = w_view(part, c, h, y)
        return remote(view, view, ss_wh.at[part.index, c], rs_wh.at[part.index, c], hpeer)

    def w_s(part, c, hh, yy):
        view = w_view(part, c, hh, yy)
        n = 2 * hh + yy
        return remote(view, view, ss_ws.at[part.index, n, c], rs_ws.at[part.index, n, c], sib)

    def w_spread(part):
        for k in (1, 2, 3):
            w_team(part, k).wait_recv()
        for c in range(part.chunks):
            w_h(part, c).start()
            w_y(part, c, 0).start()
            w_s(part, c, h, y).start()

    def w_pass(part, c):
        w_h(part, c).wait_recv()
        w_y(part, c, 1).start()
        w_s(part, c, 1 - h, y).start()

    def w_last(part):
        for c in range(part.chunks):
            w_y(part, c, 0).wait_recv()
            w_s(part, c, h, 1 - y).start()
        for c in range(part.chunks):
            w_y(part, c, 1).wait_recv()
            w_s(part, c, 1 - h, 1 - y).start()

    def w_other(part):
        for c in range(part.chunks):
            for n in range(4):
                w_s(part, c, n // 2, n % 2).wait_recv()

    for k in (1, 2, 3):
        w_team(first, k).start()
    for cp in loads[4:]:
        cp.wait()
    for hh in range(2):
        for zz in range(2):
            for yy in range(2):
                for xx in range(2):
                    at = (2 * hh + yy) * block
                    low = 320 + 64 * (zz + 2 * hh)
                    col = (xx + 2 * yy) * block
                    SU[xx + 2 * zz, :, at : at + block] = UF[low : low + 64, col : col + block].astype(BF)
    WU[s, h, z, y, x] = SU[t]
    WD[s, q] = UF[64 : 64 + block, :].astype(BF)
    for k in (1, 2, 3):
        w_team(second, k).start()

    @pl.when(s == 0)
    def _():
        w_spread(first)

    lane = lanes_of((1, 128))
    zero = jnp.zeros((1, 128), F32)
    pair = [jnp.concatenate([v[...], v[...]], axis=1) for v in (v0_ref, v1_ref, v2_ref, v3_ref, v4_ref, v5_ref)]
    lines = [jnp.where(lane // HD == x, v, zero) for v in pair]
    for xx in range(2):
        for i in range(2):
            lines.append(jnp.where(x == xx, bu_ref[:, 128 * i : 128 * i + 128], zero))
    table = jnp.concatenate([rt_ref[...], jnp.zeros((1, 96), F32)], axis=1)
    counts = jnp.where(lane == 0, il_ref[0:1, :].astype(F32), jnp.where(lane == 1, il_ref[1:2, :].astype(F32), zero))
    for piece in (table, counts):
        for xx in range(2):
            lines.append(jnp.where(x == xx, piece, zero))
    for i in range(2):
        lines.append(zero)
    for i in range(16):
        SPX[0, i : i + 1, :] = lines[i].astype(BF).astype(F32)

    def swap(n, src, dst, device):
        cp = remote(src, dst, ss_p.at[n], rs_p.at[n], device)
        cp.start()
        cp.wait()

    swap(0, SPX.at[0], SPX.at[1], p.team(1)[0])
    SPT[h, z, y, s] = SPX[0] + SPX[1]
    for n, (view, device) in enumerate(
        (
            (SPT.at[h, z, y, s], sib),
            (SPT.at[h, z, y], ypeer),
            (SPT.at[h, z], p.team(2)[0]),
            (SPT.at[h], hpeer),
        )
    ):
        swap(n + 1, view, view, device)

    for hh in range(2):
        for zz in range(2):
            for yy in range(2):
                at = (yy + 2 * zz + 4 * hh) * 128
                for i in range(2):
                    VEC[i, 0:6, at : at + 128] = SPT[hh, zz, yy, i, 0:6, :]
    for i in range(2):
        for hh in range(2):
            for yy in range(2):
                tile = SPT[hh, z, yy, i]
                for r in range(2):
                    at = (2 * hh + yy) * block + 128 * r
                    VEC[i, 6:7, at : at + 128] = jnp.where(x == 0, tile[6 + r : 7 + r], tile[8 + r : 9 + r])
    for zz in range(2):
        tile = SPT[h, zz, y, 0]
        for xx in range(2):
            count = jnp.sum(jnp.where(lane == s, tile[12 + xx : 13 + xx], 0.0), axis=1, keepdims=True)
            LEN[xx + 2 * zz] = jnp.broadcast_to(count, (8, 128))

    mark = jnp.concatenate([rb_ref[...], jnp.full((1, 128 - rows), 2 * NB, jnp.int32)], axis=1).astype(BF)
    mark = jnp.broadcast_to(mark, (8, 128))
    flip = ((lanes_of((128, 128), 0) + lanes_of((128, 128))) % 128 == 0).astype(F32).astype(BF)
    mark = dot(mark, flip)[0:1]
    onehot = (lanes_of((NB, 128), 0).astype(F32) == mark).astype(F32)
    for i in range(2):
        lines = []
        for hh in range(2):
            for zz in range(2):
                for yy in range(2):
                    tile = SPT[hh, zz, yy, i]
                    for xx in range(2):
                        for b in range(2):
                            lines.append(tile[10 + xx : 11 + xx, 16 * b : 16 * b + 16])
        by_bucket = jnp.concatenate([jnp.concatenate(lines, axis=0), jnp.zeros((NB, 112), F32)], axis=1)
        PD[...] = dot_tn(by_bucket.astype(BF), onehot.astype(BF))
        stack = []
        for hh in range(2):
            for yy in range(2):
                line = PD[pl.ds(x + 2 * yy + 4 * z + 8 * hh, 1), :]
                stack.append(jnp.broadcast_to(line, (rows, 128)))
        grid = skew(jnp.concatenate(stack, axis=0), rows, 1)[:, :rows]
        causal = lanes_of(grid.shape) <= lanes_of(grid.shape, 0) % rows
        BIAS[i] = jnp.where(causal, grid, -1000000000.0)

    def gather_copy(ref, c, k):
        return remote(ref.at[t], ref.at[t], ss_g.at[c, k], rs_g.at[c, k], p.team(k)[0])

    def gather_start(ref, c):
        gather_copy(ref, c, 1).start()
        gather_copy(ref, c, 2).start()

    def gather_take(ref, c, k):
        device, slot = p.team(k)
        remote(ref.at[slot], ref.at[slot], ss_g.at[c, k], rs_g.at[c, k], device).wait_recv()

    def reduce_copy(c, k):
        return remote(SB.at[k], RB.at[k], ss_r.at[c, k], rs_r.at[c, k], p.team(k)[0])

    def reduce_put(c, k, value):
        @pl.when(k == 0)
        def _():
            OWN[...] = value

        @pl.when(k > 0)
        def _():
            SB[k] = value.astype(BF)
            reduce_copy(c, k).start()

    def reduce_end(c):
        total = OWN[...]
        for k in (1, 2, 3):
            reduce_copy(c, k).wait()
            total = total + RB[k].astype(F32)
        return total

    def each_item(ref, c, body, aside):
        def step(k, carry):
            @pl.when(k > 0)
            def _():
                gather_take(ref, c, k)

            body(k, p.team(k)[1])

            @pl.when(k == 0)
            def _():
                gather_copy(ref, c, 3).start()

            aside(k)
            return carry

        lax.fori_loop(0, 4, step, 0)
        for k in (1, 2, 3):
            gather_copy(ref, c, k).wait_send()

    def at_step(k, here, n, what):
        @pl.when(jnp.logical_and(here, k == n))
        def _():
            what()

    pairs = ((A, XA), (MIX, XM), (C, XC), (FA, XF), (DZ, XDZ), (DAT, XDAT), (DU, XDU), (DQ, XDQ))

    def share_copy(i, layer):
        return remote(pairs[i][0].at[layer], pairs[i][1], ss_x.at[i], rs_x.at[i], sib)

    def share(layer, which):
        @pl.when(s != layer)
        def _():
            for i in which:
                share_copy(i, layer).start()

    def row(layer, index):
        return VEC[layer, index : index + 1, :]

    def w_qkv(layer):
        return WQ[layer].reshape(width, 3 * wide)

    def w_up(layer):
        return WU[layer].reshape(width, ff)

    def w_out(layer):
        return WO[layer].reshape(wide, width)

    def w_down(layer):
        return WD[layer].reshape(ff, width)

    def u_rows(layer, i):
        return pl.ds(pl.multiple_of((layer * 4 + i) * rows, 8), rows)

    position = lanes_of((rows, 1), 0).astype(F32)
    valid = (position < LEN[t][0:1, 0:1]).astype(F32)

    def g_own(part, c, hh, yy):
        if c < 2:
            return part.G.at[hh, c, yy]
        return part.R.at[2 * hh + yy, part.strip(c, part.R.shape[1])]

    def g_land(part, c, n):
        if c < 2:
            return part.Y.at[n, c]
        return part.YR.at[n, part.strip(c, part.R.shape[1])]

    def g_half(n):
        return (1 - h) + n * (2 * h - 1)

    def g_y(part, c, n):
        return remote(
            g_own(part, c, g_half(n), 1 - y), g_land(part, c, n),
            ss_gy.at[part.index, n, c], rs_gy.at[part.index, n, c], ypeer,
        )

    def g_z(part, c, out):
        if c < 2:
            return (part.ZS if out else part.ZR).at[c]
        return (part.ZSR if out else part.ZRR).at[part.strip(c, part.R.shape[1])]

    def g_h(part, c):
        return remote(
            g_z(part, c, True), g_z(part, c, False), ss_gh.at[part.index, c], rs_gh.at[part.index, c], hpeer
        )

    def g_t(part, k):
        return remote(
            part.TS.at[k], part.TR.at[k], ss_gt.at[part.index, k], rs_gt.at[part.index, k], p.team(k)[0]
        )

    def flat(ref, span):
        value = ref[:, :, span]
        return value.reshape(value.shape[0] * value.shape[1], value.shape[2])

    def product(left, right, span):
        every = pl.ds(0, right[0].shape[2])
        return dot_tn(flat(left[0], span), flat(right[0], every)) + dot_tn(
            flat(left[1], span), flat(right[1], every)
        )

    def g_make(part):
        if part is first:
            need = (0, 1, 5, 7)
            big_l, big_r = (A.at[s], XA), (DQ.at[s], XDQ)
            small_l, small_r = (MIX.at[s], XM), (DAT.at[s], XDAT)
            small_span = HD
        else:
            need = (2, 3, 4, 6)
            big_l, big_r = (C.at[s], XC), (DU.at[s], XDU)
            small_l, small_r = (FA.at[s], XF), (DZ.at[s], XDZ)
            small_span = block
        for i in need:
            share_copy(i, s).wait_recv()
        if part is first:
            value = product(small_l, small_r, pl.ds(0, wide)).astype(BF)
            for i in range(4):
                part.R[i] = value[i * small_span : (i + 1) * small_span]

        def tile(n, carry):
            hh = g_half(n)
            for zz in range(2):
                span = pl.ds(pl.multiple_of((2 * hh + zz) * 256, 256), 256)
                value = product(big_l, big_r, span).astype(BF)
                part.G[hh, zz] = value.reshape(2, 2, part_rows, value.shape[1])
                g_y(part, zz, n).start()
            if part is second:
                for yy in (1 - y, y):
                    span = pl.ds(pl.multiple_of((2 * hh + yy) * 256, 256), 256)
                    part.R[2 * hh + yy] = product(small_l, small_r, span).astype(BF)
                    if yy is not y:
                        for c in range(2, part.chunks):
                            g_y(part, c, n).start()
            else:
                g_y(part, 2, n).start()
            return carry

        lax.fori_loop(0, 2, tile, 0)

    def g_fold(part, c):
        g_y(part, c, 0).wait_recv()
        g_z(part, c, True)[...] = (
            g_own(part, c, 1 - h, y)[...].astype(F32) + g_land(part, c, 0)[...].astype(F32)
        ).astype(BF)
        g_h(part, c).start()

    def g_total(part):
        for c in range(part.chunks):
            g_y(part, c, 1).wait_recv()
            g_h(part, c).wait_recv()

        def total(xx, zz):
            return (
                part.G[h, zz, y, xx].astype(F32) + part.Y[1, zz, xx].astype(F32) + part.ZR[zz, xx].astype(F32)
            )

        for k in (1, 2, 3):
            part.TS[k] = total(*p.mate(k)).astype(BF)
            g_t(part, k).start()
        part.O[t] = total(x, z)
        part.OR[...] = part.R[q].astype(F32) + part.YR[1].astype(F32) + part.ZRR[...].astype(F32)

    def g_end(part):
        for k in (1, 2, 3):
            g_t(part, k).wait_recv()
            part.O[p.team(k)[1]] = part.TR[k].astype(F32)

    XIN[0] = x_ref[s]
    DY[2] = og_ref[s]

    @pl.when(s == 0)
    def _():
        for c in range(first.chunks):
            w_pass(first, c)
        w_spread(second)

    def forward(layer, carry):
        mine = s == layer
        coming = jnp.logical_and(s == 1, layer == 0)
        xin = XIN[layer].astype(F32)
        normed, _ = rows_norm(xin)
        A[layer, t] = (normed * row(layer, 0) + row(layer, 1)).astype(BF)
        c = 2 * layer
        gather_start(A.at[layer], c)

        @pl.when(mine)
        def _():
            w_last(first)

        @pl.when(s != layer)
        def _():
            w_other(first)

        def attend(k, i):
            qkv = dot(A[layer, i], w_qkv(layer)).astype(BF)
            QKV[layer, i] = qkv
            stack = split_heads(qkv[:, :wide], heads, HD)
            scores = dot_nt(stack, qkv[:, wide : 2 * wide]) * (HD ** (-0.5)) + BIAS[layer]
            column = lanes_of(scores.shape).astype(F32)
            scores = jnp.where(column < LEN[i][0:1, 0:1], scores, -1000000000.0)
            raised = jnp.exp(scores - jnp.max(scores, axis=-1, keepdims=True))
            probs = raised / jnp.sum(raised, axis=-1, keepdims=True)
            PR[layer, i] = probs
            mixed = join_heads(dot(probs.astype(BF), qkv[:, 2 * wide :]), heads, HD).astype(BF)
            MIX[layer, i] = mixed
            reduce_put(c, k, dot(mixed, w_out(layer)))

        def pass_on(k):
            for n in range(3):
                at_step(k, mine, n + 1, lambda n=n: w_pass(second, n))

        each_item(A.at[layer], c, attend, pass_on)
        share(layer, (0, 1))
        hmid = xin + reduce_end(c) + row(layer, 4)
        HM[layer] = hmid
        normed, _ = rows_norm(hmid)
        C[layer, t] = (normed * row(layer, 2) + row(layer, 3)).astype(BF)
        gather_start(C.at[layer], c + 1)

        @pl.when(mine)
        def _():
            w_pass(second, 3)
            w_last(second)

        @pl.when(s != layer)
        def _():
            w_other(second)

        def feed(k, i):
            u = dot(C[layer, i], w_up(layer)) + row(layer, 6)
            UF[u_rows(layer, i), :] = u
            f = (0.5 * u * (1.0 + jnp.tanh(GELU_K * (u + 0.044715 * (u * u * u))))).astype(BF)
            FA[layer, i] = f
            reduce_put(c + 1, k, dot(f, w_down(layer)))

        def prepare(k):
            at_step(k, coming, 0, lambda: w_spread(first))
            for n in range(3):
                at_step(k, coming, n + 1, lambda n=n: w_pass(first, n))
            at_step(k, coming, 3, lambda: w_spread(second))

        each_item(C.at[layer], c + 1, feed, prepare)
        share(layer, (2, 3))
        out = (valid * (HM[layer] + reduce_end(c + 1) + row(layer, 5))).astype(BF)
        XIN[layer + 1] = out
        return carry

    lax.fori_loop(0, 2, forward, 0)
    for layer in (0, 1):

        @pl.when(s == layer)
        def _(layer=layer):
            lo[s] = XIN[layer + 1]

        @pl.when(s != layer)
        def _(layer=layer):
            remote(XIN.at[layer + 1], lo.at[s], ss_o.at[0], rs_o.at[0], sib).start()

    DS[...] = jnp.zeros_like(DS)
    SBU[...] = jnp.zeros_like(SBU)
    SGV[...] = jnp.zeros_like(SGV)

    def backward(back, carry):
        layer = 1 - back
        mine = s == layer
        done = jnp.logical_and(s == 1, layer == 0)
        c = 4 + 2 * back
        dyv = valid * DY[layer + 1].astype(F32)
        DZ[layer, t] = dyv.astype(BF)
        gather_start(DZ.at[layer], c)
        SGV[layer, 5:6, :] = column_sum(dyv)

        @pl.when(done)
        def _():
            g_make(first)

        def feed(k, i):
            u = UF[u_rows(layer, i), :]
            square = u * u
            th = jnp.tanh(GELU_K * (u + 0.044715 * (square * u)))
            slope = 0.5 * (1.0 + th) + (0.5 * GELU_K) * u * (1.0 - th * th) * (1.0 + 0.134145 * square)
            du = (dot_nt(DZ[layer, i], w_down(layer)) * slope).astype(BF)
            DU[layer, i] = du
            SBU[layer] += column_sum(du.astype(F32))
            reduce_put(c, k, dot_nt(du, w_up(layer)))

        def fold_first(k):
            for n in range(3):
                at_step(k, done, n + 1, lambda n=n: g_fold(first, n))

        each_item(DZ.at[layer], c, feed, fold_first)
        share(layer, (4, 6))

        @pl.when(done)
        def _():
            g_total(second)

        dc = reduce_end(c)
        normed, scale = rows_norm(HM[layer])
        SGV[layer, 2:3, :] = column_sum(dc * normed)
        SGV[layer, 3:4, :] = column_sum(dc)
        dh = valid * DY[layer + 1].astype(F32) + norm_back(dc, normed, scale, row(layer, 2))
        DH[...] = dh
        dattn = dh.astype(BF)
        DAT[layer, t] = dattn
        gather_start(DAT.at[layer], c + 1)
        SGV[layer, 4:5, :] = column_sum(dattn.astype(F32))

        @pl.when(mine)
        def _():
            g_make(second)

        def attend(k, i):
            dmixed = dot_nt(DAT[layer, i], w_out(layer)).astype(BF)
            qkv = QKV[layer, i]
            probs = PR[layer, i]
            stack = split_heads(dmixed, heads, HD)
            dprobs = dot_nt(stack, qkv[:, 2 * wide :])
            dscores = (probs * (dprobs - jnp.sum(probs * dprobs, axis=-1, keepdims=True))).astype(BF)
            DS[layer] += dscores.astype(F32)
            dq = join_heads(dot(dscores, qkv[:, wide : 2 * wide]), heads, HD) * (HD ** (-0.5))
            dk = dot_tn(dscores, split_heads(qkv[:, :wide], heads, HD)) * (HD ** (-0.5))
            dv = dot_tn(probs.astype(BF), stack)
            DQ[layer, i, :, :wide] = dq.astype(BF)
            DQ[layer, i, :, wide : 2 * wide] = dk.astype(BF)
            DQ[layer, i, :, 2 * wide :] = dv.astype(BF)
            reduce_put(c + 1, k, dot_nt(DQ[layer, i], w_qkv(layer)))

        def fold_second(k):
            for n in range(4):
                at_step(k, mine, n, lambda n=n: g_fold(second, n))

        each_item(DAT.at[layer], c + 1, attend, fold_second)
        share(layer, (5, 7))
        da = reduce_end(c + 1)
        normed, scale = rows_norm(XIN[layer].astype(F32))
        SGV[layer, 0:1, :] = column_sum(da * normed)
        SGV[layer, 1:2, :] = column_sum(da)
        dx = DH[...] + norm_back(da, normed, scale, row(layer, 0))
        low = dx.astype(BF)
        DY[layer] = low
        result = jnp.where(layer == 1, low.astype(F32), dx)

        @pl.when(mine)
        def _():
            ig[s] = result

        @pl.when(s != layer)
        def _():
            OWN[...] = result
            cp = remote(OWN, ig.at[s], ss_o.at[1], rs_o.at[1], sib)
            cp.start()
            cp.wait_send()

        return carry

    lax.fori_loop(0, 2, backward, 0)

    @pl.when(s == 0)
    def _():
        g_make(first)

    spread = []
    for i in range(2):
        turned = skew(jnp.concatenate([DS[i], jnp.zeros((heads * rows, 128 - rows), F32)], axis=1), rows, -1)
        table = jnp.zeros((128, 128), F32)
        for hh in range(2):
            for yy in range(2):
                n = 2 * hh + yy
                line = column_sum(turned[n * rows : (n + 1) * rows])
                head = x + 2 * yy + 4 * z + 8 * hh
                table = jnp.where(lanes_of((128, 128), 0) == head, line, table)
        spread.append(
            lax.dot_general(
                onehot, table, (((1,), (1,)), ((), ())), precision=highest, preferred_element_type=F32
            )
        )
    for hh in range(2):
        for zz in range(2):
            for yy in range(2):
                j = yy + 2 * zz + 4 * hh
                for i in range(2):
                    MT[hh, zz, yy, i, 0:6, :] = SGV[i, 0:6, 128 * j : 128 * j + 128]
                    for xx in range(2):
                        for r in range(2):
                            at = (2 * hh + yy) * block + 128 * r
                            n = 6 + 2 * xx + r
                            MT[hh, zz, yy, i, n : n + 1, :] = jnp.where(
                                jnp.logical_and(z == zz, x == xx), SBU[i, :, at : at + 128], zero
                            )
                    MT[hh, zz, yy, i, 10:12, :] = jnp.zeros((2, 128), F32)
                    MT[hh, zz, yy, i, 12:16, :] = spread[i][4 * j : 4 * j + 4]

    def merge(n, send, keep, land, device):
        cp = remote(send, land, ss_m.at[n], rs_m.at[n], device)
        cp.start()
        cp.wait()
        keep[...] += land[...]

    @pl.when(s == 0)
    def _():
        for c in range(first.chunks):
            g_fold(first, c)

    merge(0, MT.at[1 - h], MT.at[h], MR.at[0], hpeer)
    merge(1, MT.at[h, 1 - z], MT.at[h, z], MR.at[1, 0], p.team(2)[0])
    merge(2, MT.at[h, z, 1 - y], MT.at[h, z, y], MR.at[1, 1, 0], ypeer)
    merge(3, MT.at[h, z, y, 1 - s], MT.at[h, z, y, s], MR.at[1, 1, 1, 0], sib)
    last = remote(MT.at[h, z, y, s], MR.at[1, 1, 1, 1], ss_m.at[4], rs_m.at[4], p.team(1)[0])
    last.start()
    last.wait()
    OT[...] = MT[h, z, y, s] + MR[1, 1, 1, 1]

    @pl.when(s == 0)
    def _():
        g_total(second)

    g_total(first)
    g_end(second)
    g_end(first)

    for part in (first, second):
        for k in (1, 2, 3):
            w_team(part, k).wait_send()
            g_t(part, k).wait_send()
        for c in range(part.chunks):
            w_h(part, c).wait_send()
            g_h(part, c).wait_send()
            for n in range(2):
                w_y(part, c, n).wait_send()
                g_y(part, c, n).wait_send()
            for n in range(4):
                w_s(part, c, n // 2, n % 2).wait_send()
    for i in range(8):
        share_copy(i, 1 - s).wait_send()
    remote(XIN.at[1], lo.at[1 - s], ss_o.at[0], rs_o.at[0], sib).wait()
    remote(OWN, ig.at[1 - s], ss_o.at[1], rs_o.at[1], sib).wait_recv()


def finish_kernel(lo_in, ig_in, OQ, OO, OU, OD, OT, half, lo, ig, oq, oo, ou, od, a0, a1, a2, a3, a4, bu, a5, tab):
    lo[...] = lo_in[...]
    ig[...] = ig_in[...]
    oo[...] = OO[...]
    od[...] = OD[...]
    block = OD.shape[0]
    for hh in range(2):
        for zz in range(2):
            for yy in range(2):
                n = 2 * hh + yy
                d = 2 * yy + 4 * zz + 8 * hh
                for i in range(3):
                    at = i * 4 * HD + n * HD
                    to = i * 16 * HD + d * HD
                    oq[:, to : to + 2 * HD] = jnp.concatenate(
                        [OQ[2 * zz, :, at : at + HD], OQ[2 * zz + 1, :, at : at + HD]], axis=1
                    )
                for xx in range(2):
                    ou[:, (d + xx) * block : (d + xx + 1) * block] = OU[xx + 2 * zz, :, n * block : (n + 1) * block]
    x = half[0]
    for i, ref in enumerate((a0, a1, a2, a3, a4, a5)):
        ref[...] = jnp.where(x == 0, OT[i : i + 1, :HD], OT[i : i + 1, HD:])
    for r in range(2):
        bu[:, 128 * r : 128 * r + 128] = jnp.where(x == 0, OT[6 + r : 7 + r, :], OT[8 + r : 9 + r, :])
    for b in range(2):
        tab[:, 16 * b : 16 * b + 16] = jnp.where(x == 0, OT[12 + b : 13 + b, :16], OT[14 + b : 15 + b, :16])


def vm(n=1):
    return [pl.BlockSpec(memory_space=pltpu.VMEM)] * n


def hb(n=1):
    return [pl.BlockSpec(memory_space=pltpu.HBM)] * n


def sems(*shape):
    return pltpu.SemaphoreType.DMA(shape)


def shape_of(dims, kind):
    return jax.ShapeDtypeStruct(dims, kind)


def team_local(
    audio_in, out_grad, item_len, rel_bucket, w_qkv, w_out, w_up, w_down,
    ln1_gain, ln1_bias, ln2_gain, ln2_bias, b_out, b_up, b_down, rel_table,
):
    rows, width = audio_in.shape[2], audio_in.shape[3]
    part = w_qkv.shape[1]
    hidden = w_up.shape[2]
    block = hidden // 16
    wide, ff = width // 4, hidden // 4
    low = lambda *dims: pltpu.VMEM(dims, BF)
    full = lambda *dims: pltpu.VMEM(dims, F32)

    lo, ig, OQ, OO, OU, OD, OT = pl.pallas_call(
        step_kernel,
        out_shape=(
            shape_of((2, rows, width), BF),
            shape_of((2, rows, width), F32),
            shape_of((4, part, 3 * wide), F32),
            shape_of((part, width), F32),
            shape_of((4, part, ff), F32),
            shape_of((block, width), F32),
            shape_of((16, 128), F32),
        ),
        in_specs=vm(4) + hb(4) + vm(8),
        out_specs=tuple(vm(7)),
        scratch_shapes=[
            low(4, part, 3 * wide), low(4, part, ff),
            low(2, 2, 2, 2, 2, part, 3 * wide), low(2, 4, part, width),
            low(2, 2, 2, 2, 2, part, ff), low(2, 4, block, width),
            low(3, rows, width), low(3, rows, width),
            low(2, 4, rows, width), low(2, 4, rows, width), low(2, 4, rows, ff), low(2, 4, rows, wide),
            low(2, 4, rows, 3 * wide), full(2, 4, 4 * rows, rows), full(8 * rows, ff), full(2, rows, width),
            low(2, 4, rows, width), low(2, 4, rows, width), low(2, 4, rows, ff), low(2, 4, rows, 3 * wide),
            low(4, rows, width), low(4, rows, width), low(4, rows, ff), low(4, rows, wide),
            low(4, rows, width), low(4, rows, width), low(4, rows, ff), low(4, rows, 3 * wide),
            low(4, rows, width), low(4, rows, width), full(rows, width), full(rows, width),
            low(2, 2, 2, 2, part, 3 * wide), low(4, part, width), low(2, 2, 2, 2, part, ff), low(4, block, width),
            low(2, 2, 2, part, 3 * wide), low(2, part, width), low(2, 2, 2, part, ff), low(2, block, width),
            low(2, 2, part, 3 * wide), low(part, width), low(2, 2, part, ff), low(block, width),
            low(2, 2, part, 3 * wide), low(part, width), low(2, 2, part, ff), low(block, width),
            low(4, part, 3 * wide), low(4, part, 3 * wide), low(4, part, ff), low(4, part, ff),
            full(2, 2, 2, 2, 16, 128), full(2, 16, 128), full(2, 8, width), full(4, 8, 128),
            full(2, 4 * rows, rows), full(128, 128), full(2, 8, width), full(2, 1, ff), full(2, 4 * rows, rows),
            full(2, 2, 2, 2, 16, 128), full(2, 2, 2, 2, 16, 128),
            sems(9), sems(2, 4), sems(2, 4), sems(2, 2, 4), sems(2, 2, 4), sems(2, 4), sems(2, 4),
            sems(2, 4, 4), sems(2, 4, 4), sems(5), sems(5),
            sems(8, 4), sems(8, 4), sems(8, 4), sems(8, 4), sems(8), sems(8), sems(2), sems(2),
            sems(2, 2, 4), sems(2, 2, 4), sems(2, 4), sems(2, 4), sems(2, 4), sems(2, 4), sems(5), sems(5),
        ],
        compiler_params=pltpu.CompilerParams(
            collective_id=0, has_side_effects=True, vmem_limit_bytes=63 << 20
        ),
        name="two_layers",
    )(
        audio_in.reshape(2, rows, width), out_grad.reshape(2, rows, width), item_len, rel_bucket[None],
        w_qkv[0], w_out[0], w_up[0], w_down[0],
        ln1_gain, ln1_bias, ln2_gain, ln2_bias, b_out, b_down, b_up, rel_table,
    )

    half = (lax.axis_index("dp") % 2).reshape(1)
    lo, ig, oq, oo, ou, od, a0, a1, a2, a3, a4, bu, a5, tab = pl.pallas_call(
        finish_kernel,
        out_shape=(
            shape_of((2, rows, width), BF),
            shape_of((2, rows, width), F32),
            shape_of((part, 3 * width), F32),
            shape_of((part, width), F32),
            shape_of((part, hidden), F32),
            shape_of((block, width), F32),
        )
        + (shape_of((1, part), F32),) * 5
        + (shape_of((1, block), F32), shape_of((1, part), F32), shape_of((1, 32), F32)),
        in_specs=vm(7) + [pl.BlockSpec(memory_space=pltpu.SMEM)],
        out_specs=tuple(vm(14)),
        compiler_params=pltpu.CompilerParams(vmem_limit_bytes=32 << 20),
        name="finish",
    )(lo, ig, OQ, OO, OU, OD, OT, half)
    return (
        lo[None, :, None], ig[None, :, None], oq[None], oo[None], ou[None], od[None],
        a0, a1, a2, a3, a4, bu, a5, tab,
    )


def solution(mesh):
    fits = mesh.shape["dp"] == 16 and mesh.shape["section"] == 2
    return jax.shard_map(
        team_local if fits else local,
        mesh=mesh,
        in_specs=(
            P(None, "dp", None, None),
            P(None, "dp", None, None),
            P(None, "dp"),
            P(),
            P("section", "dp", None),
            P("section", "dp", None),
            P("section", "dp", None),
            P("section", "dp", None),
            P("section", "dp"),
            P("section", "dp"),
            P("section", "dp"),
            P("section", "dp"),
            P("section", "dp"),
            P("section", "dp"),
            P("section", "dp"),
            P("section", "dp"),
        ),
        out_specs=(
            P("section", None, "dp", None, None),
            P("section", None, "dp", None, None),
            P("section", "dp", None),
            P("section", "dp", None),
            P("section", "dp", None),
            P("section", "dp", None),
            P("section", "dp"),
            P("section", "dp"),
            P("section", "dp"),
            P("section", "dp"),
            P("section", "dp"),
            P("section", "dp"),
            P("section", "dp"),
            P("section", "dp"),
        ),
        check_vma=False,
    )
```

```python
import jax
import jax.numpy as jnp
from jax import lax
from jax.experimental import pallas as pl
from jax.experimental.pallas import tpu as pltpu
from jax.sharding import PartitionSpec as P

H = 16
NB = 32


epsilon = 1e-05
highest = lax.Precision.HIGHEST


def passed_along(block, axis, distance):
    devices = range(lax.axis_size(axis))
    route = [(i - distance, i) for i in devices if i - distance in devices]
    return lax.ppermute(block, axis, route)


def norm_rows(values):
    centre = values - jnp.mean(values, axis=-1, keepdims=True)
    return centre * lax.rsqrt(jnp.mean(centre * centre, axis=-1, keepdims=True) + epsilon)


def norm_affine(values, gain, shift):
    return norm_rows(values) * gain + shift


def contract_rows(left, right):
    return lax.dot_general(
        left, right, (((0,), (0,)), ((), ())), preferred_element_type=jnp.float32
    )


def contract_cols(left, right):
    return lax.dot_general(
        left, right, (((1,), (1,)), ((), ())), preferred_element_type=jnp.float32
    )


def toeplitz_rows(values):
    heads, length = values.shape
    reverse = jnp.flip(values, axis=1)
    padded = jnp.concatenate([reverse, jnp.zeros_like(reverse)], axis=1)
    tiled = jnp.tile(padded, (1, length))[:, : length * (2 * length - 1)]
    return tiled.reshape(heads, length, 2 * length - 1)[:, :, length - 1 :]


def diagonal_sums(grid):
    heads, length, _ = grid.shape
    widened = jnp.concatenate([jnp.zeros((heads, length, length - 1), grid.dtype), grid], axis=2)
    flat = widened.reshape(heads, length * (2 * length - 1))
    flat = jnp.concatenate([flat, jnp.zeros((heads, length), grid.dtype)], axis=1)
    folded = jnp.sum(flat.reshape(heads, length, 2 * length), axis=1)
    return jnp.flip(folded[:, :length], axis=1)


def bucket_table(buckets):
    return (buckets[None, :] == jnp.arange(NB, dtype=jnp.int32)[:, None]).astype(jnp.float32)


def make_bias(table_flat, onehot):
    table = table_flat.astype(jnp.float32).reshape(NB, H)
    per_distance = jnp.dot(table.T, onehot, precision=highest)
    return toeplitz_rows(per_distance)


def weight_terms(factors):
    normed, d_qkv, mixed, d_attn, second, d_hidden, activated, d_branch = factors
    return (
        contract_rows(normed, d_qkv),
        contract_rows(mixed, d_attn),
        contract_rows(second, d_hidden),
        contract_rows(activated, d_branch),
    )


def forward_item(inputs, length, bias, weights):
    (
        w_qkv,
        w_out,
        w_up,
        w_down,
        gain_one,
        shift_one,
        gain_two,
        shift_two,
        bias_out,
        bias_up,
        bias_down,
    ) = weights
    rows, width = inputs.shape
    heads = bias.shape[0]
    head_dim = width // heads
    scale = head_dim ** (-0.5)
    position = jnp.arange(rows)
    visible = (position[None, :] <= position[:, None])[None] & (position[None, None, :] < length)
    valid = (position < length).astype(jnp.float32)[:, None]
    normed = norm_affine(
        inputs, gain_one.astype(jnp.float32), shift_one.astype(jnp.float32)
    ).astype(jnp.bfloat16)
    qkv = jnp.dot(normed, w_qkv, preferred_element_type=jnp.float32).astype(jnp.bfloat16)
    query = qkv[:, :width].reshape(rows, heads, head_dim)
    keys = qkv[:, width : 2 * width].reshape(rows, heads, head_dim)
    values = qkv[:, 2 * width :].reshape(rows, heads, head_dim)
    scores = (
        jnp.einsum("ihd,jhd->hij", query, keys, preferred_element_type=jnp.float32) * scale + bias
    )
    scores = jnp.where(visible, scores, -1000000000.0)
    raised = jnp.exp(scores - jnp.max(scores, axis=-1, keepdims=True))
    probs = raised / jnp.sum(raised, axis=-1, keepdims=True)
    probs_low = probs.astype(jnp.bfloat16)
    mixed = (
        jnp.einsum("hij,jhd->ihd", probs_low, values, preferred_element_type=jnp.float32)
        .reshape(rows, width)
        .astype(jnp.bfloat16)
    )
    middle = (
        inputs
        + jnp.dot(mixed, w_out, preferred_element_type=jnp.float32)
        + bias_out.astype(jnp.float32)
    )
    second = norm_affine(
        middle, gain_two.astype(jnp.float32), shift_two.astype(jnp.float32)
    ).astype(jnp.bfloat16)
    hidden = jnp.dot(second, w_up, preferred_element_type=jnp.float32) + bias_up.astype(jnp.float32)
    activated = jax.nn.gelu(hidden).astype(jnp.bfloat16)
    result = (
        middle
        + jnp.dot(activated, w_down, preferred_element_type=jnp.float32)
        + bias_down.astype(jnp.float32)
    ) * valid
    saved = (
        normed,
        query,
        keys,
        values,
        probs,
        probs_low,
        mixed,
        middle,
        second,
        hidden,
        activated,
        valid,
    )
    return (result, saved)


def backward_item(inputs, length, bias, weights, upstream, onehot):
    (
        w_qkv,
        w_out,
        w_up,
        w_down,
        gain_one,
        shift_one,
        gain_two,
        shift_two,
        bias_out,
        bias_up,
        bias_down,
    ) = weights
    _, saved = forward_item(inputs, length, bias, weights)
    (
        normed,
        query,
        keys,
        values,
        probs,
        probs_low,
        mixed,
        middle,
        second,
        hidden,
        activated,
        valid,
    ) = saved
    rows, width = inputs.shape
    heads = bias.shape[0]
    head_dim = width // heads
    scale = head_dim ** (-0.5)
    direct = upstream * valid
    d_branch = direct.astype(jnp.bfloat16)
    grad_bdown = jnp.sum(d_branch.astype(jnp.float32), axis=0)
    d_activated = contract_cols(d_branch, w_down)
    _, gelu_back = jax.vjp(jax.nn.gelu, hidden)
    d_hidden = gelu_back(d_activated)[0].astype(jnp.bfloat16)
    grad_bup = jnp.sum(d_hidden.astype(jnp.float32), axis=0)
    d_second = contract_cols(d_hidden, w_up)
    _, second_back = jax.vjp(
        norm_affine, middle, gain_two.astype(jnp.float32), shift_two.astype(jnp.float32)
    )
    d_middle, grad_gain_two, grad_shift_two = second_back(d_second)
    d_middle = d_middle + direct
    d_attn = d_middle.astype(jnp.bfloat16)
    grad_bout = jnp.sum(d_attn.astype(jnp.float32), axis=0)
    d_mixed = contract_cols(d_attn, w_out).astype(jnp.bfloat16).reshape(rows, heads, head_dim)
    grad_values = jnp.einsum("hij,ihd->jhd", probs_low, d_mixed, preferred_element_type=jnp.float32)
    d_probs = jnp.einsum("ihd,jhd->hij", d_mixed, values, preferred_element_type=jnp.float32)
    d_scores = (probs * (d_probs - jnp.sum(probs * d_probs, axis=-1, keepdims=True))).astype(
        jnp.bfloat16
    )
    grad_query = (
        jnp.einsum("hij,jhd->ihd", d_scores, keys, preferred_element_type=jnp.float32) * scale
    )
    grad_keys = (
        jnp.einsum("hij,ihd->jhd", d_scores, query, preferred_element_type=jnp.float32) * scale
    )
    d_qkv = jnp.concatenate(
        [
            grad_query.reshape(rows, width),
            grad_keys.reshape(rows, width),
            grad_values.reshape(rows, width),
        ],
        axis=1,
    ).astype(jnp.bfloat16)
    d_normed = contract_cols(d_qkv, w_qkv)
    _, first_back = jax.vjp(
        norm_affine, inputs, gain_one.astype(jnp.float32), shift_one.astype(jnp.float32)
    )
    d_inputs, grad_gain_one, grad_shift_one = first_back(d_normed)
    d_inputs = d_inputs + d_middle
    per_distance = diagonal_sums(d_scores.astype(jnp.float32))
    grad_table = jnp.dot(onehot, per_distance.T, precision=highest).reshape(-1)
    factors = (normed, d_qkv, mixed, d_attn, second, d_hidden, activated, d_branch)
    small = (
        grad_gain_one,
        grad_shift_one,
        grad_gain_two,
        grad_shift_two,
        grad_bout,
        grad_bup,
        grad_bdown,
        grad_table,
    )
    return (d_inputs, factors, small)


def local(
    audio_in,
    out_grad,
    item_len,
    rel_bucket,
    w_qkv,
    w_out,
    w_up,
    w_down,
    ln1_gain,
    ln1_bias,
    ln2_gain,
    ln2_bias,
    b_out,
    b_up,
    b_down,
    rel_table,
):
    section = lax.axis_index("section")
    micro = audio_in.shape[0]
    rows = audio_in.shape[2]
    width = audio_in.shape[3]
    qkv_part = w_qkv[0].astype(jnp.bfloat16)
    out_part = w_out[0].astype(jnp.bfloat16)
    up_part = w_up[0].astype(jnp.bfloat16)
    down_part = w_down[0].astype(jnp.bfloat16)
    gain_one_part = ln1_gain[0].astype(jnp.bfloat16)
    shift_one_part = ln1_bias[0].astype(jnp.bfloat16)
    gain_two_part = ln2_gain[0].astype(jnp.bfloat16)
    shift_two_part = ln2_bias[0].astype(jnp.bfloat16)
    bias_out_part = b_out[0].astype(jnp.bfloat16)
    bias_up_part = b_up[0].astype(jnp.bfloat16)
    bias_down_part = b_down[0].astype(jnp.bfloat16)
    table_part = rel_table[0].astype(jnp.bfloat16)
    parts = (
        qkv_part,
        out_part,
        up_part,
        down_part,
        gain_one_part,
        shift_one_part,
        gain_two_part,
        shift_two_part,
        bias_out_part,
        bias_up_part,
        bias_down_part,
        table_part,
    )
    gathered = (
        lax.all_gather(qkv_part, "dp", axis=0, tiled=True),
        lax.all_gather(out_part, "dp", axis=0, tiled=True),
        lax.all_gather(up_part, "dp", axis=0, tiled=True),
        lax.all_gather(down_part, "dp", axis=0, tiled=True),
        lax.all_gather(gain_one_part, "dp", axis=0, tiled=True),
        lax.all_gather(shift_one_part, "dp", axis=0, tiled=True),
        lax.all_gather(gain_two_part, "dp", axis=0, tiled=True),
        lax.all_gather(shift_two_part, "dp", axis=0, tiled=True),
        lax.all_gather(bias_out_part, "dp", axis=0, tiled=True),
        lax.all_gather(bias_up_part, "dp", axis=0, tiled=True),
        lax.all_gather(bias_down_part, "dp", axis=0, tiled=True),
        lax.all_gather(table_part, "dp", axis=0, tiled=True),
    )
    onehot = bucket_table(rel_bucket)
    weights = gathered[:11]
    bias = make_bias(gathered[11], onehot)
    lengths = item_len[:, 0]
    hidden_width = gathered[2].shape[1]

    def run_forward(layer_in, length):
        return forward_item(layer_in.astype(jnp.float32), length, bias, weights)[0]

    def skip_forward(layer_in, length):
        return jnp.zeros(layer_in.shape, jnp.float32)

    incoming = jnp.zeros((rows, width), jnp.bfloat16)
    produced = []
    taken = []
    for tick in range(micro + 1):
        slot = tick - section
        active = jnp.logical_and(slot >= 0, slot < micro)
        length = lengths[jnp.clip(slot, 0, micro - 1)]
        own = audio_in[min(tick, micro - 1), 0]
        layer_in = jnp.where(section == 0, own, incoming)
        layer_out = lax.cond(active, run_forward, skip_forward, layer_in, length).astype(
            jnp.bfloat16
        )
        produced.append(layer_out)
        taken.append(layer_in)
        if tick < micro:
            incoming = passed_along(layer_out, "section", 1)
    outputs = jnp.stack(
        [jnp.where(section == 0, produced[batch], produced[batch + 1]) for batch in range(micro)]
    )
    kept = jnp.stack(
        [jnp.where(section == 0, taken[batch], taken[batch + 1]) for batch in range(micro)]
    )
    regathered = (
        lax.all_gather(qkv_part, "dp", axis=0, tiled=True),
        lax.all_gather(out_part, "dp", axis=0, tiled=True),
        lax.all_gather(up_part, "dp", axis=0, tiled=True),
        lax.all_gather(down_part, "dp", axis=0, tiled=True),
        lax.all_gather(gain_one_part, "dp", axis=0, tiled=True),
        lax.all_gather(shift_one_part, "dp", axis=0, tiled=True),
        lax.all_gather(gain_two_part, "dp", axis=0, tiled=True),
        lax.all_gather(shift_two_part, "dp", axis=0, tiled=True),
        lax.all_gather(bias_out_part, "dp", axis=0, tiled=True),
        lax.all_gather(bias_up_part, "dp", axis=0, tiled=True),
        lax.all_gather(bias_down_part, "dp", axis=0, tiled=True),
        lax.all_gather(table_part, "dp", axis=0, tiled=True),
    )
    back_weights = regathered[:11]
    back_bias = make_bias(regathered[11], onehot)

    def run_backward(layer_in, length, upstream):
        return backward_item(
            layer_in.astype(jnp.float32), length, back_bias, back_weights, upstream, onehot
        )

    def skip_backward(layer_in, length, upstream):
        zero_rows = jnp.zeros((rows, width), jnp.bfloat16)
        zero_triple = jnp.zeros((rows, 3 * width), jnp.bfloat16)
        zero_hidden = jnp.zeros((rows, hidden_width), jnp.bfloat16)
        factors = (
            zero_rows,
            zero_triple,
            zero_rows,
            zero_rows,
            zero_rows,
            zero_hidden,
            zero_hidden,
            zero_rows,
        )
        small = tuple((jnp.zeros(piece.shape, jnp.float32) for piece in gathered[4:]))
        return (jnp.zeros(upstream.shape, jnp.float32), factors, small)

    small_totals = tuple((jnp.zeros(piece.shape, jnp.float32) for piece in gathered[4:]))
    shares = tuple((jnp.zeros(piece.shape, jnp.float32) for piece in parts))
    returned = jnp.zeros((rows, width), jnp.bfloat16)
    results = []
    sent_list = []
    factor_list = []
    for tick in range(micro + 1):
        slot = tick - 1 + section
        active = jnp.logical_and(slot >= 0, slot < micro)
        pick = jnp.clip(slot, 0, micro - 1)
        length = lengths[pick]
        layer_in = kept[pick]
        target = out_grad[min(tick, micro - 1), 0].astype(jnp.float32)
        upstream = jnp.where(section == 1, target, returned.astype(jnp.float32))
        d_inputs, factors, small = lax.cond(
            active, run_backward, skip_backward, layer_in, length, upstream
        )
        factor_list.append(factors)
        small_totals = tuple((total + term for total, term in zip(small_totals, small)))
        results.append(d_inputs)
        if tick < micro:
            sent = d_inputs.astype(jnp.bfloat16)
            sent_list.append(lax.optimization_barrier(sent))
            returned = passed_along(sent, "section", -1)
    stacked = tuple(
        (jnp.concatenate([entry[index] for entry in factor_list], axis=0) for index in range(8))
    )
    totals = weight_terms(stacked) + small_totals
    shares = (
        lax.psum_scatter(totals[0], "dp", scatter_dimension=0, tiled=True),
        lax.psum_scatter(totals[1], "dp", scatter_dimension=0, tiled=True),
        lax.psum_scatter(totals[2], "dp", scatter_dimension=0, tiled=True),
        lax.psum_scatter(totals[3], "dp", scatter_dimension=0, tiled=True),
        lax.psum_scatter(totals[4], "dp", scatter_dimension=0, tiled=True),
        lax.psum_scatter(totals[5], "dp", scatter_dimension=0, tiled=True),
        lax.psum_scatter(totals[6], "dp", scatter_dimension=0, tiled=True),
        lax.psum_scatter(totals[7], "dp", scatter_dimension=0, tiled=True),
        lax.psum_scatter(totals[8], "dp", scatter_dimension=0, tiled=True),
        lax.psum_scatter(totals[9], "dp", scatter_dimension=0, tiled=True),
        lax.psum_scatter(totals[10], "dp", scatter_dimension=0, tiled=True),
        lax.psum_scatter(totals[11], "dp", scatter_dimension=0, tiled=True),
    )
    input_grads = jnp.stack(
        [
            jnp.where(section == 0, results[batch + 1], sent_list[batch].astype(jnp.float32))
            for batch in range(micro)
        ]
    )
    grads_out = tuple((share[None] for share in shares))
    return (outputs[None, :, None], input_grads[None, :, None]) + grads_out


E5 = 1e-05
F32 = jnp.float32
BF = jnp.bfloat16
MESH = pl.DeviceIdType.MESH
GELU_K = 0.7978845608028654
HD = 64


class Place:
    def __init__(self):
        self.s = lax.axis_index("section")
        d = lax.axis_index("dp")
        self.x = d % 2
        self.y = (d // 2) % 2
        self.z = (d // 4) % 2
        self.h = d // 8
        self.t = self.x + 2 * self.z

    def device(self, s=None, x=None, y=None, z=None, h=None):
        s = self.s if s is None else s
        x = self.x if x is None else x
        y = self.y if y is None else y
        z = self.z if z is None else z
        h = self.h if h is None else h
        return (s, x + 2 * y + 4 * z + 8 * h)

    def sibling(self):
        return self.device(s=1 - self.s)

    def across_y(self):
        return self.device(y=1 - self.y)

    def across_h(self):
        return self.device(h=1 - self.h)

    def mate(self, k):
        return self.x + (k % 2) * (1 - 2 * self.x), self.z + (k // 2) * (1 - 2 * self.z)

    def team(self, k):
        px, pz = self.mate(k)
        return self.device(x=px, z=pz), px + 2 * pz


def remote(src, dst, send, recv, device):
    return pltpu.make_async_remote_copy(
        src_ref=src, dst_ref=dst, send_sem=send, recv_sem=recv, device_id=device, device_id_type=MESH
    )


def dot(a, b):
    return jnp.dot(a, b, preferred_element_type=F32)


def dot_nt(a, b):
    return lax.dot_general(a, b, (((1,), (1,)), ((), ())), preferred_element_type=F32)


def dot_tn(a, b):
    return lax.dot_general(a, b, (((0,), (0,)), ((), ())), preferred_element_type=F32)


def rows_norm(v):
    centre = v - jnp.mean(v, axis=-1, keepdims=True)
    scale = lax.rsqrt(jnp.mean(centre * centre, axis=-1, keepdims=True) + E5)
    return centre * scale, scale


def norm_back(cot, normed, scale, gain):
    inner = cot * gain
    return scale * (
        inner
        - jnp.mean(inner, axis=-1, keepdims=True)
        - normed * jnp.mean(inner * normed, axis=-1, keepdims=True)
    )


def column_sum(v):
    return jnp.sum(v, axis=0, keepdims=True)


def lanes_of(shape, axis=1):
    return lax.broadcasted_iota(jnp.int32, shape, axis)


def split_heads(block, count, size):
    lane = lanes_of(block.shape) // size
    return jnp.concatenate([jnp.where(lane == i, block, jnp.zeros_like(block)) for i in range(count)], axis=0)


def join_heads(block, count, size):
    rows = block.shape[0] // count
    lane = lanes_of((rows, block.shape[1])) // size
    total = jnp.where(lane == 0, block[:rows], 0.0)
    for i in range(1, count):
        total = jnp.where(lane == i, block[i * rows : (i + 1) * rows], total)
    return total


def turn(block, shift):
    width = block.shape[1]
    shift = shift % width
    return jnp.concatenate([block[:, width - shift :], block[:, : width - shift]], axis=1)


def skew(block, length, sign):
    row = lanes_of(block.shape, 0) % length
    for bit in range(7):
        block = jnp.where((row // 2**bit) % 2 == 1, turn(block, sign * 2**bit), block)
    return block


class Part:
    def __init__(self, index, pieces, **refs):
        self.index = index
        self.pieces = pieces
        self.chunks = 2 + pieces
        for name, ref in refs.items():
            setattr(self, name, ref)

    def strip(self, c, rows):
        step = rows // self.pieces
        return pl.ds((c - 2) * step, step)


def step_kernel(
    x_ref, og_ref, il_ref, rb_ref, wq_in, wo_in, wu_in, wd_in,
    v0_ref, v1_ref, v2_ref, v3_ref, v4_ref, v5_ref, bu_ref, rt_ref,
    lo, ig, OQ, OO, OU, OD, OT,
    SQ, SU, WQ, WO, WU, WD, XG, XIN, A, C, FA, MIX, QKV, PR, UF, HM, DZ, DAT, DU, DQ,
    XA, XC, XF, XM, XDZ, XDAT, XDU, XDQ, RB, SB, OWN, OWNY, DX, DH,
    GQ, GO, GU, GD, YQ, YO, YU, YD, ZSQ, ZSO, ZSU, ZSD, ZRQ, ZRO, ZRU, ZRD, TRQ, TRU,
    SPT, SPR, VEC, LEN, BIAS, PD, SGV, SBU, DS, MT, MR, M1, MN,
    ls, ss_a, rs_a, ss_wy, rs_wy, ss_wh, rs_wh, ss_ws, rs_ws, ss_p, rs_p,
    ss_g, rs_g, ss_r, rs_r, ss_x, rs_x, ss_o, rs_o,
    ss_gy, rs_gy, ss_gh, rs_gh, ss_gt, rs_gt, ss_m, rs_m,
):
    p = Place()
    s, x, y, z, h, t = p.s, p.x, p.y, p.z, p.h, p.t
    sib, ypeer, hpeer = p.sibling(), p.across_y(), p.across_h()
    rows, width = x_ref.shape[1], x_ref.shape[2]
    heads = 4
    wide = heads * HD
    ff = FA.shape[3]
    part_rows = WO.shape[2]
    block = WD.shape[2]

    def only(core, what):
        @pl.when(s == core)
        def _():
            what()

    SY, RY = DU.at[0], DAT.at[0]
    half = rows // 2
    upper, lower = pl.ds(0, half), pl.ds(half, half)
    x_dev, x_slot = p.team(1)
    z_dev, z_slot = p.team(2)
    d_slot = p.team(3)[1]

    def hop(ref, c, n, slot, span, device):
        view = ref.at[slot, span]
        return remote(view, view, ss_g.at[c, n], rs_g.at[c, n], device)

    def gather_sends(ref, c):
        return (
            hop(ref, c, 2, t, upper, z_dev), hop(ref, c, 0, t, upper, x_dev),
            hop(ref, c, 3, t, lower, z_dev), hop(ref, c, 1, t, lower, x_dev),
        )

    def relays(ref, c):
        return hop(ref, c, 4, z_slot, upper, x_dev), hop(ref, c, 5, z_slot, lower, x_dev)

    def gather_start(ref, c):
        for cp in gather_sends(ref, c):
            cp.start()

    def gather_relay(ref, c):
        onward = relays(ref, c)
        hop(ref, c, 2, z_slot, upper, z_dev).wait_recv()
        onward[0].start()
        hop(ref, c, 3, z_slot, lower, z_dev).wait_recv()
        onward[1].start()

    def gather_take(ref, c, k):
        if k == 1:
            hop(ref, c, 0, x_slot, upper, x_dev).wait_recv()
            hop(ref, c, 1, x_slot, lower, x_dev).wait_recv()
        if k == 3:
            hop(ref, c, 4, d_slot, upper, x_dev).wait_recv()
            hop(ref, c, 5, d_slot, lower, x_dev).wait_recv()

    def gather_end(ref, c):
        for cp in gather_sends(ref, c) + relays(ref, c):
            cp.wait_send()

    def reduce_copy(c, k, side=False):
        out, land = (SY, RY) if side else (SB, RB)
        return remote(out.at[k], land.at[k], ss_r.at[c, k], rs_r.at[c, k], p.team(k)[0])

    def reduce_put(c, k, value, side=False):
        @pl.when(k == 0)
        def _():
            (OWNY if side else OWN)[...] = value

        @pl.when(k > 0)
        def _():
            (SY if side else SB)[k] = value.astype(BF)
            reduce_copy(c, k, side).start()

    def reduce_end(c, side=False):
        total = (OWNY if side else OWN)[...]
        for k in (1, 2, 3):
            reduce_copy(c, k, side).wait()
            total = total + (RY if side else RB)[k].astype(F32)
        return total

    def each_item(gathers, body, aside, relay=True):
        def step(n, carry):
            if relay:

                @pl.when(n == 1)
                def _():
                    gather_relay(*gathers[0])

            for m, mate in ((2, 1), (3, 3)):

                @pl.when(n == m)
                def _(mate=mate):
                    for ref, c in gathers:
                        gather_take(ref, c, mate)

            k = 2 * (n % 2) + n // 2
            body(k, p.team(k)[1])
            aside(n)
            return carry

        lax.fori_loop(0, 4, step, 0)
        for ref, c in gathers:
            gather_end(ref, c)

    def at_step(k, here, n, what):
        @pl.when(jnp.logical_and(here, k == n))
        def _():
            what()

    first = Part(0, 1, W=WQ, V=WO, S=SQ, G=GQ, R=GO, Y=YQ, YR=YO, ZS=ZSQ, ZSR=ZSO, ZR=ZRQ, ZRR=ZRO,
                 TS=SQ, TR=TRQ, O=OQ, OR=OO)
    second = Part(1, 2, W=WU, V=WD, S=SU, G=GU, R=GD, Y=YU, YR=YD, ZS=ZSU, ZSR=ZSD, ZR=ZRU, ZRR=ZRD,
                  TS=SU, TR=TRU, O=OU, OR=OD)

    loads = [
        pltpu.make_async_copy(wq_in.at[:, pl.ds(width * i, width)], UF.at[pl.ds(576 + 64 * i, 64)], ls.at[i])
        for i in range(3)
    ]
    loads.append(pltpu.make_async_copy(wo_in, UF.at[pl.ds(0, 64)], ls.at[3]))
    loads += [
        pltpu.make_async_copy(wu_in.at[:, pl.ds(width * i, width)], UF.at[pl.ds(320 + 64 * i, 64)], ls.at[4 + i])
        for i in range(4)
    ]
    loads.append(pltpu.make_async_copy(wd_in, UF.at[pl.ds(64, 256)], ls.at[8]))
    loads.append(pltpu.make_async_copy(x_ref.at[s], XG.at[t], ls.at[9]))
    loads.append(pltpu.make_async_copy(og_ref.at[s], DZ.at[1, t], ls.at[10]))
    for cp in loads:
        cp.start()

    bell = pltpu.get_barrier_semaphore()
    around = [(a, b, e) for a in range(2) for b in range(2) for e in range(2)][1:]

    def station(a, b, e):
        return p.device(s=s + a * (1 - 2 * s), y=y + b * (1 - 2 * y), h=h + e * (1 - 2 * h))

    everyone = [p.team(k)[0] for k in (1, 2, 3)] + [station(*o) for o in around]
    for peer in everyone:
        pl.semaphore_signal(bell, inc=1, device_id=peer, device_id_type=MESH)

    for cp in loads[:4]:
        cp.wait()
    for i in range(3):
        for hh in range(2):
            for zz in range(2):
                base = (2 * zz + 4 * hh) * 128
                even = UF[576 + 64 * i : 640 + 64 * i, base : base + 128].astype(BF)
                odd = UF[576 + 64 * i : 640 + 64 * i, base + 128 : base + 256].astype(BF)
                at = (2 * i + hh) * 128
                SQ[2 * zz, :, at : at + 128] = jnp.concatenate([even[:, :HD], odd[:, :HD]], axis=1)
                SQ[2 * zz + 1, :, at : at + 128] = jnp.concatenate([even[:, HD:], odd[:, HD:]], axis=1)
    WQ[s, h, z, y, x] = SQ[t]
    q = 2 * h + y
    WO[s, q] = UF[0:64, :].astype(BF)
    pl.semaphore_wait(bell, len(everyone))

    def w_team(part, k):
        device, slot = p.team(k)
        return remote(
            part.S.at[slot], part.W.at[s, h, z, y, x], ss_a.at[part.index, k], rs_a.at[part.index, k], device
        )

    def w_view(part, c, hh, yy):
        if c < 2:
            return part.W.at[s, hh, c, yy]
        return part.V.at[s, 2 * hh + yy, part.strip(c, part.V.shape[2])]

    def w_y(part, c, n):
        view = w_view(part, c, h + n * (1 - 2 * h), y)
        return remote(view, view, ss_wy.at[part.index, n, c], rs_wy.at[part.index, n, c], ypeer)

    def w_h(part, c):
        view = w_view(part, c, h, y)
        return remote(view, view, ss_wh.at[part.index, c], rs_wh.at[part.index, c], hpeer)

    def w_s(part, c, hh, yy):
        view = w_view(part, c, hh, yy)
        n = 2 * hh + yy
        return remote(view, view, ss_ws.at[part.index, n, c], rs_ws.at[part.index, n, c], sib)

    order = ((first, 2), (first, 0), (first, 1), (second, 0), (second, 1), (second, 2), (second, 3))

    def w_share(j):
        part, c = order[j]
        if j in (1, 3):
            for k in (1, 2, 3):
                w_team(part, k).wait_recv()
        w_h(part, c).start()
        w_y(part, c, 0).start()
        w_s(part, c, h, y).start()

    def w_pass(j):
        part, c = order[j]
        w_h(part, c).wait_recv()
        w_y(part, c, 1).start()
        w_s(part, c, 1 - h, y).start()
        if j + 2 < len(order):
            w_share(j + 2)

    def w_near(part):
        for c in range(part.chunks):
            w_y(part, c, 0).wait_recv()
            w_s(part, c, h, 1 - y).start()

    def w_far(part):
        for c in range(part.chunks):
            w_y(part, c, 1).wait_recv()
            w_s(part, c, 1 - h, 1 - y).start()

    def w_other(part):
        for c in range(part.chunks):
            for n in range(4):
                w_s(part, c, n // 2, n % 2).wait_recv()

    for k in (1, 2, 3):
        w_team(first, k).start()
    loads[9].wait()

    @pl.when(s == 0)
    def _():
        w_share(0)

    for cp in loads[4:9]:
        cp.wait()
    for hh in range(2):
        for zz in range(2):
            for yy in range(2):
                for xx in range(2):
                    at = (2 * hh + yy) * block
                    low = 320 + 64 * (zz + 2 * hh)
                    col = (xx + 2 * yy) * block
                    SU[xx + 2 * zz, :, at : at + block] = UF[low : low + 64, col : col + block].astype(BF)
    WU[s, h, z, y, x] = SU[t]
    WD[s, q] = UF[64 : 64 + block, :].astype(BF)

    position = lanes_of((rows, 1), 0).astype(F32)
    count = jnp.where(s == 0, il_ref[0:1, :], il_ref[1:2, :]).astype(F32)
    valid = (position < count).astype(F32)
    loads[10].wait()
    DZ[1, t] = (valid * DZ[1, t].astype(F32)).astype(BF)

    lane = lanes_of((1, 128))
    zero = jnp.zeros((1, 128), F32)
    pair = [jnp.concatenate([v[...], v[...]], axis=1) for v in (v0_ref, v1_ref, v2_ref, v3_ref, v4_ref, v5_ref)]
    lines = [jnp.where(lane // HD == x, v, zero) for v in pair]
    for xx in range(2):
        for i in range(2):
            lines.append(jnp.where(x == xx, bu_ref[:, 128 * i : 128 * i + 128], zero))
    table = jnp.concatenate([rt_ref[...], jnp.zeros((1, 96), F32)], axis=1)
    counts = jnp.where(lane == 0, il_ref[0:1, :].astype(F32), jnp.where(lane == 1, il_ref[1:2, :].astype(F32), zero))
    for piece in (table, counts):
        for xx in range(2):
            lines.append(jnp.where(x == xx, piece, zero))
    for i in range(2):
        lines.append(zero)
    for i in range(16):
        SPR[t, h, y, s, i : i + 1, :] = lines[i].astype(BF).astype(F32)

    def near_copy(n):
        view = SPR.at[t, h, y, s]
        return remote(view, view, ss_p.at[n], rs_p.at[n], station(*around[n]))

    def team_copy(k):
        view = SPR.at[t]
        return remote(view, view, ss_p.at[6 + k], rs_p.at[6 + k], p.team(k)[0])

    for n in range(7):
        near_copy(n).start()
    only(0, lambda: w_share(1))
    gather_start(XG, 0)
    for n in range(7):
        near_copy(n).wait()
    for k in (1, 2, 3):
        team_copy(k).start()
    for k in (1, 2, 3):
        w_team(second, k).start()
    only(0, lambda: w_pass(0))
    gather_relay(XG, 0)
    for k in (1, 2, 3):
        team_copy(k).wait()
    for hh in range(2):
        for zz in range(2):
            for yy in range(2):
                for i in range(2):
                    SPT[hh, zz, yy, i] = SPR[2 * zz, hh, yy, i] + SPR[2 * zz + 1, hh, yy, i]
    gather_start(DZ.at[1], 4)
    only(0, lambda: (w_pass(1), w_pass(2)))

    for hh in range(2):
        for zz in range(2):
            for yy in range(2):
                at = (yy + 2 * zz + 4 * hh) * 128
                for i in range(2):
                    VEC[i, 0:6, at : at + 128] = SPT[hh, zz, yy, i, 0:6, :]
    for i in range(2):
        for hh in range(2):
            for yy in range(2):
                tile = SPT[hh, z, yy, i]
                for r in range(2):
                    at = (2 * hh + yy) * block + 128 * r
                    VEC[i, 6:7, at : at + 128] = jnp.where(x == 0, tile[6 + r : 7 + r], tile[8 + r : 9 + r])
    for zz in range(2):
        tile = SPT[h, zz, y, 0]
        for xx in range(2):
            tokens = jnp.sum(jnp.where(lane == s, tile[12 + xx : 13 + xx], 0.0), axis=1, keepdims=True)
            LEN[xx + 2 * zz] = jnp.broadcast_to(tokens, (8, 128))

    mark = jnp.concatenate([rb_ref[...], jnp.full((1, 128 - rows), 2 * NB, jnp.int32)], axis=1).astype(BF)
    mark = jnp.broadcast_to(mark, (8, 128))
    flip = ((lanes_of((128, 128), 0) + lanes_of((128, 128))) % 128 == 0).astype(F32).astype(BF)
    mark = dot(mark, flip)[0:1]
    onehot = (lanes_of((NB, 128), 0).astype(F32) == mark).astype(F32)
    for i in range(2):
        lines = []
        for hh in range(2):
            for zz in range(2):
                for yy in range(2):
                    tile = SPT[hh, zz, yy, i]
                    for xx in range(2):
                        for b in range(2):
                            lines.append(tile[10 + xx : 11 + xx, 16 * b : 16 * b + 16])
        by_bucket = jnp.concatenate([jnp.concatenate(lines, axis=0), jnp.zeros((NB, 112), F32)], axis=1)
        PD[...] = dot_tn(by_bucket.astype(BF), onehot.astype(BF))
        stack = []
        for hh in range(2):
            for yy in range(2):
                line = PD[pl.ds(x + 2 * yy + 4 * z + 8 * hh, 1), :]
                stack.append(jnp.broadcast_to(line, (rows, 128)))
        grid = skew(jnp.concatenate(stack, axis=0), rows, 1)[:, :rows]
        causal = lanes_of(grid.shape) <= lanes_of(grid.shape, 0) % rows
        BIAS[i] = jnp.where(causal, grid, -1000000000.0)
    gather_relay(DZ.at[1], 4)

    pairs = ((A, XA), (MIX, XM), (C, XC), (FA, XF), (DZ, XDZ), (DAT, XDAT), (DU, XDU), (DQ, XDQ))

    def share_copy(i, layer, slot):
        return remote(pairs[i][0].at[layer, slot], pairs[i][1].at[slot], ss_x.at[i, slot], rs_x.at[i, slot], sib)

    def share_item(k, layer, which):
        @pl.when(s != layer)
        def _():
            for i in which:
                share_copy(i, layer, p.team(k)[1]).start()

    def row(layer, index):
        return VEC[layer, index : index + 1, :]

    def w_qkv(layer):
        return WQ[layer].reshape(width, 3 * wide)

    def w_up(layer):
        return WU[layer].reshape(width, ff)

    def w_out(layer):
        return WO[layer].reshape(wide, width)

    def w_down(layer):
        return WD[layer].reshape(ff, width)

    def u_rows(layer, i):
        return pl.ds(pl.multiple_of((layer * 4 + i) * rows, 8), rows)

    def g_own(part, c, hh, yy):
        if c < 2:
            return part.G.at[hh, c, yy]
        return part.R.at[2 * hh + yy, part.strip(c, part.R.shape[1])]

    def g_land(part, c, n):
        if c < 2:
            return part.Y.at[n, c]
        return part.YR.at[n, part.strip(c, part.R.shape[1])]

    def g_half(n):
        return (1 - h) + n * (2 * h - 1)

    def g_big(part, c, n):
        return remote(
            part.G.at[g_half(n), c, 1 - y], part.Y.at[n, c],
            ss_gy.at[part.index, n, c], rs_gy.at[part.index, n, c], ypeer,
        )

    def g_y(part, c, n):
        return remote(
            g_own(part, c, g_half(n), 1 - y), g_land(part, c, n),
            ss_gy.at[part.index, n, c], rs_gy.at[part.index, n, c], ypeer,
        )

    def g_z(part, c, out):
        if c < 2:
            return (part.ZS if out else part.ZR).at[c]
        return (part.ZSR if out else part.ZRR).at[part.strip(c, part.R.shape[1])]

    def g_h(part, c):
        return remote(
            g_z(part, c, True), g_z(part, c, False), ss_gh.at[part.index, c], rs_gh.at[part.index, c], hpeer
        )

    def g_t(part, k):
        return remote(
            part.TS.at[k], part.TR.at[k], ss_gt.at[part.index, k], rs_gt.at[part.index, k], p.team(k)[0]
        )

    def flat(ref, span):
        value = ref[:, :, span]
        return value.reshape(value.shape[0] * value.shape[1], value.shape[2])

    def product(left, right, span):
        every = pl.ds(0, right[0].shape[2])
        return dot_tn(flat(left[0], span), flat(right[0], every)) + dot_tn(
            flat(left[1], span), flat(right[1], every)
        )

    def g_make(part, n):
        if part is first:
            need = (0, 1, 5, 7)
            big_l, big_r = (A.at[s], XA), (DQ.at[s], XDQ)
            small_l, small_r = (MIX.at[s], XM), (DAT.at[s], XDAT)
            small_span = HD
        else:
            need = (2, 3, 4, 6)
            big_l, big_r = (C.at[s], XC), (DU.at[s], XDU)
            small_l, small_r = (FA.at[s], XF), (DZ.at[s], XDZ)
            small_span = block
        if n == 0:
            for i in need:
                for slot in range(4):
                    share_copy(i, s, slot).wait_recv()
        hh = g_half(n)
        if part is first:
            if n == 0:
                value = product(small_l, small_r, pl.ds(0, wide)).astype(BF)
                for i in range(4):
                    part.R[i] = value[i * small_span : (i + 1) * small_span]
            if n == 0:
                g_y(part, 2, n).start()

        def tile(zz, carry):
            span = pl.ds(pl.multiple_of((2 * hh + zz) * 256, 256), 256)
            value = product(big_l, big_r, span).astype(BF)
            part.G[hh, zz] = value.reshape(2, 2, part_rows, value.shape[1])
            if n == 0:
                g_big(part, zz, n).start()
            return carry

        lax.fori_loop(0, 2, tile, 0)
        if part is second:

            def strip(m, carry):
                yy = (1 - y) + m * (2 * y - 1)
                span = pl.ds(pl.multiple_of((2 * hh + yy) * 256, 256), 256)
                part.R[2 * hh + yy] = product(small_l, small_r, span).astype(BF)

                if n == 0:

                    @pl.when(m == 0)
                    def _():
                        for c in range(2, part.chunks):
                            g_y(part, c, n).start()

                return carry

            lax.fori_loop(0, 2, strip, 0)

    def g_fold(part, c):
        g_y(part, c, 0).wait_recv()
        g_z(part, c, True)[...] = (
            g_own(part, c, 1 - h, y)[...].astype(F32) + g_land(part, c, 0)[...].astype(F32)
        ).astype(BF)
        g_h(part, c).start()

    def g_later(part):
        for c in range(part.chunks):
            g_y(part, c, 1).start()

    def g_total(part):
        for c in range(part.chunks):
            g_y(part, c, 1).wait_recv()
            g_h(part, c).wait_recv()

        def total(xx, zz):
            return (
                part.G[h, zz, y, xx].astype(F32) + part.Y[1, zz, xx].astype(F32) + part.ZR[zz, xx].astype(F32)
            )

        for k in (1, 2, 3):
            part.TS[k] = total(*p.mate(k)).astype(BF)
            g_t(part, k).start()
        part.O[t] = total(x, z)
        part.OR[...] = part.R[q].astype(F32) + part.YR[1].astype(F32) + part.ZRR[...].astype(F32)

    def g_end(part):
        for k in (1, 2, 3):
            g_t(part, k).wait_recv()
            part.O[p.team(k)[1]] = part.TR[k].astype(F32)

    XIN[0] = XG[t]
    DS[...] = jnp.zeros_like(DS)
    SBU[...] = jnp.zeros_like(SBU)
    SGV[...] = jnp.zeros_like(SGV)

    def scaled(value, layer, at):
        return (rows_norm(value)[0] * row(layer, at) + row(layer, at + 1)).astype(BF)

    def attention(layer):
        if layer == 1:
            A[layer, t] = scaled(XIN[layer].astype(F32), layer, 0)
            gather_start(A.at[layer], 2)
        if layer == 0:
            only(0, lambda: w_near(first))
        only(layer, lambda: w_far(first))
        only(1 - layer, lambda: w_other(first))

        def attend(k, i):
            if layer == 0:
                A[layer, i] = scaled(XG[i].astype(F32), layer, 0)
            qkv = dot(A[layer, i], w_qkv(layer)).astype(BF)
            QKV[layer, i] = qkv
            stack = split_heads(qkv[:, :wide], heads, HD)
            scores = dot_nt(stack, qkv[:, wide : 2 * wide]) * (HD ** (-0.5)) + BIAS[layer]
            column = lanes_of(scores.shape).astype(F32)
            scores = jnp.where(column < LEN[i][0:1, 0:1], scores, -1000000000.0)
            raised = jnp.exp(scores - jnp.max(scores, axis=-1, keepdims=True))
            probs = raised / jnp.sum(raised, axis=-1, keepdims=True)
            PR[layer, i] = probs
            mixed = join_heads(dot(probs.astype(BF), qkv[:, 2 * wide :]), heads, HD).astype(BF)
            MIX[layer, i] = mixed
            reduce_put(2 * layer, k, dot(mixed, w_out(layer)))

        def pass_on(k):
            if layer == 0:
                for n in range(4):
                    at_step(k, s == 0, n, lambda n=n: w_pass(3 + n))
                at_step(k, s == 0, 2, lambda: w_near(second))
                at_step(k, s == 1, 2, lambda: (w_share(0), w_share(1)))
                at_step(k, s == 1, 3, lambda: w_pass(0))
            else:
                at_step(k, s == 1, 0, lambda: w_pass(6))
                at_step(k, s == 1, 1, lambda: w_near(second))
            share_item(2 * (k % 2) + k // 2, layer, (0, 1))

        each_item(((XG, 0),) if layer == 0 else ((A.at[layer], 2),), attend, pass_on, relay=layer == 1)
        hmid = XIN[layer].astype(F32) + reduce_end(2 * layer) + row(layer, 4)
        HM[layer] = hmid
        C[layer, t] = scaled(hmid, layer, 2)
        gather_start(C.at[layer], 2 * layer + 1)

    def hidden_back(layer, i, u, th):
        square = u * u
        slope = 0.5 * (1.0 + th) + (0.5 * GELU_K) * u * (1.0 - th * th) * (1.0 + 0.134145 * square)
        du = (dot_nt(DZ[layer, i], w_down(layer)) * slope).astype(BF)
        DU[layer, i] = du
        SBU[layer] += column_sum(du.astype(F32))
        return dot_nt(du, w_up(layer))

    def feed_forward(layer):
        only(layer, lambda: w_far(second))
        only(1 - layer, lambda: w_other(second))
        if layer == 0:
            only(1, lambda: w_pass(1))

        def feed(k, i):
            u = dot(C[layer, i], w_up(layer)) + row(layer, 6)
            th = jnp.tanh(GELU_K * (u + 0.044715 * (u * u * u)))
            if layer == 0:
                UF[u_rows(layer, i), :] = u
            else:
                reduce_put(4, k, hidden_back(layer, i, u, th))
            f = (0.5 * u * (1.0 + th)).astype(BF)
            FA[layer, i] = f
            reduce_put(2 * layer + 1, k, dot(f, w_down(layer)), side=layer == 1)

        def prepare(k):
            if layer == 0:
                for n in range(4):
                    at_step(k, s == 1, n, lambda n=n: w_pass(2 + n))
                at_step(k, s == 1, 2, lambda: w_near(first))
            share_item(2 * (k % 2) + k // 2, layer, (2, 3) if layer == 0 else (2, 3, 4, 6))

        gathers = ((C.at[layer], 2 * layer + 1),)
        if layer == 1:
            gathers += ((DZ.at[layer], 4),)
        each_item(gathers, feed, prepare)

    def layer_result(layer):
        return (valid * (HM[layer] + reduce_end(2 * layer + 1, side=layer == 1) + row(layer, 5))).astype(BF)

    def give_result(layer):
        @pl.when(s == layer)
        def _():
            lo[s] = XIN[layer + 1]

        @pl.when(s != layer)
        def _():
            remote(XIN.at[layer + 1], lo.at[s], ss_o.at[0], rs_o.at[0], sib).start()

    def feed_back(layer):
        def feed(k, i):
            u = UF[u_rows(layer, i), :]
            th = jnp.tanh(GELU_K * (u + 0.044715 * (u * u * u)))
            reduce_put(6, k, hidden_back(layer, i, u, th))

        def fold_first(k):
            for n in range(2):
                at_step(k, s == 1, n, lambda n=n: g_fold(first, n))
            at_step(k, s == 1, 1, lambda: g_later(first))
            share_item(2 * (k % 2) + k // 2, layer, (4, 6))

        each_item(((DZ.at[layer], 6),), feed, fold_first)

    def middle_back(layer):
        dc = reduce_end(6 - 2 * layer)
        normed, scale = rows_norm(HM[layer])
        SGV[layer, 2:3, :] = column_sum(dc * normed)
        SGV[layer, 3:4, :] = column_sum(dc)
        dh = DZ[layer, t].astype(F32) + norm_back(dc, normed, scale, row(layer, 2))
        DH[...] = dh
        dattn = dh.astype(BF)
        DAT[layer, t] = dattn
        gather_start(DAT.at[layer], 7 - 2 * layer)
        SGV[layer, 4:5, :] = column_sum(dattn.astype(F32))
        only(layer, lambda: (g_make(second, 1), g_fold(second, 0), g_fold(second, 1)))

    def attention_back(layer):
        def attend(k, i):
            dmixed = dot_nt(DAT[layer, i], w_out(layer)).astype(BF)
            qkv = QKV[layer, i]
            probs = PR[layer, i]
            stack = split_heads(dmixed, heads, HD)
            dprobs = dot_nt(stack, qkv[:, 2 * wide :])
            dscores = (probs * (dprobs - jnp.sum(probs * dprobs, axis=-1, keepdims=True))).astype(BF)
            DS[layer] += dscores.astype(F32)
            dq = join_heads(dot(dscores, qkv[:, wide : 2 * wide]), heads, HD) * (HD ** (-0.5))
            dk = dot_tn(dscores, split_heads(qkv[:, :wide], heads, HD)) * (HD ** (-0.5))
            dv = dot_tn(probs.astype(BF), stack)
            DQ[layer, i, :, :wide] = dq.astype(BF)
            DQ[layer, i, :, wide : 2 * wide] = dk.astype(BF)
            DQ[layer, i, :, 2 * wide :] = dv.astype(BF)
            reduce_put(7 - 2 * layer, k, dot_nt(DQ[layer, i], w_qkv(layer)))

        def fold_second(k):
            for n in range(2):
                at_step(k, s == layer, n, lambda n=n: g_fold(second, n + 2))
            at_step(k, s == layer, 1, lambda: g_later(second))
            share_item(2 * (k % 2) + k // 2, layer, (5, 7))

        each_item(((DAT.at[layer], 7 - 2 * layer),), attend, fold_second)

    def inputs_back(layer):
        da = reduce_end(7 - 2 * layer)
        normed, scale = rows_norm(XIN[layer].astype(F32))
        dx = DH[...] + norm_back(da, normed, scale, row(layer, 0))
        low = dx.astype(BF)
        if layer == 1:
            dyv = valid * low.astype(F32)
            DZ[0, t] = dyv.astype(BF)
            gather_start(DZ.at[0], 6)
            SGV[0, 5:6, :] = column_sum(dyv)
        SGV[layer, 0:1, :] = column_sum(da * normed)
        SGV[layer, 1:2, :] = column_sum(da)
        result = low.astype(F32) if layer == 1 else dx

        @pl.when(s == layer)
        def _():
            ig[s] = result

        @pl.when(s != layer)
        def _():
            DX[...] = result
            remote(DX, ig.at[s], ss_o.at[1], rs_o.at[1], sib).start()

    attention(0)
    feed_forward(0)
    XIN[1] = layer_result(0)
    attention(1)
    give_result(0)
    feed_forward(1)
    for part in (first, second):
        for k in (1, 2, 3):
            w_team(part, k).wait_send()
    only(1, lambda: g_make(second, 0))
    SGV[1, 5:6, :] = column_sum(DZ[1, t].astype(F32))
    middle_back(1)
    XIN[2] = layer_result(1)
    give_result(1)
    attention_back(1)
    only(1, lambda: g_make(first, 0))
    inputs_back(1)
    only(1, lambda: (g_make(first, 1), g_fold(first, 2)))
    feed_back(0)
    only(0, lambda: g_make(second, 0))
    only(1, lambda: g_total(second))
    middle_back(0)
    attention_back(0)
    only(0, lambda: (g_make(first, 0), g_make(first, 1)))
    inputs_back(0)

    only(0, lambda: (g_fold(first, 2), g_fold(first, 0), g_fold(first, 1), g_later(first)))

    spread = []
    for i in range(2):
        turned = skew(jnp.concatenate([DS[i], jnp.zeros((heads * rows, 128 - rows), F32)], axis=1), rows, -1)
        table = jnp.zeros((128, 128), F32)
        for hh in range(2):
            for yy in range(2):
                n = 2 * hh + yy
                line = column_sum(turned[n * rows : (n + 1) * rows])
                head = x + 2 * yy + 4 * z + 8 * hh
                table = jnp.where(lanes_of((128, 128), 0) == head, line, table)
        spread.append(
            lax.dot_general(
                onehot, table, (((1,), (1,)), ((), ())), precision=highest, preferred_element_type=F32
            )
        )
    for hh in range(2):
        for zz in range(2):
            for yy in range(2):
                j = yy + 2 * zz + 4 * hh
                for i in range(2):
                    MT[hh, zz, yy, i, 0:6, :] = SGV[i, 0:6, 128 * j : 128 * j + 128]
                    for xx in range(2):
                        for r in range(2):
                            at = (2 * hh + yy) * block + 128 * r
                            n = 6 + 2 * xx + r
                            MT[hh, zz, yy, i, n : n + 1, :] = jnp.where(
                                jnp.logical_and(z == zz, x == xx), SBU[i, :, at : at + 128], zero
                            )
                    MT[hh, zz, yy, i, 10:12, :] = jnp.zeros((2, 128), F32)
                    MT[hh, zz, yy, i, 12:16, :] = spread[i][4 * j : 4 * j + 4]

    def team_merge(k):
        return remote(MT.at[:, p.mate(k)[1]], MR.at[k], ss_m.at[6 + k], rs_m.at[6 + k], p.team(k)[0])

    def near_merge(n):
        a, b, e = around[n]
        there = (h + e * (1 - 2 * h), y + b * (1 - 2 * y), s + a * (1 - 2 * s))
        return remote(M1.at[there], MN.at[n], ss_m.at[n], rs_m.at[n], station(a, b, e))

    for k in (1, 2, 3):
        team_merge(k).start()
    only(0, lambda: g_total(second))
    for k in (1, 2, 3):
        team_merge(k).wait()
    for hh in range(2):
        M1[hh] = MT[hh, z] + MR[1, hh] + MR[2, hh] + MR[3, hh]
    for n in range(7):
        near_merge(n).start()
    g_total(first)
    g_end(second)
    for n in range(7):
        near_merge(n).wait()
    tile = M1[h, y, s]
    for n in range(7):
        tile = tile + MN[n]
    OT[...] = tile
    g_end(first)

    for part in (first, second):
        for k in (1, 2, 3):
            g_t(part, k).wait_send()
        for c in range(part.chunks):
            w_h(part, c).wait_send()
            g_h(part, c).wait_send()
            for n in range(2):
                w_y(part, c, n).wait_send()
                g_y(part, c, n).wait_send()
            for n in range(4):
                w_s(part, c, n // 2, n % 2).wait_send()
    for i in range(8):
        for slot in range(4):
            share_copy(i, 1 - s, slot).wait_send()
    remote(XIN.at[1], lo.at[1 - s], ss_o.at[0], rs_o.at[0], sib).wait()
    remote(DX, ig.at[1 - s], ss_o.at[1], rs_o.at[1], sib).wait()


def finish_kernel(
    lo_in, ig_in, oq_in, oo_in, ou_in, od_in, ot_in, half,
    lo, ig, oq, oo, ou, od, a0, a1, a2, a3, a4, bu, a5, tab, OQ, OU, OT, sem,
):
    moves = ((oq_in, OQ), (ou_in, OU), (ot_in, OT), (lo_in, lo), (ig_in, ig), (oo_in, oo), (od_in, od))
    moves = [pltpu.make_async_copy(a, b, sem.at[i]) for i, (a, b) in enumerate(moves)]
    for cp in moves:
        cp.start()
    for cp in moves[:3]:
        cp.wait()
    block = od.shape[0]
    for hh in range(2):
        for zz in range(2):
            for yy in range(2):
                n = 2 * hh + yy
                d = 2 * yy + 4 * zz + 8 * hh
                for i in range(3):
                    at = i * 4 * HD + n * HD
                    to = i * 16 * HD + d * HD
                    oq[:, to : to + 2 * HD] = jnp.concatenate(
                        [OQ[2 * zz, :, at : at + HD], OQ[2 * zz + 1, :, at : at + HD]], axis=1
                    )
                for xx in range(2):
                    ou[:, (d + xx) * block : (d + xx + 1) * block] = OU[xx + 2 * zz, :, n * block : (n + 1) * block]
    x = half[0]
    for i, ref in enumerate((a0, a1, a2, a3, a4, a5)):
        ref[...] = jnp.where(x == 0, OT[i : i + 1, :HD], OT[i : i + 1, HD:])
    for r in range(2):
        bu[:, 128 * r : 128 * r + 128] = jnp.where(x == 0, OT[6 + r : 7 + r, :], OT[8 + r : 9 + r, :])
    for b in range(2):
        tab[:, 16 * b : 16 * b + 16] = jnp.where(x == 0, OT[12 + b : 13 + b, :16], OT[14 + b : 15 + b, :16])
    for cp in moves[3:]:
        cp.wait()


def vm(n=1):
    return [pl.BlockSpec(memory_space=pltpu.VMEM)] * n


def hb(n=1):
    return [pl.BlockSpec(memory_space=pltpu.HBM)] * n


def sems(*shape):
    return pltpu.SemaphoreType.DMA(shape)


def shape_of(dims, kind):
    return jax.ShapeDtypeStruct(dims, kind)


def team_local(
    audio_in, out_grad, item_len, rel_bucket, w_qkv, w_out, w_up, w_down,
    ln1_gain, ln1_bias, ln2_gain, ln2_bias, b_out, b_up, b_down, rel_table,
):
    rows, width = audio_in.shape[2], audio_in.shape[3]
    part = w_qkv.shape[1]
    hidden = w_up.shape[2]
    block = hidden // 16
    wide, ff = width // 4, hidden // 4
    low = lambda *dims: pltpu.VMEM(dims, BF)
    full = lambda *dims: pltpu.VMEM(dims, F32)

    lo, ig, OQ, OO, OU, OD, OT = pl.pallas_call(
        step_kernel,
        out_shape=(
            shape_of((2, rows, width), BF),
            shape_of((2, rows, width), F32),
            shape_of((4, part, 3 * wide), F32),
            shape_of((part, width), F32),
            shape_of((4, part, ff), F32),
            shape_of((block, width), F32),
            shape_of((16, 128), F32),
        ),
        in_specs=hb(2) + vm(2) + hb(4) + vm(8),
        out_specs=tuple(vm(7)),
        scratch_shapes=[
            low(4, part, 3 * wide), low(4, part, ff),
            low(2, 2, 2, 2, 2, part, 3 * wide), low(2, 4, part, width),
            low(2, 2, 2, 2, 2, part, ff), low(2, 4, block, width), low(4, rows, width),
            low(3, rows, width),
            low(2, 4, rows, width), low(2, 4, rows, width), low(2, 4, rows, ff), low(2, 4, rows, wide),
            low(2, 4, rows, 3 * wide), full(2, 4, 4 * rows, rows), full(8 * rows, ff), full(2, rows, width),
            low(2, 4, rows, width), low(2, 4, rows, width), low(2, 4, rows, ff), low(2, 4, rows, 3 * wide),
            low(4, rows, width), low(4, rows, width), low(4, rows, ff), low(4, rows, wide),
            low(4, rows, width), low(4, rows, width), low(4, rows, ff), low(4, rows, 3 * wide),
            low(4, rows, width), low(4, rows, width), full(rows, width),
            full(rows, width), full(rows, width), full(rows, width),
            low(2, 2, 2, 2, part, 3 * wide), low(4, part, width), low(2, 2, 2, 2, part, ff), low(4, block, width),
            low(2, 2, 2, part, 3 * wide), low(2, part, width), low(2, 2, 2, part, ff), low(2, block, width),
            low(2, 2, part, 3 * wide), low(part, width), low(2, 2, part, ff), low(block, width),
            low(2, 2, part, 3 * wide), low(part, width), low(2, 2, part, ff), low(block, width),
            low(4, part, 3 * wide), low(4, part, ff),
            full(2, 2, 2, 2, 16, 128), full(4, 2, 2, 2, 16, 128), full(2, 8, width), full(4, 8, 128),
            full(2, 4 * rows, rows), full(128, 128), full(2, 8, width), full(2, 1, ff), full(2, 4 * rows, rows),
            full(2, 2, 2, 2, 16, 128), full(4, 2, 2, 2, 16, 128), full(2, 2, 2, 16, 128), full(7, 16, 128),
            sems(11), sems(2, 4), sems(2, 4), sems(2, 2, 4), sems(2, 2, 4), sems(2, 4), sems(2, 4),
            sems(2, 4, 4), sems(2, 4, 4), sems(10), sems(10),
            sems(8, 6), sems(8, 6), sems(8, 4), sems(8, 4), sems(8, 4), sems(8, 4), sems(2), sems(2),
            sems(2, 2, 4), sems(2, 2, 4), sems(2, 4), sems(2, 4), sems(2, 4), sems(2, 4), sems(10), sems(10),
        ],
        compiler_params=pltpu.CompilerParams(
            collective_id=0, has_side_effects=True, vmem_limit_bytes=63 << 20
        ),
        name="two_layers",
    )(
        audio_in.reshape(2, rows, width), out_grad.reshape(2, rows, width), item_len, rel_bucket[None],
        w_qkv[0], w_out[0], w_up[0], w_down[0],
        ln1_gain, ln1_bias, ln2_gain, ln2_bias, b_out, b_down, b_up, rel_table,
    )

    half = (lax.axis_index("dp") % 2).reshape(1)
    lo, ig, oq, oo, ou, od, a0, a1, a2, a3, a4, bu, a5, tab = pl.pallas_call(
        finish_kernel,
        out_shape=(
            shape_of((2, rows, width), BF),
            shape_of((2, rows, width), F32),
            shape_of((part, 3 * width), F32),
            shape_of((part, width), F32),
            shape_of((part, hidden), F32),
            shape_of((block, width), F32),
        )
        + (shape_of((1, part), F32),) * 5
        + (shape_of((1, block), F32), shape_of((1, part), F32), shape_of((1, 32), F32)),
        in_specs=hb(7) + [pl.BlockSpec(memory_space=pltpu.SMEM)],
        out_specs=tuple(vm(14)),
        scratch_shapes=[full(4, part, 3 * wide), full(4, part, ff), full(16, 128), sems(7)],
        compiler_params=pltpu.CompilerParams(vmem_limit_bytes=62 << 20),
        name="finish",
    )(lo, ig, OQ, OO, OU, OD, OT, half)
    return (
        lo[None, :, None], ig[None, :, None], oq[None], oo[None], ou[None], od[None],
        a0, a1, a2, a3, a4, bu, a5, tab,
    )


def solution(mesh):
    fits = mesh.shape["dp"] == 16 and mesh.shape["section"] == 2
    return jax.shard_map(
        team_local if fits else local,
        mesh=mesh,
        in_specs=(
            P(None, "dp", None, None),
            P(None, "dp", None, None),
            P(None, "dp"),
            P(),
            P("section", "dp", None),
            P("section", "dp", None),
            P("section", "dp", None),
            P("section", "dp", None),
            P("section", "dp"),
            P("section", "dp"),
            P("section", "dp"),
            P("section", "dp"),
            P("section", "dp"),
            P("section", "dp"),
            P("section", "dp"),
            P("section", "dp"),
        ),
        out_specs=(
            P("section", None, "dp", None, None),
            P("section", None, "dp", None, None),
            P("section", "dp", None),
            P("section", "dp", None),
            P("section", "dp", None),
            P("section", "dp", None),
            P("section", "dp"),
            P("section", "dp"),
            P("section", "dp"),
            P("section", "dp"),
            P("section", "dp"),
            P("section", "dp"),
            P("section", "dp"),
            P("section", "dp"),
        ),
        check_vma=False,
    )
```

```python
import jax
import jax.numpy as jnp
from jax import lax
from jax.experimental import pallas as pl
from jax.experimental.pallas import tpu as pltpu
from jax.sharding import PartitionSpec as P

H = 16
NB = 32


epsilon = 1e-05
highest = lax.Precision.HIGHEST


def passed_along(block, axis, distance):
    devices = range(lax.axis_size(axis))
    route = [(i - distance, i) for i in devices if i - distance in devices]
    return lax.ppermute(block, axis, route)


def norm_rows(values):
    centre = values - jnp.mean(values, axis=-1, keepdims=True)
    return centre * lax.rsqrt(jnp.mean(centre * centre, axis=-1, keepdims=True) + epsilon)


def norm_affine(values, gain, shift):
    return norm_rows(values) * gain + shift


def contract_rows(left, right):
    return lax.dot_general(
        left, right, (((0,), (0,)), ((), ())), preferred_element_type=jnp.float32
    )


def contract_cols(left, right):
    return lax.dot_general(
        left, right, (((1,), (1,)), ((), ())), preferred_element_type=jnp.float32
    )


def toeplitz_rows(values):
    heads, length = values.shape
    reverse = jnp.flip(values, axis=1)
    padded = jnp.concatenate([reverse, jnp.zeros_like(reverse)], axis=1)
    tiled = jnp.tile(padded, (1, length))[:, : length * (2 * length - 1)]
    return tiled.reshape(heads, length, 2 * length - 1)[:, :, length - 1 :]


def diagonal_sums(grid):
    heads, length, _ = grid.shape
    widened = jnp.concatenate([jnp.zeros((heads, length, length - 1), grid.dtype), grid], axis=2)
    flat = widened.reshape(heads, length * (2 * length - 1))
    flat = jnp.concatenate([flat, jnp.zeros((heads, length), grid.dtype)], axis=1)
    folded = jnp.sum(flat.reshape(heads, length, 2 * length), axis=1)
    return jnp.flip(folded[:, :length], axis=1)


def bucket_table(buckets):
    return (buckets[None, :] == jnp.arange(NB, dtype=jnp.int32)[:, None]).astype(jnp.float32)


def make_bias(table_flat, onehot):
    table = table_flat.astype(jnp.float32).reshape(NB, H)
    per_distance = jnp.dot(table.T, onehot, precision=highest)
    return toeplitz_rows(per_distance)


def weight_terms(factors):
    normed, d_qkv, mixed, d_attn, second, d_hidden, activated, d_branch = factors
    return (
        contract_rows(normed, d_qkv),
        contract_rows(mixed, d_attn),
        contract_rows(second, d_hidden),
        contract_rows(activated, d_branch),
    )


def forward_item(inputs, length, bias, weights):
    (
        w_qkv,
        w_out,
        w_up,
        w_down,
        gain_one,
        shift_one,
        gain_two,
        shift_two,
        bias_out,
        bias_up,
        bias_down,
    ) = weights
    rows, width = inputs.shape
    heads = bias.shape[0]
    head_dim = width // heads
    scale = head_dim ** (-0.5)
    position = jnp.arange(rows)
    visible = (position[None, :] <= position[:, None])[None] & (position[None, None, :] < length)
    valid = (position < length).astype(jnp.float32)[:, None]
    normed = norm_affine(
        inputs, gain_one.astype(jnp.float32), shift_one.astype(jnp.float32)
    ).astype(jnp.bfloat16)
    qkv = jnp.dot(normed, w_qkv, preferred_element_type=jnp.float32).astype(jnp.bfloat16)
    query = qkv[:, :width].reshape(rows, heads, head_dim)
    keys = qkv[:, width : 2 * width].reshape(rows, heads, head_dim)
    values = qkv[:, 2 * width :].reshape(rows, heads, head_dim)
    scores = (
        jnp.einsum("ihd,jhd->hij", query, keys, preferred_element_type=jnp.float32) * scale + bias
    )
    scores = jnp.where(visible, scores, -1000000000.0)
    raised = jnp.exp(scores - jnp.max(scores, axis=-1, keepdims=True))
    probs = raised / jnp.sum(raised, axis=-1, keepdims=True)
    probs_low = probs.astype(jnp.bfloat16)
    mixed = (
        jnp.einsum("hij,jhd->ihd", probs_low, values, preferred_element_type=jnp.float32)
        .reshape(rows, width)
        .astype(jnp.bfloat16)
    )
    middle = (
        inputs
        + jnp.dot(mixed, w_out, preferred_element_type=jnp.float32)
        + bias_out.astype(jnp.float32)
    )
    second = norm_affine(
        middle, gain_two.astype(jnp.float32), shift_two.astype(jnp.float32)
    ).astype(jnp.bfloat16)
    hidden = jnp.dot(second, w_up, preferred_element_type=jnp.float32) + bias_up.astype(jnp.float32)
    activated = jax.nn.gelu(hidden).astype(jnp.bfloat16)
    result = (
        middle
        + jnp.dot(activated, w_down, preferred_element_type=jnp.float32)
        + bias_down.astype(jnp.float32)
    ) * valid
    saved = (
        normed,
        query,
        keys,
        values,
        probs,
        probs_low,
        mixed,
        middle,
        second,
        hidden,
        activated,
        valid,
    )
    return (result, saved)


def backward_item(inputs, length, bias, weights, upstream, onehot):
    (
        w_qkv,
        w_out,
        w_up,
        w_down,
        gain_one,
        shift_one,
        gain_two,
        shift_two,
        bias_out,
        bias_up,
        bias_down,
    ) = weights
    _, saved = forward_item(inputs, length, bias, weights)
    (
        normed,
        query,
        keys,
        values,
        probs,
        probs_low,
        mixed,
        middle,
        second,
        hidden,
        activated,
        valid,
    ) = saved
    rows, width = inputs.shape
    heads = bias.shape[0]
    head_dim = width // heads
    scale = head_dim ** (-0.5)
    direct = upstream * valid
    d_branch = direct.astype(jnp.bfloat16)
    grad_bdown = jnp.sum(d_branch.astype(jnp.float32), axis=0)
    d_activated = contract_cols(d_branch, w_down)
    _, gelu_back = jax.vjp(jax.nn.gelu, hidden)
    d_hidden = gelu_back(d_activated)[0].astype(jnp.bfloat16)
    grad_bup = jnp.sum(d_hidden.astype(jnp.float32), axis=0)
    d_second = contract_cols(d_hidden, w_up)
    _, second_back = jax.vjp(
        norm_affine, middle, gain_two.astype(jnp.float32), shift_two.astype(jnp.float32)
    )
    d_middle, grad_gain_two, grad_shift_two = second_back(d_second)
    d_middle = d_middle + direct
    d_attn = d_middle.astype(jnp.bfloat16)
    grad_bout = jnp.sum(d_attn.astype(jnp.float32), axis=0)
    d_mixed = contract_cols(d_attn, w_out).astype(jnp.bfloat16).reshape(rows, heads, head_dim)
    grad_values = jnp.einsum("hij,ihd->jhd", probs_low, d_mixed, preferred_element_type=jnp.float32)
    d_probs = jnp.einsum("ihd,jhd->hij", d_mixed, values, preferred_element_type=jnp.float32)
    d_scores = (probs * (d_probs - jnp.sum(probs * d_probs, axis=-1, keepdims=True))).astype(
        jnp.bfloat16
    )
    grad_query = (
        jnp.einsum("hij,jhd->ihd", d_scores, keys, preferred_element_type=jnp.float32) * scale
    )
    grad_keys = (
        jnp.einsum("hij,ihd->jhd", d_scores, query, preferred_element_type=jnp.float32) * scale
    )
    d_qkv = jnp.concatenate(
        [
            grad_query.reshape(rows, width),
            grad_keys.reshape(rows, width),
            grad_values.reshape(rows, width),
        ],
        axis=1,
    ).astype(jnp.bfloat16)
    d_normed = contract_cols(d_qkv, w_qkv)
    _, first_back = jax.vjp(
        norm_affine, inputs, gain_one.astype(jnp.float32), shift_one.astype(jnp.float32)
    )
    d_inputs, grad_gain_one, grad_shift_one = first_back(d_normed)
    d_inputs = d_inputs + d_middle
    per_distance = diagonal_sums(d_scores.astype(jnp.float32))
    grad_table = jnp.dot(onehot, per_distance.T, precision=highest).reshape(-1)
    factors = (normed, d_qkv, mixed, d_attn, second, d_hidden, activated, d_branch)
    small = (
        grad_gain_one,
        grad_shift_one,
        grad_gain_two,
        grad_shift_two,
        grad_bout,
        grad_bup,
        grad_bdown,
        grad_table,
    )
    return (d_inputs, factors, small)


def local(
    audio_in,
    out_grad,
    item_len,
    rel_bucket,
    w_qkv,
    w_out,
    w_up,
    w_down,
    ln1_gain,
    ln1_bias,
    ln2_gain,
    ln2_bias,
    b_out,
    b_up,
    b_down,
    rel_table,
):
    section = lax.axis_index("section")
    micro = audio_in.shape[0]
    rows = audio_in.shape[2]
    width = audio_in.shape[3]
    qkv_part = w_qkv[0].astype(jnp.bfloat16)
    out_part = w_out[0].astype(jnp.bfloat16)
    up_part = w_up[0].astype(jnp.bfloat16)
    down_part = w_down[0].astype(jnp.bfloat16)
    gain_one_part = ln1_gain[0].astype(jnp.bfloat16)
    shift_one_part = ln1_bias[0].astype(jnp.bfloat16)
    gain_two_part = ln2_gain[0].astype(jnp.bfloat16)
    shift_two_part = ln2_bias[0].astype(jnp.bfloat16)
    bias_out_part = b_out[0].astype(jnp.bfloat16)
    bias_up_part = b_up[0].astype(jnp.bfloat16)
    bias_down_part = b_down[0].astype(jnp.bfloat16)
    table_part = rel_table[0].astype(jnp.bfloat16)
    parts = (
        qkv_part,
        out_part,
        up_part,
        down_part,
        gain_one_part,
        shift_one_part,
        gain_two_part,
        shift_two_part,
        bias_out_part,
        bias_up_part,
        bias_down_part,
        table_part,
    )
    gathered = (
        lax.all_gather(qkv_part, "dp", axis=0, tiled=True),
        lax.all_gather(out_part, "dp", axis=0, tiled=True),
        lax.all_gather(up_part, "dp", axis=0, tiled=True),
        lax.all_gather(down_part, "dp", axis=0, tiled=True),
        lax.all_gather(gain_one_part, "dp", axis=0, tiled=True),
        lax.all_gather(shift_one_part, "dp", axis=0, tiled=True),
        lax.all_gather(gain_two_part, "dp", axis=0, tiled=True),
        lax.all_gather(shift_two_part, "dp", axis=0, tiled=True),
        lax.all_gather(bias_out_part, "dp", axis=0, tiled=True),
        lax.all_gather(bias_up_part, "dp", axis=0, tiled=True),
        lax.all_gather(bias_down_part, "dp", axis=0, tiled=True),
        lax.all_gather(table_part, "dp", axis=0, tiled=True),
    )
    onehot = bucket_table(rel_bucket)
    weights = gathered[:11]
    bias = make_bias(gathered[11], onehot)
    lengths = item_len[:, 0]
    hidden_width = gathered[2].shape[1]

    def run_forward(layer_in, length):
        return forward_item(layer_in.astype(jnp.float32), length, bias, weights)[0]

    def skip_forward(layer_in, length):
        return jnp.zeros(layer_in.shape, jnp.float32)

    incoming = jnp.zeros((rows, width), jnp.bfloat16)
    produced = []
    taken = []
    for tick in range(micro + 1):
        slot = tick - section
        active = jnp.logical_and(slot >= 0, slot < micro)
        length = lengths[jnp.clip(slot, 0, micro - 1)]
        own = audio_in[min(tick, micro - 1), 0]
        layer_in = jnp.where(section == 0, own, incoming)
        layer_out = lax.cond(active, run_forward, skip_forward, layer_in, length).astype(
            jnp.bfloat16
        )
        produced.append(layer_out)
        taken.append(layer_in)
        if tick < micro:
            incoming = passed_along(layer_out, "section", 1)
    outputs = jnp.stack(
        [jnp.where(section == 0, produced[batch], produced[batch + 1]) for batch in range(micro)]
    )
    kept = jnp.stack(
        [jnp.where(section == 0, taken[batch], taken[batch + 1]) for batch in range(micro)]
    )
    regathered = (
        lax.all_gather(qkv_part, "dp", axis=0, tiled=True),
        lax.all_gather(out_part, "dp", axis=0, tiled=True),
        lax.all_gather(up_part, "dp", axis=0, tiled=True),
        lax.all_gather(down_part, "dp", axis=0, tiled=True),
        lax.all_gather(gain_one_part, "dp", axis=0, tiled=True),
        lax.all_gather(shift_one_part, "dp", axis=0, tiled=True),
        lax.all_gather(gain_two_part, "dp", axis=0, tiled=True),
        lax.all_gather(shift_two_part, "dp", axis=0, tiled=True),
        lax.all_gather(bias_out_part, "dp", axis=0, tiled=True),
        lax.all_gather(bias_up_part, "dp", axis=0, tiled=True),
        lax.all_gather(bias_down_part, "dp", axis=0, tiled=True),
        lax.all_gather(table_part, "dp", axis=0, tiled=True),
    )
    back_weights = regathered[:11]
    back_bias = make_bias(regathered[11], onehot)

    def run_backward(layer_in, length, upstream):
        return backward_item(
            layer_in.astype(jnp.float32), length, back_bias, back_weights, upstream, onehot
        )

    def skip_backward(layer_in, length, upstream):
        zero_rows = jnp.zeros((rows, width), jnp.bfloat16)
        zero_triple = jnp.zeros((rows, 3 * width), jnp.bfloat16)
        zero_hidden = jnp.zeros((rows, hidden_width), jnp.bfloat16)
        factors = (
            zero_rows,
            zero_triple,
            zero_rows,
            zero_rows,
            zero_rows,
            zero_hidden,
            zero_hidden,
            zero_rows,
        )
        small = tuple((jnp.zeros(piece.shape, jnp.float32) for piece in gathered[4:]))
        return (jnp.zeros(upstream.shape, jnp.float32), factors, small)

    small_totals = tuple((jnp.zeros(piece.shape, jnp.float32) for piece in gathered[4:]))
    shares = tuple((jnp.zeros(piece.shape, jnp.float32) for piece in parts))
    returned = jnp.zeros((rows, width), jnp.bfloat16)
    results = []
    sent_list = []
    factor_list = []
    for tick in range(micro + 1):
        slot = tick - 1 + section
        active = jnp.logical_and(slot >= 0, slot < micro)
        pick = jnp.clip(slot, 0, micro - 1)
        length = lengths[pick]
        layer_in = kept[pick]
        target = out_grad[min(tick, micro - 1), 0].astype(jnp.float32)
        upstream = jnp.where(section == 1, target, returned.astype(jnp.float32))
        d_inputs, factors, small = lax.cond(
            active, run_backward, skip_backward, layer_in, length, upstream
        )
        factor_list.append(factors)
        small_totals = tuple((total + term for total, term in zip(small_totals, small)))
        results.append(d_inputs)
        if tick < micro:
            sent = d_inputs.astype(jnp.bfloat16)
            sent_list.append(lax.optimization_barrier(sent))
            returned = passed_along(sent, "section", -1)
    stacked = tuple(
        (jnp.concatenate([entry[index] for entry in factor_list], axis=0) for index in range(8))
    )
    totals = weight_terms(stacked) + small_totals
    shares = (
        lax.psum_scatter(totals[0], "dp", scatter_dimension=0, tiled=True),
        lax.psum_scatter(totals[1], "dp", scatter_dimension=0, tiled=True),
        lax.psum_scatter(totals[2], "dp", scatter_dimension=0, tiled=True),
        lax.psum_scatter(totals[3], "dp", scatter_dimension=0, tiled=True),
        lax.psum_scatter(totals[4], "dp", scatter_dimension=0, tiled=True),
        lax.psum_scatter(totals[5], "dp", scatter_dimension=0, tiled=True),
        lax.psum_scatter(totals[6], "dp", scatter_dimension=0, tiled=True),
        lax.psum_scatter(totals[7], "dp", scatter_dimension=0, tiled=True),
        lax.psum_scatter(totals[8], "dp", scatter_dimension=0, tiled=True),
        lax.psum_scatter(totals[9], "dp", scatter_dimension=0, tiled=True),
        lax.psum_scatter(totals[10], "dp", scatter_dimension=0, tiled=True),
        lax.psum_scatter(totals[11], "dp", scatter_dimension=0, tiled=True),
    )
    input_grads = jnp.stack(
        [
            jnp.where(section == 0, results[batch + 1], sent_list[batch].astype(jnp.float32))
            for batch in range(micro)
        ]
    )
    grads_out = tuple((share[None] for share in shares))
    return (outputs[None, :, None], input_grads[None, :, None]) + grads_out


E5 = 1e-05
F32 = jnp.float32
BF = jnp.bfloat16
MESH = pl.DeviceIdType.MESH
GELU_K = 0.7978845608028654
HD = 64


class Place:
    def __init__(self):
        self.s = lax.axis_index("section")
        d = lax.axis_index("dp")
        self.x = d % 2
        self.y = (d // 2) % 2
        self.z = (d // 4) % 2
        self.h = d // 8
        self.t = self.x + 2 * self.z

    def device(self, s=None, x=None, y=None, z=None, h=None):
        s = self.s if s is None else s
        x = self.x if x is None else x
        y = self.y if y is None else y
        z = self.z if z is None else z
        h = self.h if h is None else h
        return (s, x + 2 * y + 4 * z + 8 * h)

    def sibling(self):
        return self.device(s=1 - self.s)

    def across_y(self):
        return self.device(y=1 - self.y)

    def across_h(self):
        return self.device(h=1 - self.h)

    def mate(self, k):
        return self.x + (k % 2) * (1 - 2 * self.x), self.z + (k // 2) * (1 - 2 * self.z)

    def team(self, k):
        px, pz = self.mate(k)
        return self.device(x=px, z=pz), px + 2 * pz


def remote(src, dst, send, recv, device):
    return pltpu.make_async_remote_copy(
        src_ref=src, dst_ref=dst, send_sem=send, recv_sem=recv, device_id=device, device_id_type=MESH
    )


def dot(a, b):
    return jnp.dot(a, b, preferred_element_type=F32)


def dot_nt(a, b):
    return lax.dot_general(a, b, (((1,), (1,)), ((), ())), preferred_element_type=F32)


def dot_tn(a, b):
    return lax.dot_general(a, b, (((0,), (0,)), ((), ())), preferred_element_type=F32)


def rows_norm(v):
    centre = v - jnp.mean(v, axis=-1, keepdims=True)
    scale = lax.rsqrt(jnp.mean(centre * centre, axis=-1, keepdims=True) + E5)
    return centre * scale, scale


def norm_back(cot, normed, scale, gain):
    inner = cot * gain
    return scale * (
        inner
        - jnp.mean(inner, axis=-1, keepdims=True)
        - normed * jnp.mean(inner * normed, axis=-1, keepdims=True)
    )


def column_sum(v):
    return jnp.sum(v, axis=0, keepdims=True)


def lanes_of(shape, axis=1):
    return lax.broadcasted_iota(jnp.int32, shape, axis)


def split_heads(block, count, size):
    lane = lanes_of(block.shape) // size
    return jnp.concatenate([jnp.where(lane == i, block, jnp.zeros_like(block)) for i in range(count)], axis=0)


def join_heads(block, count, size):
    rows = block.shape[0] // count
    lane = lanes_of((rows, block.shape[1])) // size
    total = jnp.where(lane == 0, block[:rows], 0.0)
    for i in range(1, count):
        total = jnp.where(lane == i, block[i * rows : (i + 1) * rows], total)
    return total


def turn(block, shift):
    width = block.shape[1]
    shift = shift % width
    return jnp.concatenate([block[:, width - shift :], block[:, : width - shift]], axis=1)


def skew(block, length, sign):
    row = lanes_of(block.shape, 0) % length
    for bit in range(7):
        block = jnp.where((row // 2**bit) % 2 == 1, turn(block, sign * 2**bit), block)
    return block


class Part:
    def __init__(self, index, pieces, **refs):
        self.index = index
        self.pieces = pieces
        self.chunks = 2 + pieces
        for name, ref in refs.items():
            setattr(self, name, ref)

    def strip(self, c, rows):
        step = rows // self.pieces
        return pl.ds((c - 2) * step, step)


def step_kernel(
    x_ref, og_ref, il_ref, rb_ref, wq_in, wo_in, wu_in, wd_in,
    v0_ref, v1_ref, v2_ref, v3_ref, v4_ref, v5_ref, bu_ref, rt_ref,
    lo, ig, OQ, OO, OU, OD, OT,
    SQ, SU, WQ, WO, WU, WD, XG, XIN, A, C, FA, MIX, QKV, PR, UF, HM, DZ, DAT, DU, DQ,
    XA, XC, XF, XM, XDZ, XDAT, XDU, XDQ, RB, SB, SY, RY, OWN, OWNY, DX, DH,
    GQ, GO, YQ, YO, YU, YD, ZSQ, ZSO, ZSU, ZSD, ZRQ, ZRO, ZRU, ZRD, TRQ, TRU,
    SPT, SPR, VEC, LEN, BIAS, PD, SGV, SBU, DS, MT, MR, M1, MN,
    ls, ss_a, rs_a, ss_wy, rs_wy, ss_wh, rs_wh, ss_ws, rs_ws, ss_p, rs_p,
    ss_g, rs_g, ss_r, rs_r, ss_x, rs_x, ss_o, rs_o,
    ss_gy, rs_gy, ss_gh, rs_gh, ss_gt, rs_gt, ss_m, rs_m,
):
    p = Place()
    s, x, y, z, h, t = p.s, p.x, p.y, p.z, p.h, p.t
    sib, ypeer, hpeer = p.sibling(), p.across_y(), p.across_h()
    rows, width = x_ref.shape[1], x_ref.shape[2]
    heads = 4
    wide = heads * HD
    ff = FA.shape[3]
    part_rows = WO.shape[2]
    block = WD.shape[2]

    def only(core, what):
        @pl.when(s == core)
        def _():
            what()

    half = rows // 2
    upper, lower = pl.ds(0, half), pl.ds(half, half)
    x_dev, x_slot = p.team(1)
    z_dev, z_slot = p.team(2)
    d_slot = p.team(3)[1]

    def hop(ref, c, n, slot, span, device):
        view = ref.at[slot, span]
        return remote(view, view, ss_g.at[c, n], rs_g.at[c, n], device)

    def gather_sends(ref, c):
        return (
            hop(ref, c, 2, t, upper, z_dev), hop(ref, c, 0, t, upper, x_dev),
            hop(ref, c, 3, t, lower, z_dev), hop(ref, c, 1, t, lower, x_dev),
        )

    def relays(ref, c):
        return hop(ref, c, 4, z_slot, upper, x_dev), hop(ref, c, 5, z_slot, lower, x_dev)

    def gather_start(ref, c):
        for cp in gather_sends(ref, c):
            cp.start()

    def gather_relay(ref, c):
        onward = relays(ref, c)
        hop(ref, c, 2, z_slot, upper, z_dev).wait_recv()
        onward[0].start()
        hop(ref, c, 3, z_slot, lower, z_dev).wait_recv()
        onward[1].start()

    def gather_take(ref, c, k):
        if k == 1:
            hop(ref, c, 0, x_slot, upper, x_dev).wait_recv()
            hop(ref, c, 1, x_slot, lower, x_dev).wait_recv()
        if k == 3:
            hop(ref, c, 4, d_slot, upper, x_dev).wait_recv()
            hop(ref, c, 5, d_slot, lower, x_dev).wait_recv()

    def gather_end(ref, c):
        for cp in gather_sends(ref, c) + relays(ref, c):
            cp.wait_send()

    def reduce_copy(c, k, side=False):
        out, land = (SY, RY) if side else (SB, RB)
        return remote(out.at[k], land.at[k], ss_r.at[c, k], rs_r.at[c, k], p.team(k)[0])

    def reduce_put(c, k, value, side=False):
        @pl.when(k == 0)
        def _():
            (OWNY if side else OWN)[...] = value

        @pl.when(k > 0)
        def _():
            (SY if side else SB)[k] = value.astype(BF)
            if not side:
                reduce_copy(c, k).start()

    def reduce_end(c, side=False):
        total = (OWNY if side else OWN)[...]
        for k in (1, 2, 3):
            reduce_copy(c, k, side).wait()
            total = total + (RY if side else RB)[k].astype(F32)
        return total

    def each_item(gathers, body, aside, relay=True):
        def step(n, carry):
            if relay:

                @pl.when(n == 1)
                def _():
                    gather_relay(*gathers[0])

            for m, mate in ((2, 1), (3, 3)):

                @pl.when(n == m)
                def _(mate=mate):
                    for ref, c in gathers:
                        gather_take(ref, c, mate)

            k = 2 * (n % 2) + n // 2
            body(k, p.team(k)[1])
            aside(n)
            return carry

        lax.fori_loop(0, 4, step, 0)
        for ref, c in gathers:
            gather_end(ref, c)

    def at_step(k, here, n, what):
        @pl.when(jnp.logical_and(here, k == n))
        def _():
            what()

    first = Part(0, 1, W=WQ, V=WO, S=SQ, G=GQ, R=GO, Y=YQ, YR=YO, ZS=ZSQ, ZSR=ZSO, ZR=ZRQ, ZRR=ZRO,
                 TS=SQ, TR=TRQ, O=OQ, OR=OO)
    second = Part(1, 2, W=WU, V=WD, S=SU, G=WU.at[1], R=WD.at[1], Y=YU, YR=YD, ZS=ZSU, ZSR=ZSD, ZR=ZRU, ZRR=ZRD,
                  TS=SU, TR=TRU, O=OU, OR=OD)

    loads = [
        pltpu.make_async_copy(wq_in.at[:, pl.ds(width * i, width)], UF.at[pl.ds(576 + 64 * i, 64)], ls.at[i])
        for i in range(3)
    ]
    loads.append(pltpu.make_async_copy(wo_in, UF.at[pl.ds(0, 64)], ls.at[3]))
    loads += [
        pltpu.make_async_copy(wu_in.at[:, pl.ds(width * i, width)], UF.at[pl.ds(320 + 64 * i, 64)], ls.at[4 + i])
        for i in range(4)
    ]
    loads.append(pltpu.make_async_copy(wd_in, UF.at[pl.ds(64, 256)], ls.at[8]))
    loads.append(pltpu.make_async_copy(x_ref.at[s], XG.at[t], ls.at[9]))
    loads.append(pltpu.make_async_copy(og_ref.at[s], DZ.at[1, t], ls.at[10]))
    for cp in loads:
        cp.start()

    bell = pltpu.get_barrier_semaphore()
    around = [(a, b, e) for a in range(2) for b in range(2) for e in range(2)][1:]

    def station(a, b, e):
        return p.device(s=s + a * (1 - 2 * s), y=y + b * (1 - 2 * y), h=h + e * (1 - 2 * h))

    everyone = [p.team(k)[0] for k in (1, 2, 3)] + [station(*o) for o in around]
    for peer in everyone:
        pl.semaphore_signal(bell, inc=1, device_id=peer, device_id_type=MESH)

    for cp in loads[:4]:
        cp.wait()
    for i in range(3):
        for hh in range(2):
            for zz in range(2):
                base = (2 * zz + 4 * hh) * 128
                even = UF[576 + 64 * i : 640 + 64 * i, base : base + 128].astype(BF)
                odd = UF[576 + 64 * i : 640 + 64 * i, base + 128 : base + 256].astype(BF)
                at = (2 * i + hh) * 128
                SQ[2 * zz, :, at : at + 128] = jnp.concatenate([even[:, :HD], odd[:, :HD]], axis=1)
                SQ[2 * zz + 1, :, at : at + 128] = jnp.concatenate([even[:, HD:], odd[:, HD:]], axis=1)
    WQ[s, h, z, y, x] = SQ[t]
    q = 2 * h + y
    WO[s, q] = UF[0:64, :].astype(BF)
    pl.semaphore_wait(bell, len(everyone))

    def w_team(part, k):
        device, slot = p.team(k)
        return remote(
            part.S.at[slot], part.W.at[s, h, z, y, x], ss_a.at[part.index, k], rs_a.at[part.index, k], device
        )

    def w_view(part, c, hh, yy):
        if c < 2:
            return part.W.at[s, hh, c, yy]
        return part.V.at[s, 2 * hh + yy, part.strip(c, part.V.shape[2])]

    def w_y(part, c, n):
        view = w_view(part, c, h + n * (1 - 2 * h), y)
        return remote(view, view, ss_wy.at[part.index, n, c], rs_wy.at[part.index, n, c], ypeer)

    def w_h(part, c):
        view = w_view(part, c, h, y)
        return remote(view, view, ss_wh.at[part.index, c], rs_wh.at[part.index, c], hpeer)

    def w_s(part, c, hh, yy):
        view = w_view(part, c, hh, yy)
        n = 2 * hh + yy
        return remote(view, view, ss_ws.at[part.index, n, c], rs_ws.at[part.index, n, c], sib)

    order = ((first, 2), (first, 0), (first, 1), (second, 0), (second, 1), (second, 2), (second, 3))

    def w_share(j):
        part, c = order[j]
        if j in (1, 3):
            for k in (1, 2, 3):
                w_team(part, k).wait_recv()
        w_h(part, c).start()
        w_y(part, c, 0).start()
        w_s(part, c, h, y).start()

    def w_pass(j):
        part, c = order[j]
        w_h(part, c).wait_recv()
        w_y(part, c, 1).start()
        w_s(part, c, 1 - h, y).start()
        if j + 2 < len(order):
            w_share(j + 2)

    def w_near(part):
        for c in range(part.chunks):
            w_y(part, c, 0).wait_recv()
            w_s(part, c, h, 1 - y).start()

    def w_far(part):
        for c in range(part.chunks):
            w_y(part, c, 1).wait_recv()
            w_s(part, c, 1 - h, 1 - y).start()

    def w_other(part):
        for c in range(part.chunks):
            for n in range(4):
                w_s(part, c, n // 2, n % 2).wait_recv()

    for k in (1, 2, 3):
        w_team(first, k).start()
    loads[9].wait()

    @pl.when(s == 0)
    def _():
        w_share(0)

    for cp in loads[4:9]:
        cp.wait()
    for hh in range(2):
        for zz in range(2):
            for yy in range(2):
                for xx in range(2):
                    at = (2 * hh + yy) * block
                    low = 320 + 64 * (zz + 2 * hh)
                    col = (xx + 2 * yy) * block
                    SU[xx + 2 * zz, :, at : at + block] = UF[low : low + 64, col : col + block].astype(BF)
    WU[s, h, z, y, x] = SU[t]
    WD[s, q] = UF[64 : 64 + block, :].astype(BF)

    position = lanes_of((rows, 1), 0).astype(F32)
    count = jnp.where(s == 0, il_ref[:, 0:1], il_ref[:, 1:2]).astype(F32)
    valid = (position < count).astype(F32)
    loads[10].wait()
    DZ[1, t] = (valid * DZ[1, t].astype(F32)).astype(BF)

    lane = lanes_of((1, 128))
    zero = jnp.zeros((1, 128), F32)
    pair = [jnp.concatenate([v[...], v[...]], axis=1) for v in (v0_ref, v1_ref, v2_ref, v3_ref, v4_ref, v5_ref)]
    lines = [jnp.where(lane // HD == x, v, zero) for v in pair]
    for xx in range(2):
        for i in range(2):
            lines.append(jnp.where(x == xx, bu_ref[:, 128 * i : 128 * i + 128], zero))
    table = jnp.concatenate([rt_ref[...], jnp.zeros((1, 96), F32)], axis=1)
    counts = jnp.where(lane == 0, il_ref[:, 0:1].astype(F32), jnp.where(lane == 1, il_ref[:, 1:2].astype(F32), zero))
    for piece in (table, counts):
        for xx in range(2):
            lines.append(jnp.where(x == xx, piece, zero))
    for i in range(2):
        lines.append(zero)
    for i in range(16):
        SPR[t, h, y, s, i : i + 1, :] = lines[i].astype(BF).astype(F32)

    def near_copy(n):
        view = SPR.at[t, h, y, s]
        return remote(view, view, ss_p.at[n], rs_p.at[n], station(*around[n]))

    def team_copy(k):
        view = SPR.at[t]
        return remote(view, view, ss_p.at[6 + k], rs_p.at[6 + k], p.team(k)[0])

    for n in range(7):
        near_copy(n).start()
    only(0, lambda: w_share(1))
    gather_start(XG, 0)
    for n in range(7):
        near_copy(n).wait()
    for k in (1, 2, 3):
        team_copy(k).start()
    for k in (1, 2, 3):
        w_team(second, k).start()
    only(0, lambda: w_pass(0))
    gather_relay(XG, 0)
    for k in (1, 2, 3):
        team_copy(k).wait()
    for hh in range(2):
        for zz in range(2):
            for yy in range(2):
                for i in range(2):
                    SPT[hh, zz, yy, i] = SPR[2 * zz, hh, yy, i] + SPR[2 * zz + 1, hh, yy, i]
    gather_start(DZ.at[1], 4)
    only(0, lambda: (w_pass(1), w_pass(2)))

    for hh in range(2):
        for zz in range(2):
            for yy in range(2):
                at = (yy + 2 * zz + 4 * hh) * 128
                for i in range(2):
                    VEC[i, 0:6, at : at + 128] = SPT[hh, zz, yy, i, 0:6, :]
    for i in range(2):
        for hh in range(2):
            for yy in range(2):
                tile = SPT[hh, z, yy, i]
                for r in range(2):
                    at = (2 * hh + yy) * block + 128 * r
                    VEC[i, 6:7, at : at + 128] = jnp.where(x == 0, tile[6 + r : 7 + r], tile[8 + r : 9 + r])
    for zz in range(2):
        tile = SPT[h, zz, y, 0]
        for xx in range(2):
            tokens = jnp.sum(jnp.where(lane == s, tile[12 + xx : 13 + xx], 0.0), axis=1, keepdims=True)
            LEN[xx + 2 * zz] = jnp.broadcast_to(tokens, (8, 128))

    mark = jnp.concatenate([rb_ref[...], jnp.full((1, 128 - rows), 2 * NB, jnp.int32)], axis=1).astype(BF)
    mark = jnp.broadcast_to(mark, (8, 128))
    flip = ((lanes_of((128, 128), 0) + lanes_of((128, 128))) % 128 == 0).astype(F32).astype(BF)
    mark = dot(mark, flip)[0:1]
    onehot = (lanes_of((NB, 128), 0).astype(F32) == mark).astype(F32)
    for i in range(2):
        lines = []
        for hh in range(2):
            for zz in range(2):
                for yy in range(2):
                    tile = SPT[hh, zz, yy, i]
                    for xx in range(2):
                        for b in range(2):
                            lines.append(tile[10 + xx : 11 + xx, 16 * b : 16 * b + 16])
        by_bucket = jnp.concatenate([jnp.concatenate(lines, axis=0), jnp.zeros((NB, 112), F32)], axis=1)
        PD[...] = dot_tn(by_bucket.astype(BF), onehot.astype(BF))
        stack = []
        for hh in range(2):
            for yy in range(2):
                line = PD[pl.ds(x + 2 * yy + 4 * z + 8 * hh, 1), :]
                stack.append(jnp.broadcast_to(line, (rows, 128)))
        grid = skew(jnp.concatenate(stack, axis=0), rows, 1)[:, :rows]
        causal = lanes_of(grid.shape) <= lanes_of(grid.shape, 0) % rows
        BIAS[i] = jnp.where(causal, grid, -1000000000.0)
    gather_relay(DZ.at[1], 4)

    pairs = ((A, XA), (MIX, XM), (C, XC), (FA, XF), (DZ, XDZ), (DAT, XDAT), (DU, XDU), (DQ, XDQ))

    def share_copy(i, layer, slot):
        return remote(pairs[i][0].at[layer, slot], pairs[i][1].at[slot], ss_x.at[i, slot], rs_x.at[i, slot], sib)

    def share_item(k, layer, which):
        @pl.when(s != layer)
        def _():
            for i in which:
                share_copy(i, layer, p.team(k)[1]).start()

    def row(layer, index):
        return VEC[layer, index : index + 1, :]

    def w_qkv(layer):
        return WQ[layer].reshape(width, 3 * wide)

    def w_up(layer):
        return WU[layer].reshape(width, ff)

    def w_out(layer):
        return WO[layer].reshape(wide, width)

    def w_down(layer):
        return WD[layer].reshape(ff, width)

    def u_rows(layer, i):
        return pl.ds(pl.multiple_of((layer * 4 + i) * rows, 8), rows)

    def g_own(part, c, hh, yy):
        if c < 2:
            return part.G.at[hh, c, yy]
        return part.R.at[2 * hh + yy, part.strip(c, part.R.shape[1])]

    def g_land(part, c, n):
        if c < 2:
            return part.Y.at[n, c]
        return part.YR.at[n, part.strip(c, part.R.shape[1])]

    def g_half(n):
        return (1 - h) + n * (2 * h - 1)

    def g_big(part, c, n):
        return remote(
            part.G.at[g_half(n), c, 1 - y], part.Y.at[n, c],
            ss_gy.at[part.index, n, c], rs_gy.at[part.index, n, c], ypeer,
        )

    def g_y(part, c, n):
        return remote(
            g_own(part, c, g_half(n), 1 - y), g_land(part, c, n),
            ss_gy.at[part.index, n, c], rs_gy.at[part.index, n, c], ypeer,
        )

    def g_z(part, c, out):
        if c < 2:
            return (part.ZS if out else part.ZR).at[c]
        return (part.ZSR if out else part.ZRR).at[part.strip(c, part.R.shape[1])]

    def g_h(part, c):
        return remote(
            g_z(part, c, True), g_z(part, c, False), ss_gh.at[part.index, c], rs_gh.at[part.index, c], hpeer
        )

    def g_t(part, k):
        return remote(
            part.TS.at[k], part.TR.at[k], ss_gt.at[part.index, k], rs_gt.at[part.index, k], p.team(k)[0]
        )

    def flat(ref, span):
        value = ref[:, :, span]
        return value.reshape(value.shape[0] * value.shape[1], value.shape[2])

    def product(left, right, span):
        every = pl.ds(0, right[0].shape[2])
        return dot_tn(flat(left[0], span), flat(right[0], every)) + dot_tn(
            flat(left[1], span), flat(right[1], every)
        )

    def g_make(part, n):
        if part is first:
            need = (0, 1, 5, 7)
            big_l, big_r = (A.at[s], XA), (DQ.at[s], XDQ)
            small_l, small_r = (MIX.at[s], XM), (DAT.at[s], XDAT)
            small_span = HD
        else:
            need = (2, 3, 4, 6)
            big_l, big_r = (C.at[s], XC), (DU.at[s], XDU)
            small_l, small_r = (FA.at[s], XF), (DZ.at[s], XDZ)
            small_span = block
        if n == 0:
            for i in need:
                for slot in range(4):
                    share_copy(i, s, slot).wait_recv()
        hh = g_half(n)
        if part is first:
            if n == 0:
                value = product(small_l, small_r, pl.ds(0, wide)).astype(BF)
                for i in range(4):
                    part.R[i] = value[i * small_span : (i + 1) * small_span]
            if n == 0:
                g_y(part, 2, n).start()

        def tile(zz, carry):
            span = pl.ds(pl.multiple_of((2 * hh + zz) * 256, 256), 256)
            value = product(big_l, big_r, span).astype(BF)
            part.G[hh, zz] = value.reshape(2, 2, part_rows, value.shape[1])
            if n == 0:
                g_big(part, zz, n).start()
            return carry

        lax.fori_loop(0, 2, tile, 0)
        if part is second:

            def strip(m, carry):
                yy = (1 - y) + m * (2 * y - 1)
                span = pl.ds(pl.multiple_of((2 * hh + yy) * 256, 256), 256)
                part.R[2 * hh + yy] = product(small_l, small_r, span).astype(BF)

                if n == 0:

                    @pl.when(m == 0)
                    def _():
                        for c in range(2, part.chunks):
                            g_y(part, c, n).start()

                return carry

            lax.fori_loop(0, 2, strip, 0)

    def g_fold(part, c):
        g_y(part, c, 0).wait_recv()
        g_z(part, c, True)[...] = (
            g_own(part, c, 1 - h, y)[...].astype(F32) + g_land(part, c, 0)[...].astype(F32)
        ).astype(BF)
        g_h(part, c).start()

    def g_later(part):
        for c in range(part.chunks):
            g_y(part, c, 1).start()

    def g_total(part):
        for c in range(part.chunks):
            g_y(part, c, 1).wait_recv()
            g_h(part, c).wait_recv()

        def total(xx, zz):
            return (
                part.G[h, zz, y, xx].astype(F32) + part.Y[1, zz, xx].astype(F32) + part.ZR[zz, xx].astype(F32)
            )

        for k in (1, 2, 3):
            part.TS[k] = total(*p.mate(k)).astype(BF)
            g_t(part, k).start()
        part.O[t] = total(x, z)
        part.OR[...] = part.R[q].astype(F32) + part.YR[1].astype(F32) + part.ZRR[...].astype(F32)

    def g_end(part):
        for k in (1, 2, 3):
            g_t(part, k).wait_recv()
            part.O[p.team(k)[1]] = part.TR[k].astype(F32)

    XIN[0] = XG[t]
    DS[...] = jnp.zeros_like(DS)
    SBU[...] = jnp.zeros_like(SBU)
    SGV[...] = jnp.zeros_like(SGV)

    def scaled(value, layer, at):
        return (rows_norm(value)[0] * row(layer, at) + row(layer, at + 1)).astype(BF)

    def attention(layer):
        if layer == 1:
            A[layer, t] = scaled(XIN[layer].astype(F32), layer, 0)
            gather_start(A.at[layer], 2)
        if layer == 0:
            only(0, lambda: w_near(first))
        only(layer, lambda: w_far(first))
        only(1 - layer, lambda: w_other(first))

        def attend(k, i):
            if layer == 0:
                A[layer, i] = scaled(XG[i].astype(F32), layer, 0)
            qkv = dot(A[layer, i], w_qkv(layer)).astype(BF)
            QKV[layer, i] = qkv
            stack = split_heads(qkv[:, :wide], heads, HD)
            scores = dot_nt(stack, qkv[:, wide : 2 * wide]) * (HD ** (-0.5)) + BIAS[layer]
            column = lanes_of(scores.shape).astype(F32)
            scores = jnp.where(column < LEN[i][0:1, 0:1], scores, -1000000000.0)
            raised = jnp.exp(scores - jnp.max(scores, axis=-1, keepdims=True))
            probs = raised / jnp.sum(raised, axis=-1, keepdims=True)
            PR[layer, i] = probs
            mixed = join_heads(dot(probs.astype(BF), qkv[:, 2 * wide :]), heads, HD).astype(BF)
            MIX[layer, i] = mixed
            reduce_put(2 * layer, k, dot(mixed, w_out(layer)))

        def pass_on(k):
            if layer == 0:
                for n in range(4):
                    at_step(k, s == 0, n, lambda n=n: w_pass(3 + n))
                at_step(k, s == 0, 2, lambda: w_near(second))
                at_step(k, s == 1, 2, lambda: (w_share(0), w_share(1)))
                at_step(k, s == 1, 3, lambda: w_pass(0))
            else:
                at_step(k, s == 1, 0, lambda: w_pass(6))
                at_step(k, s == 1, 1, lambda: w_near(second))
            share_item(2 * (k % 2) + k // 2, layer, (0, 1))

        each_item(((XG, 0),) if layer == 0 else ((A.at[layer], 2),), attend, pass_on, relay=layer == 1)
        hmid = XIN[layer].astype(F32) + reduce_end(2 * layer) + row(layer, 4)
        HM[layer] = hmid
        C[layer, t] = scaled(hmid, layer, 2)
        gather_start(C.at[layer], 2 * layer + 1)

    def hidden_back(layer, i, u, th):
        square = u * u
        slope = 0.5 * (1.0 + th) + (0.5 * GELU_K) * u * (1.0 - th * th) * (1.0 + 0.134145 * square)
        du = (dot_nt(DZ[layer, i], w_down(layer)) * slope).astype(BF)
        DU[layer, i] = du
        SBU[layer] += column_sum(du.astype(F32))
        return dot_nt(du, w_up(layer))

    def feed_forward(layer):
        only(layer, lambda: w_far(second))
        only(1 - layer, lambda: w_other(second))
        if layer == 0:
            only(1, lambda: w_pass(1))

        def feed(k, i):
            u = dot(C[layer, i], w_up(layer)) + row(layer, 6)
            th = jnp.tanh(GELU_K * (u + 0.044715 * (u * u * u)))
            if layer == 0:
                UF[u_rows(layer, i), :] = u
            else:
                reduce_put(4, k, hidden_back(layer, i, u, th))
            f = (0.5 * u * (1.0 + th)).astype(BF)
            FA[layer, i] = f
            reduce_put(2 * layer + 1, k, dot(f, w_down(layer)), side=layer == 1)

        def prepare(k):
            if layer == 0:
                for n in range(4):
                    at_step(k, s == 1, n, lambda n=n: w_pass(2 + n))
                at_step(k, s == 1, 2, lambda: w_near(first))
            share_item(2 * (k % 2) + k // 2, layer, (2, 3) if layer == 0 else (2, 3, 4, 6))

        gathers = ((C.at[layer], 2 * layer + 1),)
        if layer == 1:
            gathers += ((DZ.at[layer], 4),)
        each_item(gathers, feed, prepare)

    def layer_result(layer):
        return (valid * (HM[layer] + reduce_end(2 * layer + 1, side=layer == 1) + row(layer, 5))).astype(BF)

    def give_result(layer):
        @pl.when(s == layer)
        def _():
            lo[s] = XIN[layer + 1]

        @pl.when(s != layer)
        def _():
            remote(XIN.at[layer + 1], lo.at[s], ss_o.at[0], rs_o.at[0], sib).start()

    def feed_back(layer):
        def feed(k, i):
            u = UF[u_rows(layer, i), :]
            th = jnp.tanh(GELU_K * (u + 0.044715 * (u * u * u)))
            reduce_put(6, k, hidden_back(layer, i, u, th))

        def fold_first(k):
            for n in range(2):
                at_step(k, s == 1, n, lambda n=n: g_fold(first, n))
            at_step(k, s == 1, 1, lambda: g_later(first))
            share_item(2 * (k % 2) + k // 2, layer, (4, 6))

        each_item(((DZ.at[layer], 6),), feed, fold_first)

    def middle_back(layer):
        dc = reduce_end(6 - 2 * layer)
        normed, scale = rows_norm(HM[layer])
        SGV[layer, 2:3, :] = column_sum(dc * normed)
        SGV[layer, 3:4, :] = column_sum(dc)
        dh = DZ[layer, t].astype(F32) + norm_back(dc, normed, scale, row(layer, 2))
        DH[...] = dh
        dattn = dh.astype(BF)
        DAT[layer, t] = dattn
        gather_start(DAT.at[layer], 7 - 2 * layer)
        SGV[layer, 4:5, :] = column_sum(dattn.astype(F32))
        only(layer, lambda: (g_make(second, 1), g_fold(second, 0), g_fold(second, 1)))

    def attention_back(layer):
        def attend(k, i):
            dmixed = dot_nt(DAT[layer, i], w_out(layer)).astype(BF)
            qkv = QKV[layer, i]
            probs = PR[layer, i]
            stack = split_heads(dmixed, heads, HD)
            dprobs = dot_nt(stack, qkv[:, 2 * wide :])
            dscores = (probs * (dprobs - jnp.sum(probs * dprobs, axis=-1, keepdims=True))).astype(BF)
            DS[layer] += dscores.astype(F32)
            dq = join_heads(dot(dscores, qkv[:, wide : 2 * wide]), heads, HD) * (HD ** (-0.5))
            dk = dot_tn(dscores, split_heads(qkv[:, :wide], heads, HD)) * (HD ** (-0.5))
            dv = dot_tn(probs.astype(BF), stack)
            DQ[layer, i, :, :wide] = dq.astype(BF)
            DQ[layer, i, :, wide : 2 * wide] = dk.astype(BF)
            DQ[layer, i, :, 2 * wide :] = dv.astype(BF)
            reduce_put(7 - 2 * layer, k, dot_nt(DQ[layer, i], w_qkv(layer)))

        def fold_second(k):
            for n in range(2):
                at_step(k, s == layer, n, lambda n=n: g_fold(second, n + 2))
            at_step(k, s == layer, 1, lambda: g_later(second))
            share_item(2 * (k % 2) + k // 2, layer, (5, 7))

        each_item(((DAT.at[layer], 7 - 2 * layer),), attend, fold_second)

    def inputs_back(layer):
        da = reduce_end(7 - 2 * layer)
        normed, scale = rows_norm(XIN[layer].astype(F32))
        dx = DH[...] + norm_back(da, normed, scale, row(layer, 0))
        low = dx.astype(BF)
        if layer == 1:
            dyv = valid * low.astype(F32)
            DZ[0, t] = dyv.astype(BF)
            gather_start(DZ.at[0], 6)
            SGV[0, 5:6, :] = column_sum(dyv)
        SGV[layer, 0:1, :] = column_sum(da * normed)
        SGV[layer, 1:2, :] = column_sum(da)
        result = low.astype(F32) if layer == 1 else dx

        @pl.when(s == layer)
        def _():
            ig[s] = result

        @pl.when(s != layer)
        def _():
            DX[...] = result
            remote(DX, ig.at[s], ss_o.at[1], rs_o.at[1], sib).start()

    attention(0)
    feed_forward(0)
    XIN[1] = layer_result(0)
    attention(1)
    give_result(0)
    feed_forward(1)
    for part in (first, second):
        for k in (1, 2, 3):
            w_team(part, k).wait_send()
        for c in range(part.chunks):
            w_h(part, c).wait_send()
            for n in range(2):
                w_y(part, c, n).wait_send()
            for n in range(4):
                w_s(part, c, n // 2, n % 2).wait_send()
    only(1, lambda: g_make(second, 0))
    SGV[1, 5:6, :] = column_sum(DZ[1, t].astype(F32))
    middle_back(1)
    attention_back(1)
    only(1, lambda: g_make(first, 0))
    inputs_back(1)
    only(1, lambda: (g_make(first, 1), g_fold(first, 2)))
    feed_back(0)
    only(0, lambda: g_make(second, 0))
    only(1, lambda: g_total(second))
    middle_back(0)
    attention_back(0)
    for k in (1, 2, 3):
        reduce_copy(3, k, True).start()
    only(0, lambda: (g_make(first, 0), g_fold(first, 2), g_make(first, 1)))
    only(0, lambda: (g_fold(first, 0), g_fold(first, 1), g_later(first)))
    inputs_back(0)

    spread = []
    for i in range(2):
        turned = skew(jnp.concatenate([DS[i], jnp.zeros((heads * rows, 128 - rows), F32)], axis=1), rows, -1)
        table = jnp.zeros((128, 128), F32)
        for hh in range(2):
            for yy in range(2):
                n = 2 * hh + yy
                line = column_sum(turned[n * rows : (n + 1) * rows])
                head = x + 2 * yy + 4 * z + 8 * hh
                table = jnp.where(lanes_of((128, 128), 0) == head, line, table)
        spread.append(
            lax.dot_general(
                onehot, table, (((1,), (1,)), ((), ())), precision=highest, preferred_element_type=F32
            )
        )
    for hh in range(2):
        for zz in range(2):
            for yy in range(2):
                j = yy + 2 * zz + 4 * hh
                for i in range(2):
                    MT[hh, zz, yy, i, 0:6, :] = SGV[i, 0:6, 128 * j : 128 * j + 128]
                    for xx in range(2):
                        for r in range(2):
                            at = (2 * hh + yy) * block + 128 * r
                            n = 6 + 2 * xx + r
                            MT[hh, zz, yy, i, n : n + 1, :] = jnp.where(
                                jnp.logical_and(z == zz, x == xx), SBU[i, :, at : at + 128], zero
                            )
                    MT[hh, zz, yy, i, 10:12, :] = jnp.zeros((2, 128), F32)
                    MT[hh, zz, yy, i, 12:16, :] = spread[i][4 * j : 4 * j + 4]

    def team_merge(k):
        return remote(MT.at[:, p.mate(k)[1]], MR.at[k], ss_m.at[6 + k], rs_m.at[6 + k], p.team(k)[0])

    def near_merge(n):
        a, b, e = around[n]
        there = (h + e * (1 - 2 * h), y + b * (1 - 2 * y), s + a * (1 - 2 * s))
        return remote(M1.at[there], MN.at[n], ss_m.at[n], rs_m.at[n], station(a, b, e))

    for k in (1, 2, 3):
        team_merge(k).start()
    only(0, lambda: g_total(second))
    for k in (1, 2, 3):
        team_merge(k).wait()
    for hh in range(2):
        M1[hh] = MT[hh, z] + MR[1, hh] + MR[2, hh] + MR[3, hh]
    for n in range(7):
        near_merge(n).start()
    XIN[2] = layer_result(1)
    give_result(1)
    g_total(first)
    g_end(second)
    for n in range(7):
        near_merge(n).wait()
    tile = M1[h, y, s]
    for n in range(7):
        tile = tile + MN[n]
    OT[...] = tile
    g_end(first)

    for part in (first, second):
        for k in (1, 2, 3):
            g_t(part, k).wait_send()
        for c in range(part.chunks):
            g_h(part, c).wait_send()
            for n in range(2):
                g_y(part, c, n).wait_send()
    for i in range(8):
        for slot in range(4):
            share_copy(i, 1 - s, slot).wait_send()
    remote(XIN.at[1], lo.at[1 - s], ss_o.at[0], rs_o.at[0], sib).wait()
    remote(DX, ig.at[1 - s], ss_o.at[1], rs_o.at[1], sib).wait()


def finish_kernel(
    lo_in, ig_in, oq_in, oo_in, ou_in, od_in, ot_in,
    lo, ig, oq, oo, ou, od, a0, a1, a2, a3, a4, bu, a5, tab, OQ, OU, OT, sem,
):
    moves = ((oq_in, OQ), (ou_in, OU), (ot_in, OT), (lo_in, lo), (ig_in, ig), (oo_in, oo), (od_in, od))
    moves = [pltpu.make_async_copy(a, b, sem.at[i]) for i, (a, b) in enumerate(moves)]
    for cp in moves:
        cp.start()
    for cp in moves[:3]:
        cp.wait()
    block = od.shape[0]
    for hh in range(2):
        for zz in range(2):
            for yy in range(2):
                n = 2 * hh + yy
                d = 2 * yy + 4 * zz + 8 * hh
                for i in range(3):
                    at = i * 4 * HD + n * HD
                    to = i * 16 * HD + d * HD
                    oq[:, to : to + 2 * HD] = jnp.concatenate(
                        [OQ[2 * zz, :, at : at + HD], OQ[2 * zz + 1, :, at : at + HD]], axis=1
                    )
                for xx in range(2):
                    ou[:, (d + xx) * block : (d + xx + 1) * block] = OU[xx + 2 * zz, :, n * block : (n + 1) * block]
    x = lax.axis_index("dp") % 2
    for i, ref in enumerate((a0, a1, a2, a3, a4, a5)):
        ref[...] = jnp.where(x == 0, OT[i : i + 1, :HD], OT[i : i + 1, HD:])
    for r in range(2):
        bu[:, 128 * r : 128 * r + 128] = jnp.where(x == 0, OT[6 + r : 7 + r, :], OT[8 + r : 9 + r, :])
    for b in range(2):
        tab[:, 16 * b : 16 * b + 16] = jnp.where(x == 0, OT[12 + b : 13 + b, :16], OT[14 + b : 15 + b, :16])
    for cp in moves[3:]:
        cp.wait()


def vm(n=1):
    return [pl.BlockSpec(memory_space=pltpu.VMEM)] * n


def hb(n=1):
    return [pl.BlockSpec(memory_space=pltpu.HBM)] * n


def sems(*shape):
    return pltpu.SemaphoreType.DMA(shape)


def shape_of(dims, kind):
    return jax.ShapeDtypeStruct(dims, kind)


def team_local(
    audio_in, out_grad, item_len, rel_bucket, w_qkv, w_out, w_up, w_down,
    ln1_gain, ln1_bias, ln2_gain, ln2_bias, b_out, b_up, b_down, rel_table,
):
    rows, width = audio_in.shape[2], audio_in.shape[3]
    part = w_qkv.shape[1]
    hidden = w_up.shape[2]
    block = hidden // 16
    wide, ff = width // 4, hidden // 4
    low = lambda *dims: pltpu.VMEM(dims, BF)
    full = lambda *dims: pltpu.VMEM(dims, F32)

    lo, ig, OQ, OO, OU, OD, OT = pl.pallas_call(
        step_kernel,
        out_shape=(
            shape_of((2, rows, width), BF),
            shape_of((2, rows, width), F32),
            shape_of((4, part, 3 * wide), F32),
            shape_of((part, width), F32),
            shape_of((4, part, ff), F32),
            shape_of((block, width), F32),
            shape_of((16, 128), F32),
        ),
        in_specs=hb(2) + vm(2) + hb(4) + vm(8),
        out_specs=tuple(vm(7)),
        scratch_shapes=[
            low(4, part, 3 * wide), low(4, part, ff),
            low(2, 2, 2, 2, 2, part, 3 * wide), low(2, 4, part, width),
            low(2, 2, 2, 2, 2, part, ff), low(2, 4, block, width), low(4, rows, width),
            low(3, rows, width),
            low(2, 4, rows, width), low(2, 4, rows, width), low(2, 4, rows, ff), low(2, 4, rows, wide),
            low(2, 4, rows, 3 * wide), full(2, 4, 4 * rows, rows), full(8 * rows, ff), full(2, rows, width),
            low(2, 4, rows, width), low(2, 4, rows, width), low(2, 4, rows, ff), low(2, 4, rows, 3 * wide),
            low(4, rows, width), low(4, rows, width), low(4, rows, ff), low(4, rows, wide),
            low(4, rows, width), low(4, rows, width), low(4, rows, ff), low(4, rows, 3 * wide),
            low(4, rows, width), low(4, rows, width), low(4, rows, width), low(4, rows, width), full(rows, width),
            full(rows, width), full(rows, width), full(rows, width),
            low(2, 2, 2, 2, part, 3 * wide), low(4, part, width),
            low(2, 2, 2, part, 3 * wide), low(2, part, width), low(2, 2, 2, part, ff), low(2, block, width),
            low(2, 2, part, 3 * wide), low(part, width), low(2, 2, part, ff), low(block, width),
            low(2, 2, part, 3 * wide), low(part, width), low(2, 2, part, ff), low(block, width),
            low(4, part, 3 * wide), low(4, part, ff),
            full(2, 2, 2, 2, 16, 128), full(4, 2, 2, 2, 16, 128), full(2, 8, width), full(4, 8, 128),
            full(2, 4 * rows, rows), full(128, 128), full(2, 8, width), full(2, 1, ff), full(2, 4 * rows, rows),
            full(2, 2, 2, 2, 16, 128), full(4, 2, 2, 2, 16, 128), full(2, 2, 2, 16, 128), full(7, 16, 128),
            sems(11), sems(2, 4), sems(2, 4), sems(2, 2, 4), sems(2, 2, 4), sems(2, 4), sems(2, 4),
            sems(2, 4, 4), sems(2, 4, 4), sems(10), sems(10),
            sems(8, 6), sems(8, 6), sems(8, 4), sems(8, 4), sems(8, 4), sems(8, 4), sems(2), sems(2),
            sems(2, 2, 4), sems(2, 2, 4), sems(2, 4), sems(2, 4), sems(2, 4), sems(2, 4), sems(10), sems(10),
        ],
        compiler_params=pltpu.CompilerParams(
            collective_id=0, has_side_effects=True, vmem_limit_bytes=63 << 20
        ),
        name="two_layers",
    )(
        audio_in.reshape(2, rows, width), out_grad.reshape(2, rows, width), item_len.T, rel_bucket[None],
        w_qkv[0], w_out[0], w_up[0], w_down[0],
        ln1_gain, ln1_bias, ln2_gain, ln2_bias, b_out, b_down, b_up, rel_table,
    )

    lo, ig, oq, oo, ou, od, a0, a1, a2, a3, a4, bu, a5, tab = pl.pallas_call(
        finish_kernel,
        out_shape=(
            shape_of((2, rows, width), BF),
            shape_of((2, rows, width), F32),
            shape_of((part, 3 * width), F32),
            shape_of((part, width), F32),
            shape_of((part, hidden), F32),
            shape_of((block, width), F32),
        )
        + (shape_of((1, part), F32),) * 5
        + (shape_of((1, block), F32), shape_of((1, part), F32), shape_of((1, 32), F32)),
        in_specs=hb(7),
        out_specs=tuple(vm(14)),
        scratch_shapes=[full(4, part, 3 * wide), full(4, part, ff), full(16, 128), sems(7)],
        compiler_params=pltpu.CompilerParams(vmem_limit_bytes=62 << 20),
        name="finish",
    )(lo, ig, OQ, OO, OU, OD, OT)
    return (
        lo[None, :, None], ig[None, :, None], oq[None], oo[None], ou[None], od[None],
        a0, a1, a2, a3, a4, bu, a5, tab,
    )


def solution(mesh):
    fits = mesh.shape["dp"] == 16 and mesh.shape["section"] == 2
    return jax.shard_map(
        team_local if fits else local,
        mesh=mesh,
        in_specs=(
            P(None, "dp", None, None),
            P(None, "dp", None, None),
            P(None, "dp"),
            P(),
            P("section", "dp", None),
            P("section", "dp", None),
            P("section", "dp", None),
            P("section", "dp", None),
            P("section", "dp"),
            P("section", "dp"),
            P("section", "dp"),
            P("section", "dp"),
            P("section", "dp"),
            P("section", "dp"),
            P("section", "dp"),
            P("section", "dp"),
        ),
        out_specs=(
            P("section", None, "dp", None, None),
            P("section", None, "dp", None, None),
            P("section", "dp", None),
            P("section", "dp", None),
            P("section", "dp", None),
            P("section", "dp", None),
            P("section", "dp"),
            P("section", "dp"),
            P("section", "dp"),
            P("section", "dp"),
            P("section", "dp"),
            P("section", "dp"),
            P("section", "dp"),
            P("section", "dp"),
        ),
        check_vma=False,
    )
```

```python
import jax
import jax.numpy as jnp
from jax import lax
from jax.experimental import pallas as pl
from jax.experimental.pallas import tpu as pltpu
from jax.sharding import PartitionSpec as P

H = 16
NB = 32


epsilon = 1e-05
highest = lax.Precision.HIGHEST


def passed_along(block, axis, distance):
    devices = range(lax.axis_size(axis))
    route = [(i - distance, i) for i in devices if i - distance in devices]
    return lax.ppermute(block, axis, route)


def norm_rows(values):
    centre = values - jnp.mean(values, axis=-1, keepdims=True)
    return centre * lax.rsqrt(jnp.mean(centre * centre, axis=-1, keepdims=True) + epsilon)


def norm_affine(values, gain, shift):
    return norm_rows(values) * gain + shift


def contract_rows(left, right):
    return lax.dot_general(
        left, right, (((0,), (0,)), ((), ())), preferred_element_type=jnp.float32
    )


def contract_cols(left, right):
    return lax.dot_general(
        left, right, (((1,), (1,)), ((), ())), preferred_element_type=jnp.float32
    )


def toeplitz_rows(values):
    heads, length = values.shape
    reverse = jnp.flip(values, axis=1)
    padded = jnp.concatenate([reverse, jnp.zeros_like(reverse)], axis=1)
    tiled = jnp.tile(padded, (1, length))[:, : length * (2 * length - 1)]
    return tiled.reshape(heads, length, 2 * length - 1)[:, :, length - 1 :]


def diagonal_sums(grid):
    heads, length, _ = grid.shape
    widened = jnp.concatenate([jnp.zeros((heads, length, length - 1), grid.dtype), grid], axis=2)
    flat = widened.reshape(heads, length * (2 * length - 1))
    flat = jnp.concatenate([flat, jnp.zeros((heads, length), grid.dtype)], axis=1)
    folded = jnp.sum(flat.reshape(heads, length, 2 * length), axis=1)
    return jnp.flip(folded[:, :length], axis=1)


def bucket_table(buckets):
    return (buckets[None, :] == jnp.arange(NB, dtype=jnp.int32)[:, None]).astype(jnp.float32)


def make_bias(table_flat, onehot):
    table = table_flat.astype(jnp.float32).reshape(NB, H)
    per_distance = jnp.dot(table.T, onehot, precision=highest)
    return toeplitz_rows(per_distance)


def weight_terms(factors):
    normed, d_qkv, mixed, d_attn, second, d_hidden, activated, d_branch = factors
    return (
        contract_rows(normed, d_qkv),
        contract_rows(mixed, d_attn),
        contract_rows(second, d_hidden),
        contract_rows(activated, d_branch),
    )


def forward_item(inputs, length, bias, weights):
    (
        w_qkv,
        w_out,
        w_up,
        w_down,
        gain_one,
        shift_one,
        gain_two,
        shift_two,
        bias_out,
        bias_up,
        bias_down,
    ) = weights
    rows, width = inputs.shape
    heads = bias.shape[0]
    head_dim = width // heads
    scale = head_dim ** (-0.5)
    position = jnp.arange(rows)
    visible = (position[None, :] <= position[:, None])[None] & (position[None, None, :] < length)
    valid = (position < length).astype(jnp.float32)[:, None]
    normed = norm_affine(
        inputs, gain_one.astype(jnp.float32), shift_one.astype(jnp.float32)
    ).astype(jnp.bfloat16)
    qkv = jnp.dot(normed, w_qkv, preferred_element_type=jnp.float32).astype(jnp.bfloat16)
    query = qkv[:, :width].reshape(rows, heads, head_dim)
    keys = qkv[:, width : 2 * width].reshape(rows, heads, head_dim)
    values = qkv[:, 2 * width :].reshape(rows, heads, head_dim)
    scores = (
        jnp.einsum("ihd,jhd->hij", query, keys, preferred_element_type=jnp.float32) * scale + bias
    )
    scores = jnp.where(visible, scores, -1000000000.0)
    raised = jnp.exp(scores - jnp.max(scores, axis=-1, keepdims=True))
    probs = raised / jnp.sum(raised, axis=-1, keepdims=True)
    probs_low = probs.astype(jnp.bfloat16)
    mixed = (
        jnp.einsum("hij,jhd->ihd", probs_low, values, preferred_element_type=jnp.float32)
        .reshape(rows, width)
        .astype(jnp.bfloat16)
    )
    middle = (
        inputs
        + jnp.dot(mixed, w_out, preferred_element_type=jnp.float32)
        + bias_out.astype(jnp.float32)
    )
    second = norm_affine(
        middle, gain_two.astype(jnp.float32), shift_two.astype(jnp.float32)
    ).astype(jnp.bfloat16)
    hidden = jnp.dot(second, w_up, preferred_element_type=jnp.float32) + bias_up.astype(jnp.float32)
    activated = jax.nn.gelu(hidden).astype(jnp.bfloat16)
    result = (
        middle
        + jnp.dot(activated, w_down, preferred_element_type=jnp.float32)
        + bias_down.astype(jnp.float32)
    ) * valid
    saved = (
        normed,
        query,
        keys,
        values,
        probs,
        probs_low,
        mixed,
        middle,
        second,
        hidden,
        activated,
        valid,
    )
    return (result, saved)


def backward_item(inputs, length, bias, weights, upstream, onehot):
    (
        w_qkv,
        w_out,
        w_up,
        w_down,
        gain_one,
        shift_one,
        gain_two,
        shift_two,
        bias_out,
        bias_up,
        bias_down,
    ) = weights
    _, saved = forward_item(inputs, length, bias, weights)
    (
        normed,
        query,
        keys,
        values,
        probs,
        probs_low,
        mixed,
        middle,
        second,
        hidden,
        activated,
        valid,
    ) = saved
    rows, width = inputs.shape
    heads = bias.shape[0]
    head_dim = width // heads
    scale = head_dim ** (-0.5)
    direct = upstream * valid
    d_branch = direct.astype(jnp.bfloat16)
    grad_bdown = jnp.sum(d_branch.astype(jnp.float32), axis=0)
    d_activated = contract_cols(d_branch, w_down)
    _, gelu_back = jax.vjp(jax.nn.gelu, hidden)
    d_hidden = gelu_back(d_activated)[0].astype(jnp.bfloat16)
    grad_bup = jnp.sum(d_hidden.astype(jnp.float32), axis=0)
    d_second = contract_cols(d_hidden, w_up)
    _, second_back = jax.vjp(
        norm_affine, middle, gain_two.astype(jnp.float32), shift_two.astype(jnp.float32)
    )
    d_middle, grad_gain_two, grad_shift_two = second_back(d_second)
    d_middle = d_middle + direct
    d_attn = d_middle.astype(jnp.bfloat16)
    grad_bout = jnp.sum(d_attn.astype(jnp.float32), axis=0)
    d_mixed = contract_cols(d_attn, w_out).astype(jnp.bfloat16).reshape(rows, heads, head_dim)
    grad_values = jnp.einsum("hij,ihd->jhd", probs_low, d_mixed, preferred_element_type=jnp.float32)
    d_probs = jnp.einsum("ihd,jhd->hij", d_mixed, values, preferred_element_type=jnp.float32)
    d_scores = (probs * (d_probs - jnp.sum(probs * d_probs, axis=-1, keepdims=True))).astype(
        jnp.bfloat16
    )
    grad_query = (
        jnp.einsum("hij,jhd->ihd", d_scores, keys, preferred_element_type=jnp.float32) * scale
    )
    grad_keys = (
        jnp.einsum("hij,ihd->jhd", d_scores, query, preferred_element_type=jnp.float32) * scale
    )
    d_qkv = jnp.concatenate(
        [
            grad_query.reshape(rows, width),
            grad_keys.reshape(rows, width),
            grad_values.reshape(rows, width),
        ],
        axis=1,
    ).astype(jnp.bfloat16)
    d_normed = contract_cols(d_qkv, w_qkv)
    _, first_back = jax.vjp(
        norm_affine, inputs, gain_one.astype(jnp.float32), shift_one.astype(jnp.float32)
    )
    d_inputs, grad_gain_one, grad_shift_one = first_back(d_normed)
    d_inputs = d_inputs + d_middle
    per_distance = diagonal_sums(d_scores.astype(jnp.float32))
    grad_table = jnp.dot(onehot, per_distance.T, precision=highest).reshape(-1)
    factors = (normed, d_qkv, mixed, d_attn, second, d_hidden, activated, d_branch)
    small = (
        grad_gain_one,
        grad_shift_one,
        grad_gain_two,
        grad_shift_two,
        grad_bout,
        grad_bup,
        grad_bdown,
        grad_table,
    )
    return (d_inputs, factors, small)


def local(
    audio_in,
    out_grad,
    item_len,
    rel_bucket,
    w_qkv,
    w_out,
    w_up,
    w_down,
    ln1_gain,
    ln1_bias,
    ln2_gain,
    ln2_bias,
    b_out,
    b_up,
    b_down,
    rel_table,
):
    section = lax.axis_index("section")
    micro = audio_in.shape[0]
    rows = audio_in.shape[2]
    width = audio_in.shape[3]
    qkv_part = w_qkv[0].astype(jnp.bfloat16)
    out_part = w_out[0].astype(jnp.bfloat16)
    up_part = w_up[0].astype(jnp.bfloat16)
    down_part = w_down[0].astype(jnp.bfloat16)
    gain_one_part = ln1_gain[0].astype(jnp.bfloat16)
    shift_one_part = ln1_bias[0].astype(jnp.bfloat16)
    gain_two_part = ln2_gain[0].astype(jnp.bfloat16)
    shift_two_part = ln2_bias[0].astype(jnp.bfloat16)
    bias_out_part = b_out[0].astype(jnp.bfloat16)
    bias_up_part = b_up[0].astype(jnp.bfloat16)
    bias_down_part = b_down[0].astype(jnp.bfloat16)
    table_part = rel_table[0].astype(jnp.bfloat16)
    parts = (
        qkv_part,
        out_part,
        up_part,
        down_part,
        gain_one_part,
        shift_one_part,
        gain_two_part,
        shift_two_part,
        bias_out_part,
        bias_up_part,
        bias_down_part,
        table_part,
    )
    gathered = (
        lax.all_gather(qkv_part, "dp", axis=0, tiled=True),
        lax.all_gather(out_part, "dp", axis=0, tiled=True),
        lax.all_gather(up_part, "dp", axis=0, tiled=True),
        lax.all_gather(down_part, "dp", axis=0, tiled=True),
        lax.all_gather(gain_one_part, "dp", axis=0, tiled=True),
        lax.all_gather(shift_one_part, "dp", axis=0, tiled=True),
        lax.all_gather(gain_two_part, "dp", axis=0, tiled=True),
        lax.all_gather(shift_two_part, "dp", axis=0, tiled=True),
        lax.all_gather(bias_out_part, "dp", axis=0, tiled=True),
        lax.all_gather(bias_up_part, "dp", axis=0, tiled=True),
        lax.all_gather(bias_down_part, "dp", axis=0, tiled=True),
        lax.all_gather(table_part, "dp", axis=0, tiled=True),
    )
    onehot = bucket_table(rel_bucket)
    weights = gathered[:11]
    bias = make_bias(gathered[11], onehot)
    lengths = item_len[:, 0]
    hidden_width = gathered[2].shape[1]

    def run_forward(layer_in, length):
        return forward_item(layer_in.astype(jnp.float32), length, bias, weights)[0]

    def skip_forward(layer_in, length):
        return jnp.zeros(layer_in.shape, jnp.float32)

    incoming = jnp.zeros((rows, width), jnp.bfloat16)
    produced = []
    taken = []
    for tick in range(micro + 1):
        slot = tick - section
        active = jnp.logical_and(slot >= 0, slot < micro)
        length = lengths[jnp.clip(slot, 0, micro - 1)]
        own = audio_in[min(tick, micro - 1), 0]
        layer_in = jnp.where(section == 0, own, incoming)
        layer_out = lax.cond(active, run_forward, skip_forward, layer_in, length).astype(
            jnp.bfloat16
        )
        produced.append(layer_out)
        taken.append(layer_in)
        if tick < micro:
            incoming = passed_along(layer_out, "section", 1)
    outputs = jnp.stack(
        [jnp.where(section == 0, produced[batch], produced[batch + 1]) for batch in range(micro)]
    )
    kept = jnp.stack(
        [jnp.where(section == 0, taken[batch], taken[batch + 1]) for batch in range(micro)]
    )
    regathered = (
        lax.all_gather(qkv_part, "dp", axis=0, tiled=True),
        lax.all_gather(out_part, "dp", axis=0, tiled=True),
        lax.all_gather(up_part, "dp", axis=0, tiled=True),
        lax.all_gather(down_part, "dp", axis=0, tiled=True),
        lax.all_gather(gain_one_part, "dp", axis=0, tiled=True),
        lax.all_gather(shift_one_part, "dp", axis=0, tiled=True),
        lax.all_gather(gain_two_part, "dp", axis=0, tiled=True),
        lax.all_gather(shift_two_part, "dp", axis=0, tiled=True),
        lax.all_gather(bias_out_part, "dp", axis=0, tiled=True),
        lax.all_gather(bias_up_part, "dp", axis=0, tiled=True),
        lax.all_gather(bias_down_part, "dp", axis=0, tiled=True),
        lax.all_gather(table_part, "dp", axis=0, tiled=True),
    )
    back_weights = regathered[:11]
    back_bias = make_bias(regathered[11], onehot)

    def run_backward(layer_in, length, upstream):
        return backward_item(
            layer_in.astype(jnp.float32), length, back_bias, back_weights, upstream, onehot
        )

    def skip_backward(layer_in, length, upstream):
        zero_rows = jnp.zeros((rows, width), jnp.bfloat16)
        zero_triple = jnp.zeros((rows, 3 * width), jnp.bfloat16)
        zero_hidden = jnp.zeros((rows, hidden_width), jnp.bfloat16)
        factors = (
            zero_rows,
            zero_triple,
            zero_rows,
            zero_rows,
            zero_rows,
            zero_hidden,
            zero_hidden,
            zero_rows,
        )
        small = tuple((jnp.zeros(piece.shape, jnp.float32) for piece in gathered[4:]))
        return (jnp.zeros(upstream.shape, jnp.float32), factors, small)

    small_totals = tuple((jnp.zeros(piece.shape, jnp.float32) for piece in gathered[4:]))
    shares = tuple((jnp.zeros(piece.shape, jnp.float32) for piece in parts))
    returned = jnp.zeros((rows, width), jnp.bfloat16)
    results = []
    sent_list = []
    factor_list = []
    for tick in range(micro + 1):
        slot = tick - 1 + section
        active = jnp.logical_and(slot >= 0, slot < micro)
        pick = jnp.clip(slot, 0, micro - 1)
        length = lengths[pick]
        layer_in = kept[pick]
        target = out_grad[min(tick, micro - 1), 0].astype(jnp.float32)
        upstream = jnp.where(section == 1, target, returned.astype(jnp.float32))
        d_inputs, factors, small = lax.cond(
            active, run_backward, skip_backward, layer_in, length, upstream
        )
        factor_list.append(factors)
        small_totals = tuple((total + term for total, term in zip(small_totals, small)))
        results.append(d_inputs)
        if tick < micro:
            sent = d_inputs.astype(jnp.bfloat16)
            sent_list.append(lax.optimization_barrier(sent))
            returned = passed_along(sent, "section", -1)
    stacked = tuple(
        (jnp.concatenate([entry[index] for entry in factor_list], axis=0) for index in range(8))
    )
    totals = weight_terms(stacked) + small_totals
    shares = (
        lax.psum_scatter(totals[0], "dp", scatter_dimension=0, tiled=True),
        lax.psum_scatter(totals[1], "dp", scatter_dimension=0, tiled=True),
        lax.psum_scatter(totals[2], "dp", scatter_dimension=0, tiled=True),
        lax.psum_scatter(totals[3], "dp", scatter_dimension=0, tiled=True),
        lax.psum_scatter(totals[4], "dp", scatter_dimension=0, tiled=True),
        lax.psum_scatter(totals[5], "dp", scatter_dimension=0, tiled=True),
        lax.psum_scatter(totals[6], "dp", scatter_dimension=0, tiled=True),
        lax.psum_scatter(totals[7], "dp", scatter_dimension=0, tiled=True),
        lax.psum_scatter(totals[8], "dp", scatter_dimension=0, tiled=True),
        lax.psum_scatter(totals[9], "dp", scatter_dimension=0, tiled=True),
        lax.psum_scatter(totals[10], "dp", scatter_dimension=0, tiled=True),
        lax.psum_scatter(totals[11], "dp", scatter_dimension=0, tiled=True),
    )
    input_grads = jnp.stack(
        [
            jnp.where(section == 0, results[batch + 1], sent_list[batch].astype(jnp.float32))
            for batch in range(micro)
        ]
    )
    grads_out = tuple((share[None] for share in shares))
    return (outputs[None, :, None], input_grads[None, :, None]) + grads_out


E5 = 1e-05
F32 = jnp.float32
BF = jnp.bfloat16
MESH = pl.DeviceIdType.MESH
GELU_K = 0.7978845608028654
HD = 64


class Place:
    def __init__(self):
        self.s = lax.axis_index("section")
        d = lax.axis_index("dp")
        self.x = d % 2
        self.y = (d // 2) % 2
        self.z = (d // 4) % 2
        self.h = d // 8
        self.t = self.x + 2 * self.z

    def device(self, s=None, x=None, y=None, z=None, h=None):
        s = self.s if s is None else s
        x = self.x if x is None else x
        y = self.y if y is None else y
        z = self.z if z is None else z
        h = self.h if h is None else h
        return (s, x + 2 * y + 4 * z + 8 * h)

    def sibling(self):
        return self.device(s=1 - self.s)

    def across_y(self):
        return self.device(y=1 - self.y)

    def across_h(self):
        return self.device(h=1 - self.h)

    def mate(self, k):
        return self.x + (k % 2) * (1 - 2 * self.x), self.z + (k // 2) * (1 - 2 * self.z)

    def team(self, k):
        px, pz = self.mate(k)
        return self.device(x=px, z=pz), px + 2 * pz


def remote(src, dst, send, recv, device):
    return pltpu.make_async_remote_copy(
        src_ref=src, dst_ref=dst, send_sem=send, recv_sem=recv, device_id=device, device_id_type=MESH
    )


def dot(a, b):
    return jnp.dot(a, b, preferred_element_type=F32)


def dot_nt(a, b):
    return lax.dot_general(a, b, (((1,), (1,)), ((), ())), preferred_element_type=F32)


def dot_tn(a, b):
    return lax.dot_general(a, b, (((0,), (0,)), ((), ())), preferred_element_type=F32)


def rows_norm(v):
    centre = v - jnp.mean(v, axis=-1, keepdims=True)
    scale = lax.rsqrt(jnp.mean(centre * centre, axis=-1, keepdims=True) + E5)
    return centre * scale, scale


def norm_back(cot, normed, scale, gain):
    inner = cot * gain
    return scale * (
        inner
        - jnp.mean(inner, axis=-1, keepdims=True)
        - normed * jnp.mean(inner * normed, axis=-1, keepdims=True)
    )


def column_sum(v):
    return jnp.sum(v, axis=0, keepdims=True)


def lanes_of(shape, axis=1):
    return lax.broadcasted_iota(jnp.int32, shape, axis)


def split_heads(block, count, size):
    lane = lanes_of(block.shape) // size
    return jnp.concatenate([jnp.where(lane == i, block, jnp.zeros_like(block)) for i in range(count)], axis=0)


def join_heads(block, count, size):
    rows = block.shape[0] // count
    lane = lanes_of((rows, block.shape[1])) // size
    total = jnp.where(lane == 0, block[:rows], 0.0)
    for i in range(1, count):
        total = jnp.where(lane == i, block[i * rows : (i + 1) * rows], total)
    return total


def turn(block, shift):
    width = block.shape[1]
    shift = shift % width
    return jnp.concatenate([block[:, width - shift :], block[:, : width - shift]], axis=1)


def skew(block, length, sign):
    row = lanes_of(block.shape, 0) % length
    for bit in range(7):
        block = jnp.where((row // 2**bit) % 2 == 1, turn(block, sign * 2**bit), block)
    return block


class Part:
    def __init__(self, index, pieces, **refs):
        self.index = index
        self.pieces = pieces
        self.chunks = 2 + pieces
        for name, ref in refs.items():
            setattr(self, name, ref)

    def strip(self, c, rows):
        step = rows // self.pieces
        return pl.ds((c - 2) * step, step)


def step_kernel(
    x_ref, og_ref, il_ref, rb_ref, wq_in, wo_in, wu_in, wd_in,
    v0_ref, v1_ref, v2_ref, v3_ref, v4_ref, v5_ref, bu_ref, rt_ref,
    lo, ig, OQ, OO, OU, OD, OT,
    SQ, SU, WQ, WO, WU, WD, XG, XIN, A, C, FA, MIX, QKV, PR, UF, HM, DZ, DAT, DU, DQ,
    XA, XC, XF, XM, XDZ, XDAT, XDU, XDQ, RB, SB, SY, RY, OWN, OWNY, DX, DH,
    GQ, GO, YQ, YO, YU, YD, ZSQ, ZSO, ZSU, ZSD, ZRQ, ZRO, ZRU, ZRD, TRQ, TRU,
    SPT, SPR, VEC, LEN, BIAS, PD, SGV, SBU, DS, MT, MR, M1, MN,
    ls, ss_a, rs_a, ss_wy, rs_wy, ss_wh, rs_wh, ss_ws, rs_ws, ss_p, rs_p,
    ss_g, rs_g, ss_r, rs_r, ss_x, rs_x, ss_o, rs_o,
    ss_gy, rs_gy, ss_gh, rs_gh, ss_gt, rs_gt, ss_m, rs_m,
):
    p = Place()
    s, x, y, z, h, t = p.s, p.x, p.y, p.z, p.h, p.t
    sib, ypeer, hpeer = p.sibling(), p.across_y(), p.across_h()
    rows, width = x_ref.shape[1], x_ref.shape[2]
    heads = 4
    wide = heads * HD
    ff = FA.shape[3]
    part_rows = WO.shape[2]
    block = WD.shape[2]

    def only(core, what):
        @pl.when(s == core)
        def _():
            what()

    half = rows // 2
    upper, lower = pl.ds(0, half), pl.ds(half, half)
    x_dev, x_slot = p.team(1)
    z_dev, z_slot = p.team(2)
    d_slot = p.team(3)[1]

    def hop(ref, c, n, slot, span, device):
        view = ref.at[slot, span]
        return remote(view, view, ss_g.at[c, n], rs_g.at[c, n], device)

    def gather_sends(ref, c):
        return (
            hop(ref, c, 2, t, upper, z_dev), hop(ref, c, 0, t, upper, x_dev),
            hop(ref, c, 3, t, lower, z_dev), hop(ref, c, 1, t, lower, x_dev),
        )

    def relays(ref, c):
        return hop(ref, c, 4, z_slot, upper, x_dev), hop(ref, c, 5, z_slot, lower, x_dev)

    def gather_start(ref, c):
        for cp in gather_sends(ref, c):
            cp.start()

    def gather_relay(ref, c):
        onward = relays(ref, c)
        hop(ref, c, 2, z_slot, upper, z_dev).wait_recv()
        onward[0].start()
        hop(ref, c, 3, z_slot, lower, z_dev).wait_recv()
        onward[1].start()

    def gather_take(ref, c, k):
        if k == 1:
            hop(ref, c, 0, x_slot, upper, x_dev).wait_recv()
            hop(ref, c, 1, x_slot, lower, x_dev).wait_recv()
        if k == 3:
            hop(ref, c, 4, d_slot, upper, x_dev).wait_recv()
            hop(ref, c, 5, d_slot, lower, x_dev).wait_recv()

    def gather_end(ref, c):
        for cp in gather_sends(ref, c) + relays(ref, c):
            cp.wait_send()

    def reduce_copy(c, k, side=False):
        out, land = (SY, RY) if side else (SB, RB)
        return remote(out.at[k], land.at[k], ss_r.at[c, k], rs_r.at[c, k], p.team(k)[0])

    def reduce_put(c, k, value, side=False):
        @pl.when(k == 0)
        def _():
            (OWNY if side else OWN)[...] = value

        @pl.when(k > 0)
        def _():
            (SY if side else SB)[k] = value.astype(BF)
            if not side:
                reduce_copy(c, k).start()

    def reduce_end(c, side=False):
        total = (OWNY if side else OWN)[...]
        for k in (1, 2, 3):
            reduce_copy(c, k, side).wait()
            total = total + (RY if side else RB)[k].astype(F32)
        return total

    def each_item(gathers, body, aside, relay=True):
        def step(n, carry):
            if relay:

                @pl.when(n == 1)
                def _():
                    gather_relay(*gathers[0])

            for m, mate in ((2, 1), (3, 3)):

                @pl.when(n == m)
                def _(mate=mate):
                    for ref, c in gathers:
                        gather_take(ref, c, mate)

            k = 2 * (n % 2) + n // 2
            body(k, p.team(k)[1])
            aside(n)
            return carry

        lax.fori_loop(0, 4, step, 0)
        for ref, c in gathers:
            gather_end(ref, c)

    def at_step(k, here, n, what):
        @pl.when(jnp.logical_and(here, k == n))
        def _():
            what()

    first = Part(0, 1, W=WQ, V=WO, S=SQ, G=GQ, R=GO, Y=YQ, YR=YO, ZS=ZSQ, ZSR=ZSO, ZR=ZRQ, ZRR=ZRO,
                 TS=SQ, TR=TRQ, O=OQ, OR=OO)
    second = Part(1, 2, W=WU, V=WD, S=SU, G=WU.at[1], R=WD.at[1], Y=YU, YR=YD, ZS=ZSU, ZSR=ZSD, ZR=ZRU, ZRR=ZRD,
                  TS=SU, TR=TRU, O=OU, OR=OD)

    loads = [
        pltpu.make_async_copy(wq_in.at[:, pl.ds(width * i, width)], UF.at[pl.ds(576 + 64 * i, 64)], ls.at[i])
        for i in range(3)
    ]
    loads.append(pltpu.make_async_copy(wo_in, UF.at[pl.ds(0, 64)], ls.at[3]))
    loads += [
        pltpu.make_async_copy(wu_in.at[:, pl.ds(width * i, width)], UF.at[pl.ds(320 + 64 * i, 64)], ls.at[4 + i])
        for i in range(4)
    ]
    loads.append(pltpu.make_async_copy(wd_in, UF.at[pl.ds(64, 256)], ls.at[8]))
    loads.append(pltpu.make_async_copy(x_ref.at[s], XG.at[t], ls.at[9]))
    loads.append(pltpu.make_async_copy(og_ref.at[s], DZ.at[1, t], ls.at[10]))
    for cp in loads:
        cp.start()

    bell = pltpu.get_barrier_semaphore()
    around = [(a, b, e) for a in range(2) for b in range(2) for e in range(2)][1:]

    def station(a, b, e):
        return p.device(s=s + a * (1 - 2 * s), y=y + b * (1 - 2 * y), h=h + e * (1 - 2 * h))

    everyone = [p.team(k)[0] for k in (1, 2, 3)] + [station(*o) for o in around]
    for peer in everyone:
        pl.semaphore_signal(bell, inc=1, device_id=peer, device_id_type=MESH)

    for cp in loads[:4]:
        cp.wait()
    for i in range(3):
        for hh in range(2):
            for zz in range(2):
                base = (2 * zz + 4 * hh) * 128
                even = UF[576 + 64 * i : 640 + 64 * i, base : base + 128].astype(BF)
                odd = UF[576 + 64 * i : 640 + 64 * i, base + 128 : base + 256].astype(BF)
                at = (2 * i + hh) * 128
                SQ[2 * zz, :, at : at + 128] = jnp.concatenate([even[:, :HD], odd[:, :HD]], axis=1)
                SQ[2 * zz + 1, :, at : at + 128] = jnp.concatenate([even[:, HD:], odd[:, HD:]], axis=1)
    WQ[s, h, z, y, x] = SQ[t]
    q = 2 * h + y
    WO[s, q] = UF[0:64, :].astype(BF)
    pl.semaphore_wait(bell, len(everyone))

    def w_team(part, k):
        device, slot = p.team(k)
        return remote(
            part.S.at[slot], part.W.at[s, h, z, y, x], ss_a.at[part.index, k], rs_a.at[part.index, k], device
        )

    def w_view(part, c, hh, yy):
        if c < 2:
            return part.W.at[s, hh, c, yy]
        return part.V.at[s, 2 * hh + yy, part.strip(c, part.V.shape[2])]

    def w_y(part, c, n):
        view = w_view(part, c, h + n * (1 - 2 * h), y)
        return remote(view, view, ss_wy.at[part.index, n, c], rs_wy.at[part.index, n, c], ypeer)

    def w_h(part, c):
        view = w_view(part, c, h, y)
        return remote(view, view, ss_wh.at[part.index, c], rs_wh.at[part.index, c], hpeer)

    def w_s(part, c, hh, yy):
        view = w_view(part, c, hh, yy)
        n = 2 * hh + yy
        return remote(view, view, ss_ws.at[part.index, n, c], rs_ws.at[part.index, n, c], sib)

    order = ((first, 2), (first, 0), (first, 1), (second, 0), (second, 1), (second, 2), (second, 3))

    def w_share(j):
        part, c = order[j]
        if j in (1, 3):
            for k in (1, 2, 3):
                w_team(part, k).wait_recv()
        w_h(part, c).start()
        w_y(part, c, 0).start()
        w_s(part, c, h, y).start()

    def w_pass(j):
        part, c = order[j]
        w_h(part, c).wait_recv()
        w_y(part, c, 1).start()
        w_s(part, c, 1 - h, y).start()
        if j + 2 < len(order):
            w_share(j + 2)

    def w_near(part):
        for c in range(part.chunks):
            w_y(part, c, 0).wait_recv()
            w_s(part, c, h, 1 - y).start()

    def w_far(part):
        for c in range(part.chunks):
            w_y(part, c, 1).wait_recv()
            w_s(part, c, 1 - h, 1 - y).start()

    def w_other(part):
        for c in range(part.chunks):
            for n in range(4):
                w_s(part, c, n // 2, n % 2).wait_recv()

    for k in (1, 2, 3):
        w_team(first, k).start()
    loads[9].wait()

    @pl.when(s == 0)
    def _():
        w_share(0)

    for cp in loads[4:9]:
        cp.wait()
    for hh in range(2):
        for zz in range(2):
            for yy in range(2):
                for xx in range(2):
                    at = (2 * hh + yy) * block
                    low = 320 + 64 * (zz + 2 * hh)
                    col = (xx + 2 * yy) * block
                    SU[xx + 2 * zz, :, at : at + block] = UF[low : low + 64, col : col + block].astype(BF)
    WU[s, h, z, y, x] = SU[t]
    WD[s, q] = UF[64 : 64 + block, :].astype(BF)

    position = lanes_of((rows, 1), 0).astype(F32)
    count = jnp.where(s == 0, il_ref[:, 0:1], il_ref[:, 1:2]).astype(F32)
    valid = (position < count).astype(F32)
    loads[10].wait()
    DZ[1, t] = (valid * DZ[1, t].astype(F32)).astype(BF)

    lane = lanes_of((1, 128))
    zero = jnp.zeros((1, 128), F32)
    pair = [jnp.concatenate([v[...], v[...]], axis=1) for v in (v0_ref, v1_ref, v2_ref, v3_ref, v4_ref, v5_ref)]
    lines = [jnp.where(lane // HD == x, v, zero) for v in pair]
    for xx in range(2):
        for i in range(2):
            lines.append(jnp.where(x == xx, bu_ref[:, 128 * i : 128 * i + 128], zero))
    table = jnp.concatenate([rt_ref[...], jnp.zeros((1, 96), F32)], axis=1)
    counts = jnp.where(lane == 0, il_ref[:, 0:1].astype(F32), jnp.where(lane == 1, il_ref[:, 1:2].astype(F32), zero))
    for piece in (table, counts):
        for xx in range(2):
            lines.append(jnp.where(x == xx, piece, zero))
    for i in range(2):
        lines.append(zero)
    for i in range(16):
        SPR[t, h, y, s, i : i + 1, :] = lines[i].astype(BF).astype(F32)

    def near_copy(n):
        view = SPR.at[t, h, y, s]
        return remote(view, view, ss_p.at[n], rs_p.at[n], station(*around[n]))

    def team_copy(k):
        view = SPR.at[t]
        return remote(view, view, ss_p.at[6 + k], rs_p.at[6 + k], p.team(k)[0])

    for n in range(7):
        near_copy(n).start()
    only(0, lambda: w_share(1))
    gather_start(XG, 0)
    for n in range(7):
        near_copy(n).wait()
    for k in (1, 2, 3):
        team_copy(k).start()
    for k in (1, 2, 3):
        w_team(second, k).start()
    only(0, lambda: w_pass(0))
    gather_relay(XG, 0)
    for k in (1, 2, 3):
        team_copy(k).wait()
    for hh in range(2):
        for zz in range(2):
            for yy in range(2):
                for i in range(2):
                    SPT[hh, zz, yy, i] = SPR[2 * zz, hh, yy, i] + SPR[2 * zz + 1, hh, yy, i]
    gather_start(DZ.at[1], 4)
    only(0, lambda: (w_pass(1), w_pass(2)))

    for hh in range(2):
        for zz in range(2):
            for yy in range(2):
                at = (yy + 2 * zz + 4 * hh) * 128
                for i in range(2):
                    VEC[i, 0:6, at : at + 128] = SPT[hh, zz, yy, i, 0:6, :]
    for i in range(2):
        for hh in range(2):
            for yy in range(2):
                tile = SPT[hh, z, yy, i]
                for r in range(2):
                    at = (2 * hh + yy) * block + 128 * r
                    VEC[i, 6:7, at : at + 128] = jnp.where(x == 0, tile[6 + r : 7 + r], tile[8 + r : 9 + r])
    for zz in range(2):
        tile = SPT[h, zz, y, 0]
        for xx in range(2):
            tokens = jnp.sum(jnp.where(lane == s, tile[12 + xx : 13 + xx], 0.0), axis=1, keepdims=True)
            LEN[xx + 2 * zz] = jnp.broadcast_to(tokens, (8, 128))

    mark = jnp.concatenate([rb_ref[...], jnp.full((1, 128 - rows), 2 * NB, jnp.int32)], axis=1).astype(BF)
    mark = jnp.broadcast_to(mark, (8, 128))
    flip = ((lanes_of((128, 128), 0) + lanes_of((128, 128))) % 128 == 0).astype(F32).astype(BF)
    mark = dot(mark, flip)[0:1]
    onehot = (lanes_of((NB, 128), 0).astype(F32) == mark).astype(F32)
    for i in range(2):
        lines = []
        for hh in range(2):
            for zz in range(2):
                for yy in range(2):
                    tile = SPT[hh, zz, yy, i]
                    for xx in range(2):
                        for b in range(2):
                            lines.append(tile[10 + xx : 11 + xx, 16 * b : 16 * b + 16])
        by_bucket = jnp.concatenate([jnp.concatenate(lines, axis=0), jnp.zeros((NB, 112), F32)], axis=1)
        PD[...] = dot_tn(by_bucket.astype(BF), onehot.astype(BF))
        stack = []
        for hh in range(2):
            for yy in range(2):
                line = PD[pl.ds(x + 2 * yy + 4 * z + 8 * hh, 1), :]
                stack.append(jnp.broadcast_to(line, (rows, 128)))
        grid = skew(jnp.concatenate(stack, axis=0), rows, 1)[:, :rows]
        causal = lanes_of(grid.shape) <= lanes_of(grid.shape, 0) % rows
        BIAS[i] = jnp.where(causal, grid, -1000000000.0)
    gather_relay(DZ.at[1], 4)

    pairs = ((A, XA), (MIX, XM), (C, XC), (FA, XF), (DZ, XDZ), (DAT, XDAT), (DU, XDU), (DQ, XDQ))

    def share_copy(i, layer, slot):
        return remote(pairs[i][0].at[layer, slot], pairs[i][1].at[slot], ss_x.at[i, slot], rs_x.at[i, slot], sib)

    def share_item(k, layer, which):
        @pl.when(s != layer)
        def _():
            for i in which:
                share_copy(i, layer, p.team(k)[1]).start()

    def row(layer, index):
        return VEC[layer, index : index + 1, :]

    def w_qkv(layer):
        return WQ[layer].reshape(width, 3 * wide)

    def w_up(layer):
        return WU[layer].reshape(width, ff)

    def w_out(layer):
        return WO[layer].reshape(wide, width)

    def w_down(layer):
        return WD[layer].reshape(ff, width)

    def u_rows(layer, i):
        return pl.ds(pl.multiple_of((layer * 4 + i) * rows, 8), rows)

    def g_own(part, c, hh, yy):
        if c < 2:
            return part.G.at[hh, c, yy]
        return part.R.at[2 * hh + yy, part.strip(c, part.R.shape[1])]

    def g_land(part, c, n):
        if c < 2:
            return part.Y.at[n, c]
        return part.YR.at[n, part.strip(c, part.R.shape[1])]

    def g_half(n):
        return (1 - h) + n * (2 * h - 1)

    def g_big(part, c, n):
        return remote(
            part.G.at[g_half(n), c, 1 - y], part.Y.at[n, c],
            ss_gy.at[part.index, n, c], rs_gy.at[part.index, n, c], ypeer,
        )

    def g_y(part, c, n):
        return remote(
            g_own(part, c, g_half(n), 1 - y), g_land(part, c, n),
            ss_gy.at[part.index, n, c], rs_gy.at[part.index, n, c], ypeer,
        )

    def g_z(part, c, out):
        if c < 2:
            return (part.ZS if out else part.ZR).at[c]
        return (part.ZSR if out else part.ZRR).at[part.strip(c, part.R.shape[1])]

    def g_h(part, c):
        return remote(
            g_z(part, c, True), g_z(part, c, False), ss_gh.at[part.index, c], rs_gh.at[part.index, c], hpeer
        )

    def g_t(part, k):
        return remote(
            part.TS.at[k], part.TR.at[k], ss_gt.at[part.index, k], rs_gt.at[part.index, k], p.team(k)[0]
        )

    def flat(ref, span):
        value = ref[:, :, span]
        return value.reshape(value.shape[0] * value.shape[1], value.shape[2])

    def product(left, right, span):
        every = pl.ds(0, right[0].shape[2])
        return dot_tn(flat(left[0], span), flat(right[0], every)) + dot_tn(
            flat(left[1], span), flat(right[1], every)
        )

    def g_make(part, n):
        if part is first:
            need = (0, 1, 5, 7)
            big_l, big_r = (A.at[s], XA), (DQ.at[s], XDQ)
            small_l, small_r = (MIX.at[s], XM), (DAT.at[s], XDAT)
            small_span = HD
        else:
            need = (2, 3, 4, 6)
            big_l, big_r = (C.at[s], XC), (DU.at[s], XDU)
            small_l, small_r = (FA.at[s], XF), (DZ.at[s], XDZ)
            small_span = block
        if n == 0:
            for i in need:
                for slot in range(4):
                    share_copy(i, s, slot).wait_recv()
        hh = g_half(n)
        if part is first:
            if n == 0:
                value = product(small_l, small_r, pl.ds(0, wide)).astype(BF)
                for i in range(4):
                    part.R[i] = value[i * small_span : (i + 1) * small_span]
            if n == 0:
                g_y(part, 2, n).start()

        def tile(zz, carry):
            span = pl.ds(pl.multiple_of((2 * hh + zz) * 256, 256), 256)
            value = product(big_l, big_r, span).astype(BF)
            part.G[hh, zz] = value.reshape(2, 2, part_rows, value.shape[1])
            if n == 0:
                g_big(part, zz, n).start()
            return carry

        lax.fori_loop(0, 2, tile, 0)
        if part is second:

            def strip(m, carry):
                yy = (1 - y) + m * (2 * y - 1)
                span = pl.ds(pl.multiple_of((2 * hh + yy) * 256, 256), 256)
                part.R[2 * hh + yy] = product(small_l, small_r, span).astype(BF)

                if n == 0:

                    @pl.when(m == 0)
                    def _():
                        for c in range(2, part.chunks):
                            g_y(part, c, n).start()

                return carry

            lax.fori_loop(0, 2, strip, 0)

    def g_fold(part, c):
        g_y(part, c, 0).wait_recv()
        g_z(part, c, True)[...] = (
            g_own(part, c, 1 - h, y)[...].astype(F32) + g_land(part, c, 0)[...].astype(F32)
        ).astype(BF)
        g_h(part, c).start()

    def g_later(part):
        for c in range(part.chunks):
            g_y(part, c, 1).start()

    def g_total(part):
        for c in range(part.chunks):
            g_y(part, c, 1).wait_recv()
            g_h(part, c).wait_recv()

        def total(xx, zz):
            return (
                part.G[h, zz, y, xx].astype(F32) + part.Y[1, zz, xx].astype(F32) + part.ZR[zz, xx].astype(F32)
            )

        for k in (1, 2, 3):
            part.TS[k] = total(*p.mate(k)).astype(BF)
            g_t(part, k).start()
        part.O[t] = total(x, z)
        part.OR[...] = part.R[q].astype(F32) + part.YR[1].astype(F32) + part.ZRR[...].astype(F32)

    def g_end(part):
        for k in (1, 2, 3):
            g_t(part, k).wait_recv()
            part.O[p.team(k)[1]] = part.TR[k].astype(F32)

    XIN[0] = XG[t]
    DS[...] = jnp.zeros_like(DS)
    SBU[...] = jnp.zeros_like(SBU)
    SGV[...] = jnp.zeros_like(SGV)

    def scaled(value, layer, at):
        return (rows_norm(value)[0] * row(layer, at) + row(layer, at + 1)).astype(BF)

    def attention(layer):
        if layer == 1:
            A[layer, t] = scaled(XIN[layer].astype(F32), layer, 0)
            gather_start(A.at[layer], 2)
        if layer == 0:
            only(0, lambda: w_near(first))
        only(layer, lambda: w_far(first))
        only(1 - layer, lambda: w_other(first))

        def attend(k, i):
            if layer == 0:
                A[layer, i] = scaled(XG[i].astype(F32), layer, 0)
            qkv = dot(A[layer, i], w_qkv(layer)).astype(BF)
            QKV[layer, i] = qkv
            stack = split_heads(qkv[:, :wide], heads, HD)
            scores = dot_nt(stack, qkv[:, wide : 2 * wide]) * (HD ** (-0.5)) + BIAS[layer]
            column = lanes_of(scores.shape).astype(F32)
            scores = jnp.where(column < LEN[i][0:1, 0:1], scores, -1000000000.0)
            raised = jnp.exp(scores - jnp.max(scores, axis=-1, keepdims=True))
            probs = raised / jnp.sum(raised, axis=-1, keepdims=True)
            PR[layer, i] = probs
            mixed = join_heads(dot(probs.astype(BF), qkv[:, 2 * wide :]), heads, HD).astype(BF)
            MIX[layer, i] = mixed
            reduce_put(2 * layer, k, dot(mixed, w_out(layer)))

        def pass_on(k):
            if layer == 0:
                for n in range(4):
                    at_step(k, s == 0, n, lambda n=n: w_pass(3 + n))
                at_step(k, s == 0, 2, lambda: w_near(second))
                at_step(k, s == 1, 2, lambda: (w_share(0), w_share(1)))
                at_step(k, s == 1, 3, lambda: w_pass(0))
            else:
                at_step(k, s == 1, 0, lambda: w_pass(6))
                at_step(k, s == 1, 1, lambda: w_near(second))
            share_item(2 * (k % 2) + k // 2, layer, (0, 1))

        each_item(((XG, 0),) if layer == 0 else ((A.at[layer], 2),), attend, pass_on, relay=layer == 1)
        hmid = XIN[layer].astype(F32) + reduce_end(2 * layer) + row(layer, 4)
        HM[layer] = hmid
        C[layer, t] = scaled(hmid, layer, 2)
        gather_start(C.at[layer], 2 * layer + 1)

    def hidden_back(layer, i, u, th):
        square = u * u
        slope = 0.5 * (1.0 + th) + (0.5 * GELU_K) * u * (1.0 - th * th) * (1.0 + 0.134145 * square)
        du = (dot_nt(DZ[layer, i], w_down(layer)) * slope).astype(BF)
        DU[layer, i] = du
        SBU[layer] += column_sum(du.astype(F32))
        return dot_nt(du, w_up(layer))

    def feed_forward(layer):
        only(layer, lambda: w_far(second))
        only(1 - layer, lambda: w_other(second))
        if layer == 0:
            only(1, lambda: w_pass(1))

        def feed(k, i):
            u = dot(C[layer, i], w_up(layer)) + row(layer, 6)
            th = jnp.tanh(GELU_K * (u + 0.044715 * (u * u * u)))
            if layer == 0:
                UF[u_rows(layer, i), :] = u
            else:
                reduce_put(4, k, hidden_back(layer, i, u, th))
            f = (0.5 * u * (1.0 + th)).astype(BF)
            FA[layer, i] = f
            reduce_put(2 * layer + 1, k, dot(f, w_down(layer)), side=layer == 1)

        def prepare(k):
            if layer == 0:
                for n in range(4):
                    at_step(k, s == 1, n, lambda n=n: w_pass(2 + n))
                at_step(k, s == 1, 2, lambda: w_near(first))
            share_item(2 * (k % 2) + k // 2, layer, (2, 3) if layer == 0 else (2, 3, 4, 6))

        gathers = ((C.at[layer], 2 * layer + 1),)
        if layer == 1:
            gathers += ((DZ.at[layer], 4),)
        each_item(gathers, feed, prepare)

    def layer_result(layer):
        return (valid * (HM[layer] + reduce_end(2 * layer + 1, side=layer == 1) + row(layer, 5))).astype(BF)

    def give_result(layer):
        @pl.when(s == layer)
        def _():
            lo[s] = XIN[layer + 1]

        @pl.when(s != layer)
        def _():
            remote(XIN.at[layer + 1], lo.at[s], ss_o.at[0], rs_o.at[0], sib).start()

    def feed_back(layer):
        def feed(k, i):
            u = UF[u_rows(layer, i), :]
            th = jnp.tanh(GELU_K * (u + 0.044715 * (u * u * u)))
            reduce_put(6, k, hidden_back(layer, i, u, th))

        def fold_first(k):
            for n in range(2):
                at_step(k, s == 1, n, lambda n=n: g_fold(first, n))
            at_step(k, s == 1, 1, lambda: g_later(first))
            share_item(2 * (k % 2) + k // 2, layer, (4, 6))

        each_item(((DZ.at[layer], 6),), feed, fold_first)

    def middle_back(layer):
        dc = reduce_end(6 - 2 * layer)
        normed, scale = rows_norm(HM[layer])
        dh = DZ[layer, t].astype(F32) + norm_back(dc, normed, scale, row(layer, 2))
        DH[...] = dh
        dattn = dh.astype(BF)
        DAT[layer, t] = dattn
        gather_start(DAT.at[layer], 7 - 2 * layer)
        SGV[layer, 2:3, :] = column_sum(dc * normed)
        SGV[layer, 3:4, :] = column_sum(dc)
        SGV[layer, 4:5, :] = column_sum(dattn.astype(F32))
        only(layer, lambda: (g_make(second, 1), g_fold(second, 0), g_fold(second, 1)))

    def attention_back(layer):
        def attend(k, i):
            dmixed = dot_nt(DAT[layer, i], w_out(layer)).astype(BF)
            qkv = QKV[layer, i]
            probs = PR[layer, i]
            stack = split_heads(dmixed, heads, HD)
            dprobs = dot_nt(stack, qkv[:, 2 * wide :])
            dscores = (probs * (dprobs - jnp.sum(probs * dprobs, axis=-1, keepdims=True))).astype(BF)
            DS[layer] += dscores.astype(F32)
            dq = join_heads(dot(dscores, qkv[:, wide : 2 * wide]), heads, HD) * (HD ** (-0.5))
            dk = dot_tn(dscores, split_heads(qkv[:, :wide], heads, HD)) * (HD ** (-0.5))
            dv = dot_tn(probs.astype(BF), stack)
            DQ[layer, i, :, :wide] = dq.astype(BF)
            DQ[layer, i, :, wide : 2 * wide] = dk.astype(BF)
            DQ[layer, i, :, 2 * wide :] = dv.astype(BF)
            reduce_put(7 - 2 * layer, k, dot_nt(DQ[layer, i], w_qkv(layer)))

        def fold_second(k):
            for n in range(2):
                at_step(k, s == layer, n, lambda n=n: g_fold(second, n + 2))
            at_step(k, s == layer, 1, lambda: g_later(second))
            share_item(2 * (k % 2) + k // 2, layer, (5, 7))

        each_item(((DAT.at[layer], 7 - 2 * layer),), attend, fold_second)

    def inputs_back(layer):
        da = reduce_end(7 - 2 * layer)
        normed, scale = rows_norm(XIN[layer].astype(F32))
        dx = DH[...] + norm_back(da, normed, scale, row(layer, 0))
        low = dx.astype(BF)
        if layer == 1:
            dyv = valid * low.astype(F32)
            DZ[0, t] = dyv.astype(BF)
            gather_start(DZ.at[0], 6)
            SGV[0, 5:6, :] = column_sum(dyv)
        SGV[layer, 0:1, :] = column_sum(da * normed)
        SGV[layer, 1:2, :] = column_sum(da)
        result = low.astype(F32) if layer == 1 else dx

        @pl.when(s == layer)
        def _():
            ig[s] = result

        @pl.when(s != layer)
        def _():
            DX[...] = result
            remote(DX, ig.at[s], ss_o.at[1], rs_o.at[1], sib).start()

    attention(0)
    feed_forward(0)
    XIN[1] = layer_result(0)
    attention(1)
    give_result(0)
    feed_forward(1)
    for part in (first, second):
        for k in (1, 2, 3):
            w_team(part, k).wait_send()
        for c in range(part.chunks):
            w_h(part, c).wait_send()
            for n in range(2):
                w_y(part, c, n).wait_send()
            for n in range(4):
                w_s(part, c, n // 2, n % 2).wait_send()
    only(1, lambda: g_make(second, 0))
    SGV[1, 5:6, :] = column_sum(DZ[1, t].astype(F32))
    middle_back(1)
    attention_back(1)
    only(1, lambda: g_make(first, 0))
    inputs_back(1)
    only(1, lambda: (g_make(first, 1), g_fold(first, 2)))
    feed_back(0)
    only(0, lambda: g_make(second, 0))
    only(1, lambda: g_total(second))
    middle_back(0)
    attention_back(0)
    only(0, lambda: (g_make(first, 0), g_fold(first, 2), g_make(first, 1)))
    only(0, lambda: (g_fold(first, 0), g_fold(first, 1), g_later(first)))
    inputs_back(0)

    spread = []
    for i in range(2):
        turned = skew(jnp.concatenate([DS[i], jnp.zeros((heads * rows, 128 - rows), F32)], axis=1), rows, -1)
        table = jnp.zeros((128, 128), F32)
        for hh in range(2):
            for yy in range(2):
                n = 2 * hh + yy
                line = column_sum(turned[n * rows : (n + 1) * rows])
                head = x + 2 * yy + 4 * z + 8 * hh
                table = jnp.where(lanes_of((128, 128), 0) == head, line, table)
        spread.append(
            lax.dot_general(
                onehot, table, (((1,), (1,)), ((), ())), precision=highest, preferred_element_type=F32
            )
        )
    for hh in range(2):
        for zz in range(2):
            for yy in range(2):
                j = yy + 2 * zz + 4 * hh
                for i in range(2):
                    MT[hh, zz, yy, i, 0:6, :] = SGV[i, 0:6, 128 * j : 128 * j + 128]
                    for xx in range(2):
                        for r in range(2):
                            at = (2 * hh + yy) * block + 128 * r
                            n = 6 + 2 * xx + r
                            MT[hh, zz, yy, i, n : n + 1, :] = jnp.where(
                                jnp.logical_and(z == zz, x == xx), SBU[i, :, at : at + 128], zero
                            )
                    MT[hh, zz, yy, i, 10:12, :] = jnp.zeros((2, 128), F32)
                    MT[hh, zz, yy, i, 12:16, :] = spread[i][4 * j : 4 * j + 4]

    def team_merge(k):
        return remote(MT.at[:, p.mate(k)[1]], MR.at[k], ss_m.at[6 + k], rs_m.at[6 + k], p.team(k)[0])

    def near_merge(n):
        a, b, e = around[n]
        there = (h + e * (1 - 2 * h), y + b * (1 - 2 * y), s + a * (1 - 2 * s))
        return remote(M1.at[there], MN.at[n], ss_m.at[n], rs_m.at[n], station(a, b, e))

    for k in (1, 2, 3):
        team_merge(k).start()
    for k in (1, 2, 3):
        reduce_copy(3, k, True).start()
    only(0, lambda: g_total(second))
    for k in (1, 2, 3):
        team_merge(k).wait()
    for hh in range(2):
        M1[hh] = MT[hh, z] + MR[1, hh] + MR[2, hh] + MR[3, hh]
    for n in range(7):
        near_merge(n).start()
    g_total(first)
    g_end(second)
    XIN[2] = layer_result(1)
    give_result(1)
    for n in range(7):
        near_merge(n).wait()
    tile = M1[h, y, s]
    for n in range(7):
        tile = tile + MN[n]
    OT[...] = tile
    g_end(first)

    for part in (first, second):
        for k in (1, 2, 3):
            g_t(part, k).wait_send()
        for c in range(part.chunks):
            g_h(part, c).wait_send()
            for n in range(2):
                g_y(part, c, n).wait_send()
    for i in range(8):
        for slot in range(4):
            share_copy(i, 1 - s, slot).wait_send()
    remote(XIN.at[1], lo.at[1 - s], ss_o.at[0], rs_o.at[0], sib).wait()
    remote(DX, ig.at[1 - s], ss_o.at[1], rs_o.at[1], sib).wait()


def finish_kernel(
    lo_in, ig_in, oq_in, oo_in, ou_in, od_in, ot_in,
    lo, ig, oq, oo, ou, od, a0, a1, a2, a3, a4, bu, a5, tab,
    OQ, OU, OT, LO, IG, OO, OD, FQ, FU, came, left,
):
    moves = ((oq_in, OQ), (ou_in, OU), (ot_in, OT), (ig_in, IG), (od_in, OD), (lo_in, LO), (oo_in, OO))
    moves = [pltpu.make_async_copy(a, b, came.at[i]) for i, (a, b) in enumerate(moves)]
    for cp in moves:
        cp.start()
    block = OD.shape[0]
    outs = []

    def leave(src, dst):
        cp = pltpu.make_async_copy(src, dst, left.at[len(outs)])
        cp.start()
        outs.append(cp)

    moves[0].wait()
    for hh in range(2):
        for zz in range(2):
            for yy in range(2):
                for i in range(3):
                    at = (4 * i + 2 * hh + yy) * HD
                    to = (16 * i + 2 * yy + 4 * zz + 8 * hh) * HD
                    FQ[:, to : to + 2 * HD] = jnp.concatenate(
                        [OQ[2 * zz, :, at : at + HD], OQ[2 * zz + 1, :, at : at + HD]], axis=1
                    )
    leave(FQ, oq)
    moves[1].wait()
    for hh in range(2):
        for zz in range(2):
            for yy in range(2):
                for xx in range(2):
                    n = 2 * hh + yy
                    d = xx + 2 * yy + 4 * zz + 8 * hh
                    FU[:, d * block : (d + 1) * block] = OU[xx + 2 * zz, :, n * block : (n + 1) * block]
    leave(FU, ou)
    for i, (src, dst) in enumerate(((IG, ig), (OD, od), (LO, lo), (OO, oo))):
        moves[3 + i].wait()
        leave(src, dst)
    moves[2].wait()
    x = lax.axis_index("dp") % 2
    for i, ref in enumerate((a0, a1, a2, a3, a4, a5)):
        ref[...] = jnp.where(x == 0, OT[i : i + 1, :HD], OT[i : i + 1, HD:])
    for r in range(2):
        bu[:, 128 * r : 128 * r + 128] = jnp.where(x == 0, OT[6 + r : 7 + r, :], OT[8 + r : 9 + r, :])
    for b in range(2):
        tab[:, 16 * b : 16 * b + 16] = jnp.where(x == 0, OT[12 + b : 13 + b, :16], OT[14 + b : 15 + b, :16])
    for cp in outs:
        cp.wait()


def vm(n=1):
    return [pl.BlockSpec(memory_space=pltpu.VMEM)] * n


def hb(n=1):
    return [pl.BlockSpec(memory_space=pltpu.HBM)] * n


def sems(*shape):
    return pltpu.SemaphoreType.DMA(shape)


def shape_of(dims, kind):
    return jax.ShapeDtypeStruct(dims, kind)


def team_local(
    audio_in, out_grad, item_len, rel_bucket, w_qkv, w_out, w_up, w_down,
    ln1_gain, ln1_bias, ln2_gain, ln2_bias, b_out, b_up, b_down, rel_table,
):
    rows, width = audio_in.shape[2], audio_in.shape[3]
    part = w_qkv.shape[1]
    hidden = w_up.shape[2]
    block = hidden // 16
    wide, ff = width // 4, hidden // 4
    low = lambda *dims: pltpu.VMEM(dims, BF)
    full = lambda *dims: pltpu.VMEM(dims, F32)

    lo, ig, OQ, OO, OU, OD, OT = pl.pallas_call(
        step_kernel,
        out_shape=(
            shape_of((2, rows, width), BF),
            shape_of((2, rows, width), F32),
            shape_of((4, part, 3 * wide), F32),
            shape_of((part, width), F32),
            shape_of((4, part, ff), F32),
            shape_of((block, width), F32),
            shape_of((16, 128), F32),
        ),
        in_specs=hb(2) + vm(2) + hb(4) + vm(8),
        out_specs=tuple(vm(7)),
        scratch_shapes=[
            low(4, part, 3 * wide), low(4, part, ff),
            low(2, 2, 2, 2, 2, part, 3 * wide), low(2, 4, part, width),
            low(2, 2, 2, 2, 2, part, ff), low(2, 4, block, width), low(4, rows, width),
            low(3, rows, width),
            low(2, 4, rows, width), low(2, 4, rows, width), low(2, 4, rows, ff), low(2, 4, rows, wide),
            low(2, 4, rows, 3 * wide), full(2, 4, 4 * rows, rows), full(8 * rows, ff), full(2, rows, width),
            low(2, 4, rows, width), low(2, 4, rows, width), low(2, 4, rows, ff), low(2, 4, rows, 3 * wide),
            low(4, rows, width), low(4, rows, width), low(4, rows, ff), low(4, rows, wide),
            low(4, rows, width), low(4, rows, width), low(4, rows, ff), low(4, rows, 3 * wide),
            low(4, rows, width), low(4, rows, width), low(4, rows, width), low(4, rows, width), full(rows, width),
            full(rows, width), full(rows, width), full(rows, width),
            low(2, 2, 2, 2, part, 3 * wide), low(4, part, width),
            low(2, 2, 2, part, 3 * wide), low(2, part, width), low(2, 2, 2, part, ff), low(2, block, width),
            low(2, 2, part, 3 * wide), low(part, width), low(2, 2, part, ff), low(block, width),
            low(2, 2, part, 3 * wide), low(part, width), low(2, 2, part, ff), low(block, width),
            low(4, part, 3 * wide), low(4, part, ff),
            full(2, 2, 2, 2, 16, 128), full(4, 2, 2, 2, 16, 128), full(2, 8, width), full(4, 8, 128),
            full(2, 4 * rows, rows), full(128, 128), full(2, 8, width), full(2, 1, ff), full(2, 4 * rows, rows),
            full(2, 2, 2, 2, 16, 128), full(4, 2, 2, 2, 16, 128), full(2, 2, 2, 16, 128), full(7, 16, 128),
            sems(11), sems(2, 4), sems(2, 4), sems(2, 2, 4), sems(2, 2, 4), sems(2, 4), sems(2, 4),
            sems(2, 4, 4), sems(2, 4, 4), sems(10), sems(10),
            sems(8, 6), sems(8, 6), sems(8, 4), sems(8, 4), sems(8, 4), sems(8, 4), sems(2), sems(2),
            sems(2, 2, 4), sems(2, 2, 4), sems(2, 4), sems(2, 4), sems(2, 4), sems(2, 4), sems(10), sems(10),
        ],
        compiler_params=pltpu.CompilerParams(
            collective_id=0, has_side_effects=True, vmem_limit_bytes=63 << 20
        ),
        name="two_layers",
    )(
        audio_in.reshape(2, rows, width), out_grad.reshape(2, rows, width), item_len.T, rel_bucket[None],
        w_qkv[0], w_out[0], w_up[0], w_down[0],
        ln1_gain, ln1_bias, ln2_gain, ln2_bias, b_out, b_down, b_up, rel_table,
    )

    lo, ig, oq, oo, ou, od, a0, a1, a2, a3, a4, bu, a5, tab = pl.pallas_call(
        finish_kernel,
        out_shape=(
            shape_of((2, rows, width), BF),
            shape_of((2, rows, width), F32),
            shape_of((part, 3 * width), F32),
            shape_of((part, width), F32),
            shape_of((part, hidden), F32),
            shape_of((block, width), F32),
        )
        + (shape_of((1, part), F32),) * 5
        + (shape_of((1, block), F32), shape_of((1, part), F32), shape_of((1, 32), F32)),
        in_specs=hb(7),
        out_specs=tuple(hb(6) + vm(8)),
        scratch_shapes=[
            full(4, part, 3 * wide), full(4, part, ff), full(16, 128),
            low(2, rows, width), full(2, rows, width), full(part, width), full(block, width),
            full(part, 3 * width), full(part, hidden), sems(7), sems(6),
        ],
        compiler_params=pltpu.CompilerParams(vmem_limit_bytes=62 << 20),
        name="finish",
    )(lo, ig, OQ, OO, OU, OD, OT)
    return (
        lo[None, :, None], ig[None, :, None], oq[None], oo[None], ou[None], od[None],
        a0, a1, a2, a3, a4, bu, a5, tab,
    )


def solution(mesh):
    fits = mesh.shape["dp"] == 16 and mesh.shape["section"] == 2
    return jax.shard_map(
        team_local if fits else local,
        mesh=mesh,
        in_specs=(
            P(None, "dp", None, None),
            P(None, "dp", None, None),
            P(None, "dp"),
            P(),
            P("section", "dp", None),
            P("section", "dp", None),
            P("section", "dp", None),
            P("section", "dp", None),
            P("section", "dp"),
            P("section", "dp"),
            P("section", "dp"),
            P("section", "dp"),
            P("section", "dp"),
            P("section", "dp"),
            P("section", "dp"),
            P("section", "dp"),
        ),
        out_specs=(
            P("section", None, "dp", None, None),
            P("section", None, "dp", None, None),
            P("section", "dp", None),
            P("section", "dp", None),
            P("section", "dp", None),
            P("section", "dp", None),
            P("section", "dp"),
            P("section", "dp"),
            P("section", "dp"),
            P("section", "dp"),
            P("section", "dp"),
            P("section", "dp"),
            P("section", "dp"),
            P("section", "dp"),
        ),
        check_vma=False,
    )
```
